32 devices in a mesh: blk: 16 (over z, x, core), head: 2 (over y).
Axes of the slice: x: 2, y: 2, z: 4, core: 2. Of those that a mesh axis runs over, the one named last changes fastest.
Arguments:
- tokens: bfloat16 [16384, 512], P(('blk', 'head')), may hold values from -6 to 6
- memory: bfloat16 [16384, 512], P(('blk', 'head')), may hold values from -6 to 6
- cotangent: float32 [16384, 512], P(('blk', 'head')), may hold values from -6 to 6
- deal_order: int32 [16384], P('blk'), may hold values from 0 to 16383, as said below
- lengths: int32 [32], replicated, may hold values from 1 to 1024, 16384 in all
- mem_index: int32 [32], replicated, may hold values from 0 to 15
- self_qkv: bfloat16 [512, 1536], P(None, ('blk', 'head')), may hold values from -0.25 to 0.25
- self_out: bfloat16 [512, 512], P(None, ('blk', 'head')), may hold values from -4 to 4
- cross_qkv: bfloat16 [512, 1536], P(None, ('blk', 'head')), may hold values from -0.25 to 0.25
- cross_out: bfloat16 [512, 512], P(None, ('blk', 'head')), may hold values from -4 to 4
- ffn_in: bfloat16 [512, 2048], P(None, ('blk', 'head')), may hold values from -0.25 to 0.25
- ffn_out: bfloat16 [2048, 512], P(None, ('blk', 'head')), may hold values from -0.125 to 0.125
- norm_gains: bfloat16 [3, 512], P(None, ('blk', 'head')), may hold values from 0.25 to 1.75
- biases: bfloat16 [10, 512], P(None, ('blk', 'head')), may hold values from -2 to 2
- ffn_bias: bfloat16 [2048], P(('blk', 'head')), may hold values from -2 to 2
Outputs:
- layer_out: float32 [16384, 512], P(('blk', 'head'))
- grad_tokens: float32 [16384, 512], P(('blk', 'head'))
- grad_memory: float32 [16384, 512], P(('blk', 'head'))
- grad_self_qkv: float32 [512, 1536], P(None, ('blk', 'head'))
- grad_self_out: float32 [512, 512], P(None, ('blk', 'head'))
- grad_cross_qkv: float32 [512, 1536], P(None, ('blk', 'head'))
- grad_cross_out: float32 [512, 512], P(None, ('blk', 'head'))
- grad_ffn_in: float32 [512, 2048], P(None, ('blk', 'head'))
- grad_ffn_out: float32 [2048, 512], P(None, ('blk', 'head'))
- grad_gains: float32 [3, 512], P(None, ('blk', 'head'))
- grad_biases: float32 [10, 512], P(None, ('blk', 'head'))
- grad_ffn_bias: float32 [2048], P(('blk', 'head'))
The draws below stay inside these ranges and needn't reach their ends.
Inputs may be any that keep to these rules, and one draw needn't show every extreme that they name: `deal_order`: each of 0 to 16383 appears once; the rows of each aligned block of 1024 rows hold the places of that same block. The lengths add up to 16384; the longest is exactly 1024.
All inputs are finite; a program needn't handle non-finite values.
Results may differ from the reference program's by a relative error of at most 0.035.
Values may be sent and summed in bfloat16 or wider, within the bound.
No kernel may reach another device: no remote copies, remote signals or barrier semaphores. Data moves between devices by JAX's collectives and lax.ppermute only.
A program may use at most 192 MiB of HBM per device.

```python
import math
import jax
import jax.numpy as jnp
import numpy as np
from jax import lax

D = 512
HEADS = 8
FF = 2048
MEM = 1024
GROUP = 1024
MAXLEN = 1024
TOKENS = 16384
NSEQ = 32
NMEM = 16
MROWS = 16384


def draw_deal_order(key, part):
    group_keys = jax.random.split(key, TOKENS // GROUP)
    shuffled = jax.vmap(lambda one_key: jax.random.permutation(one_key, GROUP))(group_keys)
    bases = jnp.arange(TOKENS // GROUP, dtype=jnp.int32) * GROUP
    return (shuffled.astype(jnp.int32) + bases[:, None]).reshape(TOKENS)


def touch_ends(values, key, smallest, top_value):
    shape = values.shape
    place = [jax.random.randint(jax.random.fold_in(key, axis), (), 0, shape[axis]) for axis in range(len(shape))]
    values = values.at[tuple(place)].set(smallest)
    longest = shape.index(max(shape))
    place[longest] = (place[longest] + 1) % shape[longest]
    return values.at[tuple(place)].set(top_value)


def shard_levels(key, shape, cuts, smallest, largest):
    def one(axis_at, blocks):
        steps = jax.random.uniform(jax.random.fold_in(jax.random.fold_in(key, 6), axis_at), (blocks,), jnp.float32, smallest / len(cuts), largest / len(cuts))
        return jnp.repeat(jnp.exp(steps), shape[axis_at] // blocks).reshape((-1,) + (1,) * (len(shape) - axis_at - 1))

    level = one(*cuts[0])
    for cut in cuts[1:]:
        level = level * one(*cut)
    return level


def split_up(count, total, limit, skew):
    loads = [(1 << 20) // math.isqrt(grade ** skew) + 1 for grade in range(2, count + 1)]
    spare, counts = total - limit - (count - 1), [1] * (count - 1)
    while spare > 0:
        free = [i for i in range(count - 1) if counts[i] < limit]
        pool, left = sum([loads[i] for i in free]), spare
        for i in free:
            addition = min(limit - counts[i], max(1, left * loads[i] // pool), spare)
            counts[i] = counts[i] + addition
            spare = spare - addition
    return np.array([limit] + counts)


def uneven(key, number_of, total, reach, skew):
    if number_of == 2:
        one = jax.random.randint(key, (), max(1, total - reach), min(reach, total - 1) + 1)
        return jnp.stack([one, total - one])
    sizes = jnp.asarray(split_up(number_of, total, reach, skew), jnp.int32)
    twos = (number_of - 1) // 2
    donor, sink = sizes[1:1 + 2 * twos:2], sizes[2:2 + 2 * twos:2]
    margin = jnp.minimum(donor - 1, reach - sink)
    moved = jax.random.randint(jax.random.fold_in(key, 1), (twos,), 0, 1 << 20) % (margin + 1)
    sizes = sizes.at[1:1 + 2 * twos:2].set(donor - moved).at[2:2 + 2 * twos:2].set(sink + moved)
    return sizes[jax.random.permutation(jax.random.fold_in(key, 2), number_of)]


def gaussian(key, extent, spread, reach, cuts=(), held_as=jnp.bfloat16):
    array = spread * jax.random.normal(key, extent, jnp.float32)
    if cuts:
        array = array * shard_levels(key, extent, cuts, -0.22, 0.18)
    return jnp.clip(array, -reach, reach).astype(held_as)


def setup_inputs(seed: int = 0) -> dict:
    seeds = jax.random.split(jax.random.key(seed), 16)
    tokens = gaussian(seeds[0], (TOKENS, D), 1.0, 6.0, ((0, 32),))
    memory = gaussian(seeds[1], (MROWS, D), 1.0, 6.0, ((0, 32),))
    cotangent = gaussian(seeds[2], (TOKENS, D), 1.0, 6.0, ((0, 32),), jnp.float32)
    deal_order = draw_deal_order(jax.random.fold_in(seeds[15], 71), 0)
    lengths = uneven(seeds[4], NSEQ, TOKENS, MAXLEN, 2).astype(jnp.int32)
    mem_index = touch_ends(jax.random.randint(seeds[5], (NSEQ,), 0, NMEM), jax.random.fold_in(seeds[5], 1), 0, NMEM - 1).astype(jnp.int32)
    self_qkv = gaussian(seeds[6], (D, 3 * D), D ** -0.5, 0.25, ((1, 32),))
    self_out = gaussian(seeds[7], (D, D), 2 ** -0.5, 4.0, ((1, 32),))
    cross_qkv = gaussian(seeds[8], (D, 3 * D), D ** -0.5, 0.25, ((1, 32),))
    cross_out = gaussian(seeds[9], (D, D), 2 ** -0.5, 4.0, ((1, 32),))
    ffn_in = gaussian(seeds[10], (D, FF), D ** -0.5, 0.25, ((1, 32),))
    ffn_out = gaussian(seeds[11], (FF, D), FF ** -0.5, 0.125, ((1, 32),))
    norm_gains = jnp.clip(1.0 + 0.15 * jax.random.normal(seeds[12], (3, D), jnp.float32), 0.25, 1.75).astype(jnp.bfloat16)
    biases = gaussian(seeds[13], (10, D), 0.3, 2.0, ((1, 32),))
    ffn_bias = gaussian(seeds[14], (FF,), 0.3, 2.0, ((0, 32),))
    return dict(tokens=tokens, memory=memory, cotangent=cotangent, deal_order=deal_order, lengths=lengths, mem_index=mem_index, self_qkv=self_qkv, self_out=self_out, cross_qkv=cross_qkv, cross_out=cross_out, ffn_in=ffn_in, ffn_out=ffn_out, norm_gains=norm_gains, biases=biases, ffn_bias=ffn_bias)


MASK_FILL = -1e+30
EPSILON = 1e-05
GELU_SCALE = 0.7978845608028654
HIGHEST_PRECISION = lax.Precision.HIGHEST

@jax.custom_vjp
def low(v):
    return lax.optimization_barrier(v.astype(jnp.bfloat16)).astype(jnp.float32)

@jax.custom_vjp
def low_back(v):
    return v

def low_keep(v):
    return (low(v), None)

def low_pass(kept, grad):
    return (grad,)

def back_keep(v):
    return (v, None)

def back_low(kept, grad):
    return (low(grad),)
low.defvjp(low_keep, low_pass)
low_back.defvjp(back_keep, back_low)

def gelu_tanh(entries):
    return 0.5 * entries * (1.0 + jnp.tanh(GELU_SCALE * (entries + 0.044715 * entries * entries * entries)))

def matmul(left_side, right_side):
    return jnp.dot(left_side, right_side, precision=HIGHEST_PRECISION)

def both_round(entries):
    return low_back(low(entries))

def layer_norm(entries, gain_row, shift_row):
    centre = entries - lax.optimization_barrier(jnp.mean(entries, axis=1, keepdims=True))
    inverse = lax.rsqrt(lax.optimization_barrier(jnp.mean(centre * centre, axis=1, keepdims=True)) + EPSILON)
    return centre * inverse * gain_row + shift_row

def attention(queries, keys_all, values_all, query_starts, key_starts, key_lengths, key_rows, segment_ids, offsets_in):
    col_width = queries.shape[1]
    key_scale = 1.0 / math.sqrt(D // HEADS)
    padded_q = jnp.concatenate([queries, jnp.zeros((MAXLEN, col_width), jnp.float32)], axis=0)
    padded_k = jnp.concatenate([keys_all, jnp.zeros((key_rows, col_width), jnp.float32)], axis=0)
    padded_v = jnp.concatenate([values_all, jnp.zeros((key_rows, col_width), jnp.float32)], axis=0)

    def one_sequence(number):
        query_rows = lax.dynamic_slice_in_dim(padded_q, query_starts[number], MAXLEN, 0).reshape(MAXLEN, HEADS, -1)
        key_block = lax.dynamic_slice_in_dim(padded_k, key_starts[number], key_rows, 0).reshape(key_rows, HEADS, -1)
        value_block = lax.dynamic_slice_in_dim(padded_v, key_starts[number], key_rows, 0).reshape(key_rows, HEADS, -1)
        scores = low_back(jnp.einsum('qhd,khd->hqk', query_rows, key_block, precision=HIGHEST_PRECISION) * key_scale)
        usable = jnp.arange(key_rows, dtype=jnp.int32) < key_lengths[number]
        scores = jnp.where(usable[None, None, :], scores, MASK_FILL)
        weights = jnp.exp(scores - jax.nn.logsumexp(scores, axis=2, keepdims=True))
        return jnp.einsum('hqk,khd->qhd', low(weights), value_block, precision=HIGHEST_PRECISION).reshape(MAXLEN, col_width)
    per_sequence = lax.map(jax.checkpoint(one_sequence), jnp.arange(NSEQ, dtype=jnp.int32))
    return per_sequence[segment_ids, offsets_in]

def reference(tokens, memory, cotangent, deal_order, lengths, mem_index, self_qkv, self_out, cross_qkv, cross_out, ffn_in, ffn_out, norm_gains, biases, ffn_bias):
    seq_lengths = lengths.astype(jnp.int32)
    seq_ends = jnp.cumsum(seq_lengths).astype(jnp.int32)
    seq_starts = (seq_ends - seq_lengths).astype(jnp.int32)
    positions = jnp.arange(TOKENS, dtype=jnp.int32)
    segment_ids = lax.optimization_barrier(jnp.sum((positions[:, None] >= seq_ends[None, :]).astype(jnp.int32), axis=1)).astype(jnp.int32)
    offsets_in = (positions - seq_starts[segment_ids]).astype(jnp.int32)
    slot_of = jnp.zeros((TOKENS,), jnp.int32).at[deal_order.astype(jnp.int32)].set(positions)
    mem_starts = (mem_index.astype(jnp.int32) * MEM).astype(jnp.int32)
    mem_lengths = jnp.full((NSEQ,), MEM, jnp.int32)
    zero_row = jnp.zeros((D,), jnp.float32)

    def forward(tokens_f, memory_f, attn_qkv, attn_out, mem_qkv, mem_out, ffn_up, ffn_down, gain_rows, bias_rows, up_bias):
        inputs = tokens_f[slot_of]
        self_proj = both_round(matmul(inputs, attn_qkv) + jnp.concatenate([bias_rows[0], zero_row, bias_rows[1]]))
        attended = both_round(attention(self_proj[:, :D], self_proj[:, D:2 * D], self_proj[:, 2 * D:], seq_starts, seq_starts, seq_lengths, MAXLEN, segment_ids, offsets_in))
        self_branch = low_back(matmul(attended, attn_out) + bias_rows[2])
        first_norm = layer_norm(inputs + self_branch, gain_rows[0], bias_rows[7])
        cross_q = both_round(matmul(low(first_norm), mem_qkv[:, :D]) + bias_rows[3])
        mem_kv = both_round(matmul(memory_f, mem_qkv[:, D:]) + jnp.concatenate([zero_row, bias_rows[4]]))
        crossed = both_round(attention(cross_q, mem_kv[:, :D], mem_kv[:, D:], seq_starts, mem_starts, mem_lengths, MEM, segment_ids, offsets_in))
        cross_branch = low_back(matmul(crossed, mem_out) + bias_rows[5])
        second_norm = layer_norm(first_norm + cross_branch, gain_rows[1], bias_rows[8])
        pre_act = low_back(matmul(low(second_norm), ffn_up) + up_bias)
        hidden = low(gelu_tanh(pre_act))
        ffn_branch = low_back(matmul(hidden, ffn_down) + bias_rows[6])
        final_norm = layer_norm(second_norm + ffn_branch, gain_rows[2], bias_rows[9])
        return final_norm[deal_order.astype(jnp.int32)]
    primal = (tokens.astype(jnp.float32), memory.astype(jnp.float32), self_qkv.astype(jnp.float32), self_out.astype(jnp.float32), cross_qkv.astype(jnp.float32), cross_out.astype(jnp.float32), ffn_in.astype(jnp.float32), ffn_out.astype(jnp.float32), norm_gains.astype(jnp.float32), biases.astype(jnp.float32), ffn_bias.astype(jnp.float32))
    result, pullback = jax.vjp(forward, *primal)
    grads = pullback(cotangent.astype(jnp.float32))
    return (result, grads[0], grads[1], grads[2], grads[3], grads[4], grads[5], grads[6], grads[7], grads[8], grads[9], grads[10])
```

```python
import functools
import math

import jax
import jax.numpy as jnp
import numpy as np
from jax import lax
from jax.experimental import pallas as pl
from jax.experimental.pallas import tpu as pltpu
from jax.sharding import PartitionSpec as P

D = 512
HEADS = 8
MEM = 1024
HD = D // HEADS
PAIRS = HEADS // 2
SCALE = 1.0 / math.sqrt(HD)
EPSILON = 1e-05
GELU_SCALE = 0.7978845608028654
FILL = -1e30
FLOOR = -1e20
BOTH = ("blk", "head")
BF = jnp.bfloat16
F32 = jnp.float32
VMEM_BYTES = 60 * 1024 * 1024


def dot_nn(a, b):
    return lax.dot_general(a, b, (((1,), (0,)), ((), ())), preferred_element_type=F32)


def dot_nt(a, b):
    return lax.dot_general(a, b, (((1,), (1,)), ((), ())), preferred_element_type=F32)


def dot_tn(a, b):
    return lax.dot_general(a, b, (((0,), (0,)), ((), ())), preferred_element_type=F32)


def hi_lo(x):
    hi = x.astype(BF)
    return hi, (x - hi.astype(F32)).astype(BF)


class Grid:
    def __init__(self):
        self.blk = lax.axis_size("blk")
        self.head = lax.axis_size("head")
        self.core = 2 if self.blk % 2 == 0 else 1
        rest = self.blk // self.core
        major = 4 if rest % 4 == 0 else rest
        self.size = {"z": major, "x": rest // major, "c": self.core, "y": self.head}
        self.stride = {
            "y": 1,
            "c": self.head,
            "x": self.head * self.core,
            "z": self.head * self.core * (rest // major),
        }
        self.count = self.blk * self.head
        b = lax.axis_index("blk")
        self.at = {
            "y": lax.axis_index("head"),
            "c": b % self.core,
            "x": (b // self.core) % self.size["x"],
            "z": b // (self.core * self.size["x"]),
        }

    def shift(self, array, dim, step=1):
        size, stride = self.size[dim], self.stride[dim]
        route = []
        for i in range(self.count):
            at = (i // stride) % size
            route.append((i, i + ((at + step) % size - at) * stride))
        return lax.ppermute(array, BOTH, route)

    def others(self, array, dim):
        return [self.shift(array, dim, k) for k in range(1, self.size[dim])]

    def reduce(self, buffer, axis, dim):
        size, at = self.size[dim], self.at[dim]
        if size == 1:
            return jnp.squeeze(buffer, axis)

        def entry(k):
            return lax.dynamic_index_in_dim(buffer, (at + k) % size, axis, keepdims=False)

        moved = [self.shift(entry(k).astype(BF), dim, k) for k in range(1, size)]
        total = entry(0).astype(F32)
        for part in moved:
            total = total + part.astype(F32)
        return total


def after(value, *first):
    return lax.optimization_barrier((value, *first))[0]


def cost(us, nbytes=0):
    return pl.CostEstimate(flops=int(us * 1e9), transcendentals=0, bytes_accessed=int(nbytes))


def along(grid, held, dim, join):
    if grid.size[dim] == 1:
        return held
    out = []
    for array, places in held:
        arrays = [array] + grid.others(array, dim)
        tagged = [[dict(p, **{dim: k}) for p in places] for k in range(len(arrays))]
        if join:
            out.append((jnp.concatenate(arrays, axis=0), sum(tagged, [])))
        else:
            out += list(zip(arrays, tagged))
    return out


def place_kernel(size, rows, index_ref, *refs):
    arrays, outs = refs[: len(refs) - len(rows)], refs[len(refs) - len(rows) :]
    for a, array in enumerate(arrays):

        @pl.when(pl.program_id(0) == a)
        def _(array=array):
            for z in range(size):
                source = (index_ref[0] - z + size) % size
                start = 0
                for out, n in zip(outs, rows):
                    out[z, 0] = array[source, start : start + n, :]
                    start += n


def place(grid, held, rows):
    arrays = [a for a, _ in held]
    size = grid.size["z"]
    other = grid.count // size
    slot = []
    for _, places in held:
        at = 0
        for dim in ("x", "c", "y"):
            at = at * grid.size[dim] + (grid.at[dim] - places[0].get(dim, 0)) % grid.size[dim]
        slot.append(at)
    index = jnp.stack([grid.at["z"]] + slot).astype(jnp.int32)
    outs = pl.pallas_call(
        functools.partial(place_kernel, size, rows),
        grid_spec=pltpu.PrefetchScalarGridSpec(
            num_scalar_prefetch=1,
            grid=(len(arrays),),
            in_specs=[pl.BlockSpec(a.shape, lambda i, _: (0, 0, 0)) for a in arrays],
            out_specs=[
                pl.BlockSpec((size, 1, n, D), lambda i, index: (0, index[i + 1], 0, 0)) for n in rows
            ],
        ),
        out_shape=[jax.ShapeDtypeStruct((size, other, n, D), BF) for n in rows],
        compiler_params=pltpu.CompilerParams(vmem_limit_bytes=VMEM_BYTES),
        cost_estimate=cost(5),
        name="place_weights",
    )(index, *arrays)
    return [out.reshape(grid.count * n, D) for out, n in zip(outs, rows)]


def lane_mask(rows):
    return lax.broadcasted_iota(jnp.int32, (rows, 2 * HD), 1) < HD


def two(low, x):
    zero = jnp.zeros_like(x)
    return jnp.concatenate([jnp.where(low, x, zero), jnp.where(low, zero, x)], axis=0)


def pick(low, x):
    half = x.shape[0] // 2
    return jnp.where(low, x[:half], x[half:])


def with_ones(v):
    return jnp.concatenate([v, jnp.ones_like(v)], axis=1)


def pair_cols(g):
    return slice(g * 2 * HD, (g + 1) * 2 * HD)


def self_forward_kernel(
    pairs, tq, tk, lo_ref, hi_ref, q_ref, k_ref, v_ref, range_ref, att_ref, lse_ref, score_ref, top_ref, acc_ref
):
    width = 2 * HD
    low = lane_mask(tq)
    for i in range(q_ref.shape[0] // tq):
        rows = pl.ds(i * tq, tq)
        begin = jnp.concatenate([range_ref[rows, 0:1]] * 2, axis=0)
        end = jnp.concatenate([range_ref[rows, 1:2]] * 2, axis=0)
        first = lo_ref[i]
        top_ref[...] = jnp.full_like(top_ref, FILL)
        acc_ref[...] = jnp.zeros_like(acc_ref)

        def scores(t, carry, i=i):
            keys = pl.ds(pl.multiple_of(t * tk, tk), tk)
            spot = pl.ds(pl.multiple_of((t - first) * tk, tk), tk)
            place = lax.broadcasted_iota(jnp.int32, (2 * tq, tk), 1) + t * tk
            allowed = (place >= begin) & (place < end)
            for g in range(pairs):
                s = dot_nt(two(low, q_ref[pl.ds(i * tq, tq), pair_cols(g)]), k_ref[keys, pair_cols(g)])
                s = jnp.where(allowed, s, FILL)
                score_ref[g, :, spot] = s
                peak = top_ref[g]
                for c in range(tk // width):
                    peak = jnp.maximum(peak, s[:, c * width : (c + 1) * width])
                top_ref[g] = peak
            return carry

        lax.fori_loop(first, hi_ref[i], scores, 0)
        for g in range(pairs):
            peak = jnp.max(top_ref[g], axis=1, keepdims=True)
            top_ref[g] = jnp.broadcast_to(peak, (2 * tq, width))

        def weigh(t, carry):
            keys = pl.ds(pl.multiple_of(t * tk, tk), tk)
            spot = pl.ds(pl.multiple_of((t - first) * tk, tk), tk)
            for g in range(pairs):
                p = jnp.exp(score_ref[g, :, spot] - top_ref[g, :, 0:1]).astype(BF)
                acc_ref[g] += dot_nn(p, with_ones(v_ref[keys, pair_cols(g)]))
            return carry

        lax.fori_loop(first, hi_ref[i], weigh, 0)
        for g in range(pairs):
            mass = acc_ref[g, :, width:]
            att_ref[rows, pair_cols(g)] = pick(low, acc_ref[g, :, :width] / mass).astype(BF)
            flat = (top_ref[g] + jnp.log(mass)).T
            lse_ref[g, 0:1, rows] = flat[0:1, :tq]
            lse_ref[g, 1:2, rows] = flat[0:1, tq:]


def self_forward(q, kv, ranges, lo, hi, tq, tk, pairs):
    rows, keys = q.shape[0], kv.shape[0]
    width = pairs * 2 * HD
    groups = PAIRS // pairs
    return pl.pallas_call(
        functools.partial(self_forward_kernel, pairs, tq, tk),
        grid_spec=pltpu.PrefetchScalarGridSpec(
            num_scalar_prefetch=2,
            grid=(groups,),
            in_specs=[
                pl.BlockSpec((rows, width), lambda g, *_: (0, g)),
                pl.BlockSpec((keys, width), lambda g, *_: (0, g)),
                pl.BlockSpec((keys, width), lambda g, *_: (0, groups + g)),
                pl.BlockSpec((rows, 128), lambda g, *_: (0, 0)),
            ],
            out_specs=[
                pl.BlockSpec((rows, width), lambda g, *_: (0, g)),
                pl.BlockSpec((pairs, 8, rows), lambda g, *_: (g, 0, 0)),
            ],
            scratch_shapes=[
                pltpu.VMEM((pairs, 2 * tq, keys), F32),
                pltpu.VMEM((pairs, 2 * tq, 2 * HD), F32),
                pltpu.VMEM((pairs, 2 * tq, 4 * HD), F32),
            ],
        ),
        out_shape=[
            jax.ShapeDtypeStruct((rows, D), BF),
            jax.ShapeDtypeStruct((PAIRS, 8, rows), F32),
        ],
        compiler_params=pltpu.CompilerParams(vmem_limit_bytes=VMEM_BYTES),
        cost_estimate=cost(20),
        name="self_forward",
    )(lo, hi, q, kv, kv, ranges)


def self_backward_kernel(
    pairs, tq, tk, lo_ref, hi_ref, q_ref, do_ref, k_ref, v_ref, row_ref, lse_ref, delta_ref, dq_ref, dk_ref, dv_ref,
    acc_q, acc_k, acc_v,
):
    low = lane_mask(tq)
    acc_k[...] = jnp.zeros_like(acc_k)
    acc_v[...] = jnp.zeros_like(acc_v)
    for i in range(q_ref.shape[0] // tq):
        rows = pl.ds(i * tq, tq)
        begin = jnp.concatenate([row_ref[0:1, rows]] * 2, axis=1)
        end = jnp.concatenate([row_ref[1:2, rows]] * 2, axis=1)
        acc_q[...] = jnp.zeros_like(acc_q)

        def step(t, carry, i=i):
            rows = pl.ds(i * tq, tq)
            keys = pl.ds(pl.multiple_of(t * tk, tk), tk)
            place = lax.broadcasted_iota(jnp.int32, (tk, 2 * tq), 0) + t * tk
            allowed = (place >= begin) & (place < end)
            for g in range(pairs):
                cols = pair_cols(g)
                k, v = k_ref[keys, cols], v_ref[keys, cols]
                q2, do2 = two(low, q_ref[rows, cols]), two(low, do_ref[rows, cols])
                lse = jnp.concatenate([lse_ref[g, 0:1, rows], lse_ref[g, 1:2, rows]], axis=1)
                delta = jnp.concatenate([delta_ref[g, 0:1, rows], delta_ref[g, 1:2, rows]], axis=1)
                p = jnp.exp(jnp.where(allowed, dot_nt(k, q2) - lse, FILL))
                ds = (p * (dot_nt(v, do2) - delta)).astype(BF)
                acc_v[keys, cols] += dot_nn(p.astype(BF), do2)
                acc_k[keys, cols] += dot_nn(ds, q2)
                acc_q[g] += dot_tn(ds, k)
            return carry

        lax.fori_loop(lo_ref[i], hi_ref[i], step, 0)
        for g in range(pairs):
            dq_ref[rows, pair_cols(g)] = (pick(low, acc_q[g]) * SCALE).astype(BF)
    dk_ref[...] = acc_k[...].astype(BF)
    dv_ref[...] = acc_v[...].astype(BF)


def self_backward(q, do, kv, row_range, lse, delta, lo, hi, tq, tk, pairs):
    rows, keys = q.shape[0], kv.shape[0]
    width = pairs * 2 * HD
    groups = PAIRS // pairs
    return pl.pallas_call(
        functools.partial(self_backward_kernel, pairs, tq, tk),
        grid_spec=pltpu.PrefetchScalarGridSpec(
            num_scalar_prefetch=2,
            grid=(groups,),
            in_specs=[
                pl.BlockSpec((rows, width), lambda g, *_: (0, g)),
                pl.BlockSpec((rows, width), lambda g, *_: (0, g)),
                pl.BlockSpec((keys, width), lambda g, *_: (0, g)),
                pl.BlockSpec((keys, width), lambda g, *_: (0, groups + g)),
                pl.BlockSpec((8, rows), lambda g, *_: (0, 0)),
                pl.BlockSpec((pairs, 8, rows), lambda g, *_: (g, 0, 0)),
                pl.BlockSpec((pairs, 8, rows), lambda g, *_: (g, 0, 0)),
            ],
            out_specs=[
                pl.BlockSpec((rows, width), lambda g, *_: (0, g)),
                pl.BlockSpec((keys, width), lambda g, *_: (0, g)),
                pl.BlockSpec((keys, width), lambda g, *_: (0, g)),
            ],
            scratch_shapes=[
                pltpu.VMEM((pairs, 2 * tq, 2 * HD), F32),
                pltpu.VMEM((keys, width), F32),
                pltpu.VMEM((keys, width), F32),
            ],
        ),
        out_shape=[
            jax.ShapeDtypeStruct((rows, D), BF),
            jax.ShapeDtypeStruct((keys, D), BF),
            jax.ShapeDtypeStruct((keys, D), BF),
        ],
        compiler_params=pltpu.CompilerParams(vmem_limit_bytes=VMEM_BYTES),
        cost_estimate=cost(40),
        name="self_backward",
    )(lo, hi, q, do, kv, kv, row_range, lse, delta)


def memory_kv_kernel(starts, half, mem_ref, entry_ref, *refs):
    arrays, (w_ref, b_ref, m_ref, kv_ref) = refs[:-4], refs[-4:]
    j = pl.program_id(0)
    fresh = (j == 0) | (mem_ref[j] != mem_ref[jnp.maximum(j - 1, 0)])
    for a, (array, start) in enumerate(zip(arrays, starts)):

        @pl.when(fresh & (entry_ref[j * len(starts) + a] >= 0))
        def _(array=array, start=start):
            rows = array[0]
            m_ref[0, start : start + half] = rows
            kv_ref[0, start : start + half] = (dot_nt(rows, w_ref[...]) + b_ref[...]).astype(BF)


def memory_kv(grid, mem, held, weights, bias):
    arrays, starts = [a for a, _, _ in held], tuple(s for _, _, s in held)
    half = arrays[0].shape[1]
    entries = []
    for _, places, _ in held:
        behind = {d: np.array([p.get(d, 0) for p in places], np.int32) for d in "zxc"}
        at = 0
        for dim in "zxc":
            at = at * grid.size[dim] + (grid.at[dim] - behind[dim]) % grid.size[dim]
        hit = at[None, :] == mem[:-1, None]
        entries.append(jnp.max(jnp.where(hit, jnp.arange(len(places))[None, :], -1), axis=1))
    table = jnp.stack(entries, axis=1).reshape(-1).astype(jnp.int32)
    count = len(held)
    n = 2 * half
    by_memory = lambda j, mem, _: (mem[j], 0, 0)
    return pl.pallas_call(
        functools.partial(memory_kv_kernel, starts, half),
        grid_spec=pltpu.PrefetchScalarGridSpec(
            num_scalar_prefetch=2,
            grid=(mem.shape[0] - 1,),
            in_specs=[
                pl.BlockSpec(
                    (1, half, D), lambda j, mem, table, a=a: (jnp.maximum(table[j * count + a], 0), 0, 0)
                )
                for a in range(count)
            ]
            + [
                pl.BlockSpec((2 * D, D), lambda j, *_: (0, 0)),
                pl.BlockSpec((1, 2 * D), lambda j, *_: (0, 0)),
            ],
            out_specs=[pl.BlockSpec((1, n, D), by_memory), pl.BlockSpec((1, n, 2 * D), by_memory)],
        ),
        out_shape=[
            jax.ShapeDtypeStruct((grid.blk, n, D), BF),
            jax.ShapeDtypeStruct((grid.blk, n, 2 * D), BF),
        ],
        compiler_params=pltpu.CompilerParams(vmem_limit_bytes=VMEM_BYTES),
        cost_estimate=cost(6),
        name="memory_kv",
    )(mem, table, *arrays, weights, bias)


def cross_forward_kernel(parts, tq, mem_ref, table_ref, kv_ref, *refs):
    qs, outs, lses = refs[:parts], refs[parts : 2 * parts], refs[2 * parts : 3 * parts]
    width = 2 * HD
    j = pl.program_id(0)
    low = lane_mask(tq)
    for part in range(parts):
        first_row = table_ref[j * 2 * parts + 2 * part]
        last_row = table_ref[j * 2 * parts + 2 * part + 1]

        def step(t, carry, part=part, first_row=first_row, last_row=last_row):
            offset = pl.multiple_of(t * tq, tq)
            rows = pl.ds(offset, tq)
            at = lax.broadcasted_iota(jnp.int32, (tq, width), 0) + offset
            mine = (at >= first_row) & (at < last_row)
            at_row = lax.broadcasted_iota(jnp.int32, (1, tq), 1) + offset
            mine_row = (at_row >= first_row) & (at_row < last_row)
            for g in range(PAIRS):
                cols = pair_cols(g)
                s = dot_nt(two(low, qs[part][rows, cols]), kv_ref[0, :, cols])
                peak = jnp.max(s, axis=1, keepdims=True)
                p = jnp.exp(s - peak).astype(BF)
                acc = dot_nn(p, with_ones(kv_ref[0, :, pair_cols(PAIRS + g)]))
                mass = acc[:, width:]
                new = pick(low, acc[:, :width] / mass).astype(BF)
                outs[part][rows, cols] = jnp.where(mine, new, outs[part][rows, cols])
                flat = (peak + jnp.log(mass)).T
                for i in range(2):
                    head = slice(2 * g + i, 2 * g + i + 1)
                    lses[part][head, rows] = jnp.where(
                        mine_row, flat[0:1, i * tq : (i + 1) * tq], lses[part][head, rows]
                    )
            return carry

        lax.fori_loop(first_row // tq, (last_row + tq - 1) // tq, step, 0)


def cross_forward(mem, table, kv, queries, tq):
    parts, rows, n = len(queries), queries[0].shape[0], kv.shape[1]
    whole = pl.BlockSpec((rows, D), lambda j, *_: (0, 0))
    flat = pl.BlockSpec((HEADS, rows), lambda j, *_: (0, 0))
    out = pl.pallas_call(
        functools.partial(cross_forward_kernel, parts, tq),
        grid_spec=pltpu.PrefetchScalarGridSpec(
            num_scalar_prefetch=2,
            grid=(mem.shape[0] - 1,),
            in_specs=[pl.BlockSpec((1, n, 2 * D), lambda j, mem, _: (mem[j], 0, 0))] + [whole] * parts,
            out_specs=[whole] * parts + [flat] * parts,
        ),
        out_shape=[jax.ShapeDtypeStruct((rows, D), BF)] * parts
        + [jax.ShapeDtypeStruct((HEADS, rows), F32)] * parts,
        compiler_params=pltpu.CompilerParams(vmem_limit_bytes=VMEM_BYTES),
        cost_estimate=cost(16),
        name="cross_forward",
    )(mem, table, kv, *queries)
    return out[:parts], out[parts:]


def cross_backward_kernel(parts, tq, mem_ref, table_ref, kv_ref, m_ref, w_ref, zero_ref, *refs):
    qs, dos, stats = refs[:parts], refs[parts : 2 * parts], refs[2 * parts : 3 * parts]
    gm_ref, gw_ref, gb_ref = refs[3 * parts : 3 * parts + 3]
    dqs = refs[3 * parts + 3 : 4 * parts + 3]
    acc_k, acc_v, acc_q = refs[4 * parts + 3 :]
    j = pl.program_id(0)
    steps = mem_ref[pl.num_programs(0)]
    low = lane_mask(tq)

    @pl.when(j == 0)
    def _():
        acc_q[...] = jnp.zeros_like(acc_q)
        gw_ref[...] = jnp.zeros_like(gw_ref)
        gb_ref[...] = jnp.zeros_like(gb_ref)

    @pl.when((j == 0) | (mem_ref[j] != mem_ref[jnp.maximum(j - 1, 0)]))
    def _():
        acc_k[...] = jnp.zeros_like(acc_k)
        acc_v[...] = jnp.zeros_like(acc_v)

    for part in range(parts):
        first_row = table_ref[j * 2 * parts + 2 * part]
        last_row = table_ref[j * 2 * parts + 2 * part + 1]

        def step(t, carry, part=part, first_row=first_row, last_row=last_row):
            offset = pl.multiple_of(t * tq, tq)
            rows = pl.ds(offset, tq)
            at_row = lax.broadcasted_iota(jnp.int32, (1, tq), 1) + offset
            mine = (at_row >= first_row) & (at_row < last_row)
            for g in range(PAIRS):
                cols = pair_cols(g)
                k, v = kv_ref[0, :, cols], kv_ref[0, :, pair_cols(PAIRS + g)]
                q2, do2 = two(low, qs[part][rows, cols]), two(low, dos[part][rows, cols])

                def stat(base, part=part, g=g):
                    return [stats[part][base + 2 * g + i : base + 2 * g + i + 1, rows] for i in range(2)]

                lse = jnp.concatenate([jnp.where(mine, x, -FILL) for x in stat(0)], axis=1)
                delta = jnp.concatenate(stat(HEADS), axis=1)
                p = jnp.exp(dot_nt(k, q2) - lse)
                ds = (p * (dot_nt(v, do2) - delta)).astype(BF)
                acc_v[:, cols] += dot_nn(p.astype(BF), do2)
                acc_k[:, cols] += dot_nn(ds, q2)
                acc_q[part, rows, cols] += pick(low, dot_tn(ds, k))
            return carry

        lax.fori_loop(first_row // tq, (last_row + tq - 1) // tq, step, 0)

    @pl.when((j == steps - 1) | ((j < steps) & (mem_ref[j] != mem_ref[j + 1])))
    def _():
        dk, dv = acc_k[...].astype(BF), acc_v[...].astype(BF)
        gm_ref[0] = (dot_nn(dk, w_ref[0:D, :]) + dot_nn(dv, w_ref[D : 2 * D, :])).astype(BF)
        gw_ref[0:D, :] += dot_tn(dk, m_ref[0])
        gw_ref[D : 2 * D, :] += dot_tn(dv, m_ref[0])
        gb_ref[0:1, :] += jnp.sum(dv.astype(F32), axis=0, keepdims=True)

    @pl.when(j == steps - 1)
    def _():
        for part in range(parts):
            dqs[part][...] = (acc_q[part] * SCALE).astype(BF)


def cross_backward(mem, table, kv, rows_of_memory, weights, zeros, queries, upstream, stats, tq):
    parts, rows, n = len(queries), queries[0].shape[0], kv.shape[1]
    blocks = kv.shape[0]
    whole = pl.BlockSpec((rows, D), lambda j, *_: (0, 0))
    flat = pl.BlockSpec((2 * HEADS, rows), lambda j, *_: (0, 0))
    by_memory = lambda j, mem, _: (mem[j], 0, 0)
    return pl.pallas_call(
        functools.partial(cross_backward_kernel, parts, tq),
        grid_spec=pltpu.PrefetchScalarGridSpec(
            num_scalar_prefetch=2,
            grid=(mem.shape[0] - 1,),
            in_specs=[
                pl.BlockSpec((1, n, 2 * D), by_memory),
                pl.BlockSpec((1, n, D), by_memory),
                pl.BlockSpec((2 * D, D), lambda j, *_: (0, 0)),
                pl.BlockSpec(memory_space=pl.ANY),
            ]
            + [whole] * (2 * parts)
            + [flat] * parts,
            out_specs=[
                pl.BlockSpec((1, n, D), by_memory),
                pl.BlockSpec((2 * D, D), lambda j, *_: (0, 0)),
                pl.BlockSpec((8, D), lambda j, *_: (0, 0)),
            ]
            + [whole] * parts,
            scratch_shapes=[
                pltpu.VMEM((n, D), F32),
                pltpu.VMEM((n, D), F32),
                pltpu.VMEM((parts, rows, D), F32),
            ],
        ),
        out_shape=[
            jax.ShapeDtypeStruct((blocks, n, D), BF),
            jax.ShapeDtypeStruct((2 * D, D), F32),
            jax.ShapeDtypeStruct((8, D), F32),
        ]
        + [jax.ShapeDtypeStruct((rows, D), BF)] * parts,
        input_output_aliases={5: 0},
        compiler_params=pltpu.CompilerParams(vmem_limit_bytes=VMEM_BYTES),
        cost_estimate=cost(32),
        name="cross_backward",
    )(mem, table, kv, rows_of_memory, weights, zeros, *queries, *upstream, *stats)


def norm(z):
    centre = z - jnp.mean(z, axis=1, keepdims=True)
    inverse = lax.rsqrt(jnp.mean(centre * centre, axis=1, keepdims=True) + EPSILON)
    return centre * inverse, inverse


def norm_back(upstream, normed, inverse, gain):
    scaled = upstream * gain
    return inverse * (
        scaled
        - jnp.mean(scaled, axis=1, keepdims=True)
        - normed * jnp.mean(scaled * normed, axis=1, keepdims=True)
    )


def total(x):
    return jnp.sum(x, axis=0, keepdims=True)


def head_rows():
    lane = lax.broadcasted_iota(jnp.int32, (HEADS, D), 1) // HD
    return (lane == lax.broadcasted_iota(jnp.int32, (HEADS, D), 0)).astype(F32).astype(BF)


def per_head(product):
    hi, lo = hi_lo(product)
    heads = head_rows()
    return dot_nt(heads, hi) + dot_nt(heads, lo)


def spread(rows):
    hi, lo = hi_lo(rows)
    heads = head_rows()
    return dot_tn(hi, heads) + dot_tn(lo, heads)


def first_kernel(x_ref, att_ref, wo_ref, wq_ref, vec_ref, z_ref, cq_ref):
    z = x_ref[...].astype(F32) + dot_nt(att_ref[...], wo_ref[...]) + vec_ref[5:6, :]
    z_ref[...] = z
    n, _ = norm(z)
    low = (n * vec_ref[0:1, :] + vec_ref[10:11, :]).astype(BF)
    cq_ref[...] = ((dot_nt(low, wq_ref[...]) + vec_ref[6:7, :]).astype(BF) * SCALE).astype(BF)


def first_rows(x, att, wo, wq, vec):
    rows = x.shape[0]
    return pl.pallas_call(
        first_kernel,
        out_shape=[jax.ShapeDtypeStruct((rows, D), F32), jax.ShapeDtypeStruct((rows, D), BF)],
        compiler_params=pltpu.CompilerParams(vmem_limit_bytes=VMEM_BYTES),
        cost_estimate=cost(4),
        name="first_rows",
    )(x, att, wo, wq, vec)


def middle_kernel(parts, chunks, *refs):
    z1_ref, cot_ref = refs[:2]
    outs = refs[2 : 2 + parts]
    lses = refs[2 + parts : 2 + 2 * parts]
    wco_ref, w1_ref, w2_ref, vec_ref, fb_ref = refs[2 + 2 * parts : 7 + 2 * parts]
    (
        y_ref, dz2_ref, dcatt_ref, stat_ref, gwco_ref, gw1_ref, gw2_ref, gvec_ref, gfb_ref, hid_ref, slope_ref,
    ) = refs[7 + 2 * parts :]
    vec = lambda i: vec_ref[i : i + 1, :]
    peak = lses[0][...]
    for part in range(1, parts):
        peak = jnp.maximum(peak, lses[part][...])
    mass = 0.0
    for part in range(parts):
        mass = mass + jnp.exp(lses[part][...] - peak)
    lse = peak + jnp.log(mass)
    catt32 = 0.0
    for part in range(parts):
        catt32 = catt32 + spread(jnp.exp(lses[part][...] - lse)) * outs[part][...].astype(F32)
    catt = catt32.astype(BF)
    n1, _ = norm(z1_ref[...])
    h1 = n1 * vec(0) + vec(10)
    z2 = h1 + dot_nt(catt, wco_ref[...]) + vec(8)
    n2, r2 = norm(z2)
    h2 = n2 * vec(1) + vec(11)
    h2_low = h2.astype(BF)
    z3 = h2 + vec(9)
    for c in range(chunks):
        cols = slice(c * D, (c + 1) * D)
        u = dot_nt(h2_low, w1_ref[cols, :]) + fb_ref[:, cols]
        square = u * u
        t = jnp.tanh(GELU_SCALE * (u + 0.044715 * u * square))
        hid = (0.5 * u * (1.0 + t)).astype(BF)
        hid_ref[:, cols] = hid
        slope_ref[:, cols] = 0.5 * (1.0 + t) + 0.5 * u * (1.0 - t * t) * (
            GELU_SCALE * (1.0 + 3.0 * 0.044715 * square)
        )
        z3 = z3 + dot_nt(hid, w2_ref[c])
    n3, r3 = norm(z3)
    y_ref[...] = n3 * vec(2) + vec(12)
    cot = cot_ref[...]
    dz3 = norm_back(cot, n3, r3, vec(2))
    df = dz3.astype(BF)
    gvec_ref[...] = jnp.zeros_like(gvec_ref)
    gvec_ref[0:1, :] = total(cot * n3)
    gvec_ref[1:2, :] = total(cot)
    gvec_ref[2:3, :] = total(df.astype(F32))
    e2 = dz3
    for c in range(chunks):
        cols = slice(c * D, (c + 1) * D)
        hid = hid_ref[:, cols]
        gw2_ref[c] = dot_tn(df, hid).astype(BF)
        du = (dot_nn(df, w2_ref[c]) * slope_ref[:, cols]).astype(BF)
        gw1_ref[cols, :] = dot_tn(du, h2_low).astype(BF)
        gfb_ref[:, cols] = total(du.astype(F32))
        e2 = e2 + dot_nn(du, w1_ref[cols, :])
    dz2 = norm_back(e2, n2, r2, vec(1))
    dz2_ref[...] = dz2
    dca = dz2.astype(BF)
    gvec_ref[3:4, :] = total(e2 * n2)
    gvec_ref[4:5, :] = total(e2)
    gvec_ref[5:6, :] = total(dca.astype(F32))
    gwco_ref[...] = dot_tn(dca, catt).astype(BF)
    dcatt = dot_nn(dca, wco_ref[...]).astype(BF)
    dcatt_ref[...] = dcatt
    stat_ref[0:HEADS, :] = lse
    stat_ref[HEADS : 2 * HEADS, :] = per_head(dcatt.astype(F32) * catt32)


def middle_rows(z1, cot, outs, lses, wco, w1, w2, vec, fb):
    rows, parts, chunks = z1.shape[0], len(outs), w2.shape[0]
    hidden = chunks * D
    return pl.pallas_call(
        functools.partial(middle_kernel, parts, chunks),
        out_shape=[
            jax.ShapeDtypeStruct((rows, D), F32),
            jax.ShapeDtypeStruct((rows, D), F32),
            jax.ShapeDtypeStruct((rows, D), BF),
            jax.ShapeDtypeStruct((2 * HEADS, rows), F32),
            jax.ShapeDtypeStruct((D, D), BF),
            jax.ShapeDtypeStruct((hidden, D), BF),
            jax.ShapeDtypeStruct((chunks, D, D), BF),
            jax.ShapeDtypeStruct((8, D), F32),
            jax.ShapeDtypeStruct((1, hidden), F32),
        ],
        scratch_shapes=[pltpu.VMEM((rows, hidden), BF), pltpu.VMEM((rows, hidden), F32)],
        compiler_params=pltpu.CompilerParams(vmem_limit_bytes=VMEM_BYTES),
        cost_estimate=cost(18),
        name="middle_rows",
    )(z1, cot, *outs, *lses, wco, w1, w2, vec, fb)


def last_kernel(parts, *refs):
    z1_ref, dz2_ref, att_ref = refs[:3]
    dcqs = refs[3 : 3 + parts]
    wq_ref, wo_ref, vec_ref = refs[3 + parts : 6 + parts]
    dz1_ref, datt_ref, delta_ref, gwo_ref, gwq_ref, gvec_ref = refs[6 + parts :]
    dcq = 0.0
    for part in dcqs:
        dcq = dcq + part[...].astype(F32)
    dcq = dcq.astype(BF)
    n1, r1 = norm(z1_ref[...])
    low = (n1 * vec_ref[0:1, :] + vec_ref[10:11, :]).astype(BF)
    e1 = dz2_ref[...] + dot_nn(dcq, wq_ref[...])
    dz1 = norm_back(e1, n1, r1, vec_ref[0:1, :])
    dz1_ref[...] = dz1
    da = dz1.astype(BF)
    datt = dot_nn(da, wo_ref[...]).astype(BF)
    datt_ref[...] = datt
    delta_ref[...] = per_head(datt.astype(F32) * att_ref[...].astype(F32))
    gwo_ref[...] = dot_tn(da, att_ref[...]).astype(BF)
    gwq_ref[...] = dot_tn(dcq, low).astype(BF)
    gvec_ref[...] = jnp.zeros_like(gvec_ref)
    gvec_ref[0:1, :] = total(e1 * n1)
    gvec_ref[1:2, :] = total(e1)
    gvec_ref[2:3, :] = total(da.astype(F32))
    gvec_ref[3:4, :] = total(dcq.astype(F32))


def last_rows(z1, dz2, att, dcqs, wq, wo, vec):
    rows = z1.shape[0]
    return pl.pallas_call(
        functools.partial(last_kernel, len(dcqs)),
        out_shape=[
            jax.ShapeDtypeStruct((rows, D), F32),
            jax.ShapeDtypeStruct((rows, D), BF),
            jax.ShapeDtypeStruct((HEADS, rows), F32),
            jax.ShapeDtypeStruct((D, D), BF),
            jax.ShapeDtypeStruct((D, D), BF),
            jax.ShapeDtypeStruct((8, D), F32),
        ],
        compiler_params=pltpu.CompilerParams(vmem_limit_bytes=VMEM_BYTES),
        cost_estimate=cost(6),
        name="last_rows",
    )(z1, dz2, att, *dcqs, wq, wo, vec)


def scatter_rows(grid, groups):
    z, x, c, y = (grid.size[d] for d in ("z", "x", "c", "y"))
    packed = jnp.concatenate(
        [g.reshape(z, x, c, y, g.shape[0] // grid.count, D).astype(BF) for g in groups], axis=4
    )
    packed = grid.reduce(packed, 2, "c")
    half = packed.shape[3] // 2
    a, b = packed[:, :, :, :half], packed[:, :, :, half:]
    a = grid.reduce(grid.reduce(a.astype(BF), 2, "y").astype(BF), 1, "x")
    b = grid.reduce(grid.reduce(b.astype(BF), 1, "x").astype(BF), 1, "y")
    a = grid.reduce(a.astype(BF), 0, "z")
    b = grid.reduce(b.astype(BF), 0, "z")
    out = jnp.concatenate([a, b], axis=0)
    pieces, start = [], 0
    for g in groups:
        n = g.shape[0] // grid.count
        pieces.append(out[start : start + n])
        start += n
    return pieces


def scatter_memory(grid, grads):
    z, x, c = (grid.size[d] for d in ("z", "x", "c"))
    n = grads.shape[1]
    buffer = grid.reduce(grads.reshape(z, x, c, n, D), 2, "c")
    half = n // 2
    a, b = buffer[:, :, :half], buffer[:, :, half:]
    a = grid.reduce(grid.reduce(a, 1, "x").astype(BF), 0, "z")
    b = grid.reduce(grid.reduce(b, 0, "z").astype(BF), 0, "x")
    return jnp.concatenate([a, b], axis=0)


def one_hot(targets, count):
    return (lax.broadcasted_iota(jnp.int32, (count, targets.shape[0]), 0) == targets[None, :]).astype(BF)


def body(
    tokens,
    memory,
    cotangent,
    deal_order,
    lengths,
    mem_index,
    self_qkv,
    self_out,
    cross_qkv,
    cross_out,
    ffn_in,
    ffn_out,
    norm_gains,
    biases,
    ffn_bias,
):
    grid = Grid()
    heads, blocks = grid.head, grid.blk
    rows = tokens.shape[0]
    block_rows = rows * heads
    mem_rows = memory.shape[0]
    assert mem_rows * heads == MEM
    block = lax.axis_index("blk")
    here = lax.axis_index("head")
    chunks = ffn_out.shape[0] // D

    w_qkv, w_so, w_cqkv, w_co, w_in = (
        w.T for w in (self_qkv, self_out, cross_qkv, cross_out, ffn_in)
    )
    w_out = jnp.transpose(ffn_out.reshape(chunks, D, -1), (0, 2, 1)).reshape(-1, D)
    n_out = w_so.shape[0]
    lanes = norm_gains.shape[1]
    small = jnp.concatenate([norm_gains.reshape(-1), biases.reshape(-1), ffn_bias])
    small = jnp.pad(small[None], ((0, 15), (0, D - small.shape[0])))
    nowhere = [{}]

    near = [tokens] + grid.others(tokens, "y")
    in_group = deal_order - block * block_rows
    groups = [lax.dynamic_slice_in_dim(in_group, ((here - k) % heads) * rows, rows) for k in range(heads)]
    stream_rows = dot_nn(one_hot(jnp.concatenate(groups), block_rows), jnp.concatenate(near, axis=0)).astype(BF)
    up = [(i, i + heads) for i in range(grid.count - heads)]
    down = [(j, i) for i, j in up]
    before = lax.ppermute(stream_rows, BOTH, up)
    behind = lax.ppermute(stream_rows, BOTH, down)
    ext = jnp.concatenate([before, stream_rows, behind], axis=0)

    first_z = along(grid, [(jnp.concatenate([w_qkv, small], axis=0)[None], nowhere)], "z", True)
    held = first_z
    for dim in "xyc":
        held = along(grid, held, dim, False)
    wt_qkv, wt_small = place(grid, held, [w_qkv.shape[0], 16])
    middle = after(jnp.concatenate([w_so, w_cqkv], axis=0)[None], first_z[0][0])
    middle_z = along(grid, [(middle, nowhere)], "z", True)
    held = middle_z
    for dim in "xyc":
        held = along(grid, held, dim, False)
    wt_so, wt_cqkv = place(grid, held, [n_out, w_cqkv.shape[0]])

    half = mem_rows // 2
    mem_a = along(grid, [(after(memory[None, :half], first_z[0][0]), nowhere)], "z", True)
    mem_b = along(grid, [(after(memory[None, half:], first_z[0][0]), nowhere)], "x", True)
    mem_a = along(grid, along(grid, mem_a, "x", False), "c", False)
    mem_b = along(grid, along(grid, mem_b, "z", True), "c", False)
    held_memory = [(x, p, 0) for x, p in mem_a] + [(x, p, half) for x, p in mem_b]

    late = after(jnp.concatenate([w_co, w_in, w_out], axis=0)[None], middle_z[0][0])
    held = along(grid, [(late, nowhere)], "z", True)
    for dim in "xyc":
        held = along(grid, held, dim, False)
    wt_co, wt_in, *wt_out = place(grid, held, [n_out, w_in.shape[0]] + [n_out] * chunks)
    w2 = jnp.stack(wt_out)
    smalls = wt_small.reshape(grid.count, 16, D)[:, 0, : 13 * lanes + ffn_bias.shape[0]].astype(F32)
    vec = jnp.transpose(smalls[:, : 13 * lanes].reshape(grid.count, 13, lanes), (1, 0, 2)).reshape(13, D)
    vec = jnp.pad(vec, ((0, 3), (0, 0)))
    hidden_bias = smalls[:, 13 * lanes :].reshape(1, -1)

    place_own = groups[0]
    rank = jnp.sum((place_own[None, :] < place_own[:, None]).astype(jnp.int32), axis=1)
    order = one_hot(rank, rows)
    x = dot_nn(order, tokens).astype(BF)
    cot_hi, cot_lo = hi_lo(cotangent)
    cot = dot_nn(order, cot_hi) + dot_nn(order, cot_lo)
    spot = jnp.sum(jnp.where(rank[None, :] == jnp.arange(rows)[:, None], place_own[None, :], 0), axis=1)
    spot = spot + block_rows
    count = lengths.shape[0]
    tri = jnp.arange(count)[None, :] <= jnp.arange(count)[:, None]
    ends = jnp.sum(jnp.where(tri, lengths[None, :], 0), axis=1)
    starts = ends - lengths
    base = (block - 1) * block_rows
    ext_ends, ext_starts = ends - base, starts - base
    passed = ext_ends[None, :] <= spot[:, None]
    row_begin = jnp.max(jnp.where(passed, ext_ends[None, :], -base), axis=1)
    row_end = jnp.min(jnp.where(passed, jnp.int32(1 << 30), ext_ends[None, :]), axis=1)
    lane = jnp.arange(128)[None, :]
    ranges = jnp.where(lane == 0, row_begin[:, None], row_end[:, None])
    row_ranges = jnp.where(jnp.arange(8)[:, None] == 0, row_begin[None, :], row_end[None, :])
    tq = min(128, rows)
    tk = 256
    lo = jnp.min(row_begin.reshape(-1, tq), axis=1) // tk
    hi = (jnp.max(row_end.reshape(-1, tq), axis=1) + tk - 1) // tk
    lo = jnp.maximum(lo, 0)
    hi = jnp.minimum(hi, 3 * block_rows // tk)

    inside = (ext_starts < 2 * block_rows) & (ext_ends > block_rows)
    number = jnp.arange(count)
    key = jnp.where(inside, mem_index * count + number, blocks * count * 2 + number)
    slot = jnp.sum((key[None, :] < key[:, None]).astype(jnp.int32), axis=1)
    stacked = jnp.stack(groups)
    first = jnp.sum((stacked[None] + block_rows < ext_starts[:, None, None]).astype(jnp.int32), axis=2)
    final = jnp.sum((stacked[None] + block_rows < ext_ends[:, None, None]).astype(jnp.int32), axis=2)
    columns = jnp.concatenate(
        [mem_index[:, None], jnp.stack([first, final], axis=2).reshape(count, -1)], axis=1
    )
    sorted_columns = jnp.sum(
        jnp.where((slot[None, :] == number[:, None])[:, :, None], columns[None], 0), axis=1
    )
    steps = jnp.sum(inside.astype(jnp.int32))
    live = number < steps
    final_mem = jnp.sum(jnp.where(number == steps - 1, sorted_columns[:, 0], 0))
    mem_table = jnp.concatenate([jnp.where(live, sorted_columns[:, 0], final_mem), steps[None]])
    row_table = jnp.where(live[:, None], sorted_columns[:, 1:], 0).reshape(-1)

    bias_q, bias_v = vec[3], vec[4]
    q = ((dot_nt(x, wt_qkv[:D]) + bias_q).astype(BF) * SCALE).astype(BF)
    kv = (dot_nt(ext, wt_qkv[D:]) + jnp.concatenate([jnp.zeros((D,), F32), bias_v])).astype(BF)
    pairs = PAIRS if 3 * block_rows <= 4096 else 1
    att, lse = self_forward(q, kv, ranges, lo, hi, tq, tk, pairs)
    z1, cq = first_rows(x, att, wt_so, wt_cqkv[:D], vec)

    queries = [cq] + grid.others(cq, "y")
    wt_ckv = wt_cqkv[D:]
    bias_kv = jnp.concatenate([jnp.zeros((D,), F32), vec[7]])[None]
    mem_all, mem_kv = memory_kv(grid, mem_table, held_memory, wt_ckv, bias_kv)
    ctq = min(128, rows)
    outs, lses = cross_forward(mem_table, row_table, mem_kv, queries, ctq)
    own_outs = [outs[0]] + [grid.shift(outs[k], "y", -k) for k in range(1, heads)]
    own_lses = [lses[0]] + [grid.shift(lses[k], "y", -k) for k in range(1, heads)]

    y, dz2, dcatt, stat, g_co, g_in, g_out, gvec2, g_fb = middle_rows(
        z1, cot, own_outs, own_lses, wt_co, wt_in, w2, vec, hidden_bias
    )
    upstream = [dcatt] + grid.others(dcatt, "y")
    stats = [stat] + grid.others(stat, "y")
    zeros = jnp.zeros((blocks, mem_rows, D), BF)
    gm, g_ckv, g_bv, *dcqs = cross_backward(
        mem_table, row_table, mem_kv, mem_all, wt_ckv, zeros, queries, upstream, stats, ctq
    )
    own_dcqs = [dcqs[0]] + [grid.shift(dcqs[k], "y", -k) for k in range(1, heads)]
    dz1, datt, delta, g_so, g_cq, gvec1 = last_rows(z1, dz2, att, own_dcqs, wt_cqkv[:D], wt_so, vec)
    delta = jnp.pad(delta.reshape(PAIRS, 2, rows), ((0, 0), (0, 6), (0, 0)))
    dq, dk, dv = self_backward(q, datt, kv, row_ranges, lse, delta, lo, hi, tq, tk, pairs)

    back = (dot_nn(dk, wt_qkv[D : 2 * D]) + dot_nn(dv, wt_qkv[2 * D :])).astype(BF)
    from_next = lax.ppermute(back[:block_rows], BOTH, down)
    from_prior = lax.ppermute(back[2 * block_rows :], BOTH, up)
    shared = (
        back[block_rows : 2 * block_rows].astype(F32) + from_next.astype(F32) + from_prior.astype(F32)
    ).astype(BF)

    def dealt(k):
        picks = lax.broadcasted_iota(jnp.int32, (rows, block_rows), 1) == groups[k][:, None]
        return dot_nn(picks.astype(BF), shared)

    grad_in = dz1 + dot_nn(dq, wt_qkv[:D])
    grad_hi, grad_lo = hi_lo(grad_in)
    grad_input = dot_tn(order, grad_hi) + dot_tn(order, grad_lo) + dealt(0)
    for k in range(1, heads):
        grad_input = grad_input + grid.shift(dealt(k).astype(BF), "y", -k).astype(F32)
    y_hi, y_lo = hi_lo(y)
    layer_out = dot_tn(order, y_hi) + dot_tn(order, y_lo)
    grad_memory = scatter_memory(grid, gm)

    g_qkv = jnp.concatenate([dot_tn(dq, x), dot_tn(dk, ext), dot_tn(dv, ext)], axis=0)
    sum_q = jnp.sum(dq.astype(F32), axis=0)
    sum_v = jnp.sum(dv.astype(F32), axis=0)
    gvec = jnp.stack(
        [
            gvec1[0],
            gvec2[3],
            gvec2[0],
            sum_q,
            sum_v,
            gvec1[2],
            gvec1[3],
            g_bv[0],
            gvec2[5],
            gvec2[2],
            gvec1[1],
            gvec2[4],
            gvec2[1],
        ]
    )
    g_small = jnp.concatenate(
        [
            jnp.transpose(gvec.reshape(13, grid.count, lanes), (1, 0, 2)).reshape(grid.count, -1),
            g_fb.reshape(grid.count, -1),
        ],
        axis=1,
    )
    g_small = jnp.pad(g_small[:, None], ((0, 0), (0, 15), (0, D - g_small.shape[1])))
    s_in, s_co, *s_out = scatter_rows(grid, [g_in, g_co] + [g_out[c] for c in range(chunks)])
    s_so, s_cq, s_ckv = scatter_rows(grid, [g_so, jnp.concatenate([g_cq, g_ckv.astype(BF)], axis=0)]) + [None]
    s_qkv, s_small = scatter_rows(grid, [g_qkv, g_small.reshape(-1, D)])
    s_small = s_small[0]
    return (
        layer_out,
        grad_input,
        grad_memory,
        s_qkv.T,
        s_so.T,
        s_cq.T,
        s_co.T,
        s_in.T,
        jnp.concatenate([s.T for s in s_out], axis=0),
        s_small[: 3 * lanes].reshape(3, lanes),
        s_small[3 * lanes : 13 * lanes].reshape(10, lanes),
        s_small[13 * lanes : 13 * lanes + ffn_bias.shape[0]],
    )


def solution(mesh):
    rows = P(BOTH, None)
    cols = P(None, BOTH)
    return jax.shard_map(
        body,
        mesh=mesh,
        in_specs=(rows, rows, rows, P("blk"), P(), P()) + (cols,) * 8 + (P(BOTH),),
        out_specs=(rows,) * 3 + (cols,) * 8 + (P(BOTH),),
        check_vma=False,
    )
```

```python
import functools
import math

import jax
import jax.numpy as jnp
import numpy as np
from jax import lax
from jax.experimental import pallas as pl
from jax.experimental.pallas import tpu as pltpu
from jax.sharding import PartitionSpec as P

D = 512
HEADS = 8
MEM = 1024
HD = D // HEADS
PAIRS = HEADS // 2
SCALE = 1.0 / math.sqrt(HD)
EPSILON = 1e-05
GELU_SCALE = 0.7978845608028654
FILL = -1e30
FLOOR = -1e20
BOTH = ("blk", "head")
BF = jnp.bfloat16
F32 = jnp.float32
VMEM_BYTES = 60 * 1024 * 1024


def dot_nn(a, b):
    return lax.dot_general(a, b, (((1,), (0,)), ((), ())), preferred_element_type=F32)


def dot_nt(a, b):
    return lax.dot_general(a, b, (((1,), (1,)), ((), ())), preferred_element_type=F32)


def dot_tn(a, b):
    return lax.dot_general(a, b, (((0,), (0,)), ((), ())), preferred_element_type=F32)


def hi_lo(x):
    hi = x.astype(BF)
    return hi, (x - hi.astype(F32)).astype(BF)


class Grid:
    def __init__(self):
        self.blk = lax.axis_size("blk")
        self.head = lax.axis_size("head")
        self.core = 2 if self.blk % 2 == 0 else 1
        rest = self.blk // self.core
        major = 4 if rest % 4 == 0 else rest
        self.size = {"z": major, "x": rest // major, "c": self.core, "y": self.head}
        self.stride = {
            "y": 1,
            "c": self.head,
            "x": self.head * self.core,
            "z": self.head * self.core * (rest // major),
        }
        self.count = self.blk * self.head
        b = lax.axis_index("blk")
        self.at = {
            "y": lax.axis_index("head"),
            "c": b % self.core,
            "x": (b // self.core) % self.size["x"],
            "z": b // (self.core * self.size["x"]),
        }

    def shift(self, array, **steps):
        route = []
        for i in range(self.count):
            to = i
            for dim, step in steps.items():
                size, stride = self.size[dim], self.stride[dim]
                at = (i // stride) % size
                to += ((at + step) % size - at) * stride
            route.append((i, to))
        return lax.ppermute(array, BOTH, route)

    def offsets(self, dims):
        out = [{}]
        for dim in dims:
            out = [dict(o, **{dim: k}) for o in out for k in range(self.size[dim])]
        return out[1:]

    def others(self, array, dims):
        return [self.shift(array, **o) for o in self.offsets(dims)]

    def entry(self, buffer, first, dims, steps):
        for dim in reversed(dims):
            axis = first + dims.index(dim)
            index = (self.at[dim] + steps.get(dim, 0)) % self.size[dim]
            buffer = lax.dynamic_index_in_dim(buffer, index, axis, keepdims=False)
        return buffer

    def ahead(self, buffer, dim):
        return [buffer[0]] + [self.shift(buffer[k], **{dim: k}) for k in range(1, self.size[dim])]

    def terms(self, buffer, first, dims):
        moved = [self.shift(self.entry(buffer, first, dims, o).astype(BF), **o) for o in self.offsets(dims)]
        return [self.entry(buffer, first, dims, {})] + moved


def add(terms, dtype=BF):
    return sum(t.astype(F32) for t in terms).astype(dtype)


def beside(outputs, arrays):
    return lax.optimization_barrier((outputs, arrays))


def after(values, *first):
    return lax.optimization_barrier((values, *first))[0]


def cost(us):
    return pl.CostEstimate(flops=int(us * 1e3), transcendentals=0, bytes_accessed=0)


def along(grid, held, dims, join):
    out = []
    for array, places in held:
        arrays = [array] + grid.others(array, dims)
        tagged = [[dict(p, **o) for p in places] for o in [{}] + grid.offsets(dims)]
        if join:
            out.append((jnp.concatenate(arrays, axis=0), sum(tagged, [])))
        else:
            out += list(zip(arrays, tagged))
    return out


def place_kernel(z_size, rows, index_ref, *refs):
    arrays, outs = refs[: len(refs) - len(rows)], refs[len(refs) - len(rows) :]
    each = arrays[0].shape[0] // z_size
    i = pl.program_id(0)
    for a, array in enumerate(arrays):

        @pl.when(i // each == a)
        def _(array=array):
            for z in range(z_size):
                source = (i % each) * z_size + (index_ref[0] - z + z_size) % z_size
                start = 0
                for out, n in zip(outs, rows):
                    out[z, 0] = array[source, start : start + n, :]
                    start += n


def place(grid, held, rows):
    arrays = [a for a, _ in held]
    z_size = grid.size["z"]
    other = grid.count // z_size
    slot = []
    for _, places in held:
        for p in places[::z_size]:
            at = 0
            for dim in "xcy":
                at = at * grid.size[dim] + (grid.at[dim] - p.get(dim, 0)) % grid.size[dim]
            slot.append(at)
    index = jnp.stack([grid.at["z"]] + slot).astype(jnp.int32)
    outs = pl.pallas_call(
        functools.partial(place_kernel, z_size, rows),
        grid_spec=pltpu.PrefetchScalarGridSpec(
            num_scalar_prefetch=1,
            grid=(other,),
            in_specs=[pl.BlockSpec(a.shape, lambda i, _: (0, 0, 0)) for a in arrays],
            out_specs=[
                pl.BlockSpec((z_size, 1, n, D), lambda i, index: (0, index[i + 1], 0, 0)) for n in rows
            ],
        ),
        out_shape=[jax.ShapeDtypeStruct((z_size, other, n, D), BF) for n in rows],
        compiler_params=pltpu.CompilerParams(vmem_limit_bytes=VMEM_BYTES),
        cost_estimate=cost(5),
        name="place_weights",
    )(index, *arrays)
    return [out.reshape(grid.count * n, D) for out, n in zip(outs, rows)]


def lane_mask(rows):
    return lax.broadcasted_iota(jnp.int32, (rows, 2 * HD), 1) < HD


def two(low, x):
    zero = jnp.zeros_like(x)
    return jnp.concatenate([jnp.where(low, x, zero), jnp.where(low, zero, x)], axis=0)


def pick(low, x):
    half = x.shape[0] // 2
    return jnp.where(low, x[:half], x[half:])


def with_ones(v):
    return jnp.concatenate([v, jnp.ones_like(v)], axis=1)


def pair_cols(g):
    return slice(g * 2 * HD, (g + 1) * 2 * HD)


def self_forward_kernel(
    pairs, tq, tk, lo_ref, hi_ref, q_ref, k_ref, v_ref, range_ref, att_ref, lse_ref, score_ref, top_ref, acc_ref
):
    width = 2 * HD
    low = lane_mask(tq)
    for i in range(q_ref.shape[0] // tq):
        rows = pl.ds(i * tq, tq)
        begin = jnp.concatenate([range_ref[rows, 0:1]] * 2, axis=0)
        end = jnp.concatenate([range_ref[rows, 1:2]] * 2, axis=0)
        first = lo_ref[i]
        top_ref[...] = jnp.full_like(top_ref, FILL)
        acc_ref[...] = jnp.zeros_like(acc_ref)

        def scores(t, carry, i=i):
            keys = pl.ds(pl.multiple_of(t * tk, tk), tk)
            spot = pl.ds(pl.multiple_of((t - first) * tk, tk), tk)
            place = lax.broadcasted_iota(jnp.int32, (2 * tq, tk), 1) + t * tk
            allowed = (place >= begin) & (place < end)
            for g in range(pairs):
                s = dot_nt(two(low, q_ref[pl.ds(i * tq, tq), pair_cols(g)]), k_ref[keys, pair_cols(g)])
                s = jnp.where(allowed, s, FILL)
                score_ref[g, :, spot] = s
                peak = top_ref[g]
                for c in range(tk // width):
                    peak = jnp.maximum(peak, s[:, c * width : (c + 1) * width])
                top_ref[g] = peak
            return carry

        lax.fori_loop(first, hi_ref[i], scores, 0)
        for g in range(pairs):
            peak = jnp.max(top_ref[g], axis=1, keepdims=True)
            top_ref[g] = jnp.broadcast_to(peak, (2 * tq, width))

        def weigh(t, carry):
            keys = pl.ds(pl.multiple_of(t * tk, tk), tk)
            spot = pl.ds(pl.multiple_of((t - first) * tk, tk), tk)
            for g in range(pairs):
                p = jnp.exp(score_ref[g, :, spot] - top_ref[g, :, 0:1]).astype(BF)
                acc_ref[g] += dot_nn(p, with_ones(v_ref[keys, pair_cols(g)]))
            return carry

        lax.fori_loop(first, hi_ref[i], weigh, 0)
        for g in range(pairs):
            mass = acc_ref[g, :, width:]
            att_ref[rows, pair_cols(g)] = pick(low, acc_ref[g, :, :width] / mass).astype(BF)
            flat = (top_ref[g] + jnp.log(mass)).T
            lse_ref[g, 0:1, rows] = flat[0:1, :tq]
            lse_ref[g, 1:2, rows] = flat[0:1, tq:]


def self_forward(q, kv, ranges, lo, hi, tq, tk, pairs):
    rows, keys = q.shape[0], kv.shape[0]
    width = pairs * 2 * HD
    groups = PAIRS // pairs
    return pl.pallas_call(
        functools.partial(self_forward_kernel, pairs, tq, tk),
        grid_spec=pltpu.PrefetchScalarGridSpec(
            num_scalar_prefetch=2,
            grid=(groups,),
            in_specs=[
                pl.BlockSpec((rows, width), lambda g, *_: (0, g)),
                pl.BlockSpec((keys, width), lambda g, *_: (0, g)),
                pl.BlockSpec((keys, width), lambda g, *_: (0, groups + g)),
                pl.BlockSpec((rows, 128), lambda g, *_: (0, 0)),
            ],
            out_specs=[
                pl.BlockSpec((rows, width), lambda g, *_: (0, g)),
                pl.BlockSpec((pairs, 8, rows), lambda g, *_: (g, 0, 0)),
            ],
            scratch_shapes=[
                pltpu.VMEM((pairs, 2 * tq, keys), F32),
                pltpu.VMEM((pairs, 2 * tq, 2 * HD), F32),
                pltpu.VMEM((pairs, 2 * tq, 4 * HD), F32),
            ],
        ),
        out_shape=[
            jax.ShapeDtypeStruct((rows, D), BF),
            jax.ShapeDtypeStruct((PAIRS, 8, rows), F32),
        ],
        compiler_params=pltpu.CompilerParams(vmem_limit_bytes=VMEM_BYTES),
        cost_estimate=cost(20),
        name="self_forward",
    )(lo, hi, q, kv, kv, ranges)


def self_backward_kernel(
    pairs, tq, tk, lo_ref, hi_ref, q_ref, do_ref, k_ref, v_ref, row_ref, lse_ref, delta_ref, dq_ref, dk_ref, dv_ref,
    acc_q, acc_k, acc_v,
):
    low = lane_mask(tq)
    acc_k[...] = jnp.zeros_like(acc_k)
    acc_v[...] = jnp.zeros_like(acc_v)
    for i in range(q_ref.shape[0] // tq):
        rows = pl.ds(i * tq, tq)
        begin = jnp.concatenate([row_ref[0:1, rows]] * 2, axis=1)
        end = jnp.concatenate([row_ref[1:2, rows]] * 2, axis=1)
        acc_q[...] = jnp.zeros_like(acc_q)

        def step(t, carry, i=i):
            rows = pl.ds(i * tq, tq)
            keys = pl.ds(pl.multiple_of(t * tk, tk), tk)
            place = lax.broadcasted_iota(jnp.int32, (tk, 2 * tq), 0) + t * tk
            allowed = (place >= begin) & (place < end)
            for g in range(pairs):
                cols = pair_cols(g)
                k, v = k_ref[keys, cols], v_ref[keys, cols]
                q2, do2 = two(low, q_ref[rows, cols]), two(low, do_ref[rows, cols])
                lse = jnp.concatenate([lse_ref[g, 0:1, rows], lse_ref[g, 1:2, rows]], axis=1)
                delta = jnp.concatenate([delta_ref[g, 0:1, rows], delta_ref[g, 1:2, rows]], axis=1)
                p = jnp.exp(jnp.where(allowed, dot_nt(k, q2) - lse, FILL))
                ds = (p * (dot_nt(v, do2) - delta)).astype(BF)
                acc_v[keys, cols] += dot_nn(p.astype(BF), do2)
                acc_k[keys, cols] += dot_nn(ds, q2)
                acc_q[g] += dot_tn(ds, k)
            return carry

        lax.fori_loop(lo_ref[i], hi_ref[i], step, 0)
        for g in range(pairs):
            dq_ref[rows, pair_cols(g)] = (pick(low, acc_q[g]) * SCALE).astype(BF)
    dk_ref[...] = acc_k[...].astype(BF)
    dv_ref[...] = acc_v[...].astype(BF)


def self_backward(q, do, kv, row_range, lse, delta, lo, hi, tq, tk, pairs, half):
    rows, keys = q.shape[0], kv.shape[0]
    width = pairs * 2 * HD
    groups = PAIRS // pairs
    steps = groups // 2
    base = half * steps
    return pl.pallas_call(
        functools.partial(self_backward_kernel, pairs, tq, tk),
        grid_spec=pltpu.PrefetchScalarGridSpec(
            num_scalar_prefetch=2,
            grid=(steps,),
            in_specs=[
                pl.BlockSpec((rows, width), lambda g, *_: (0, base + g)),
                pl.BlockSpec((rows, width), lambda g, *_: (0, base + g)),
                pl.BlockSpec((keys, width), lambda g, *_: (0, base + g)),
                pl.BlockSpec((keys, width), lambda g, *_: (0, groups + base + g)),
                pl.BlockSpec((8, rows), lambda g, *_: (0, 0)),
                pl.BlockSpec((pairs, 8, rows), lambda g, *_: (base + g, 0, 0)),
                pl.BlockSpec((pairs, 8, rows), lambda g, *_: (base + g, 0, 0)),
            ],
            out_specs=[
                pl.BlockSpec((rows, width), lambda g, *_: (0, g)),
                pl.BlockSpec((keys, width), lambda g, *_: (0, g)),
                pl.BlockSpec((keys, width), lambda g, *_: (0, g)),
            ],
            scratch_shapes=[
                pltpu.VMEM((pairs, 2 * tq, 2 * HD), F32),
                pltpu.VMEM((keys, width), F32),
                pltpu.VMEM((keys, width), F32),
            ],
        ),
        out_shape=[
            jax.ShapeDtypeStruct((rows, D // 2), BF),
            jax.ShapeDtypeStruct((keys, D // 2), BF),
            jax.ShapeDtypeStruct((keys, D // 2), BF),
        ],
        compiler_params=pltpu.CompilerParams(vmem_limit_bytes=VMEM_BYTES),
        cost_estimate=cost(20),
        name="self_backward",
    )(lo, hi, q, do, kv, kv, row_range, lse, delta)


def memory_kv_kernel(mem_ref, m_ref, w_ref, b_ref, kv_ref):
    j = pl.program_id(0)

    @pl.when((j == 0) | (mem_ref[j] != mem_ref[jnp.maximum(j - 1, 0)]))
    def _():
        kv_ref[0] = (dot_nt(m_ref[0], w_ref[...]) + b_ref[...]).astype(BF)


def memory_kv(mem, gathered, n, weights, bias):
    blocks = gathered.shape[0]
    by_memory = lambda j, mem: (mem[j], 0, 0)
    return pl.pallas_call(
        memory_kv_kernel,
        grid_spec=pltpu.PrefetchScalarGridSpec(
            num_scalar_prefetch=1,
            grid=(mem.shape[0] - 1,),
            in_specs=[
                pl.BlockSpec((1, n, D), by_memory),
                pl.BlockSpec((2 * D, D), lambda j, *_: (0, 0)),
                pl.BlockSpec((1, 2 * D), lambda j, *_: (0, 0)),
            ],
            out_specs=pl.BlockSpec((1, n, 2 * D), by_memory),
        ),
        out_shape=jax.ShapeDtypeStruct((blocks, n, 2 * D), BF),
        compiler_params=pltpu.CompilerParams(vmem_limit_bytes=VMEM_BYTES),
        cost_estimate=cost(6),
        name="memory_kv",
    )(mem, gathered, weights, bias)


def cross_forward_kernel(parts, tq, mem_ref, table_ref, kv_ref, *refs):
    qs, outs, lses = refs[:parts], refs[parts : 2 * parts], refs[2 * parts : 3 * parts]
    width = 2 * HD
    j = pl.program_id(0)
    low = lane_mask(tq)
    for part in range(parts):
        first_row = table_ref[j * 2 * parts + 2 * part]
        last_row = table_ref[j * 2 * parts + 2 * part + 1]

        def step(t, carry, part=part, first_row=first_row, last_row=last_row):
            offset = pl.multiple_of(t * tq, tq)
            rows = pl.ds(offset, tq)
            at = lax.broadcasted_iota(jnp.int32, (tq, width), 0) + offset
            mine = (at >= first_row) & (at < last_row)
            at_row = lax.broadcasted_iota(jnp.int32, (1, tq), 1) + offset
            mine_row = (at_row >= first_row) & (at_row < last_row)
            for g in range(PAIRS):
                cols = pair_cols(g)
                s = dot_nt(two(low, qs[part][rows, cols]), kv_ref[0, :, cols])
                peak = jnp.max(s, axis=1, keepdims=True)
                p = jnp.exp(s - peak).astype(BF)
                acc = dot_nn(p, with_ones(kv_ref[0, :, pair_cols(PAIRS + g)]))
                mass = acc[:, width:]
                new = pick(low, acc[:, :width] / mass).astype(BF)
                outs[part][rows, cols] = jnp.where(mine, new, outs[part][rows, cols])
                flat = (peak + jnp.log(mass)).T
                for i in range(2):
                    head = slice(2 * g + i, 2 * g + i + 1)
                    lses[part][head, rows] = jnp.where(
                        mine_row, flat[0:1, i * tq : (i + 1) * tq], lses[part][head, rows]
                    )
            return carry

        lax.fori_loop(first_row // tq, (last_row + tq - 1) // tq, step, 0)


def cross_forward(mem, table, kv, queries, tq):
    parts, rows, n = len(queries), queries[0].shape[0], kv.shape[1]
    whole = pl.BlockSpec((rows, D), lambda j, *_: (0, 0))
    flat = pl.BlockSpec((HEADS, rows), lambda j, *_: (0, 0))
    out = pl.pallas_call(
        functools.partial(cross_forward_kernel, parts, tq),
        grid_spec=pltpu.PrefetchScalarGridSpec(
            num_scalar_prefetch=2,
            grid=(mem.shape[0] - 1,),
            in_specs=[pl.BlockSpec((1, n, 2 * D), lambda j, mem, _: (mem[j], 0, 0))] + [whole] * parts,
            out_specs=[whole] * parts + [flat] * parts,
        ),
        out_shape=[jax.ShapeDtypeStruct((rows, D), BF)] * parts
        + [jax.ShapeDtypeStruct((HEADS, rows), F32)] * parts,
        compiler_params=pltpu.CompilerParams(vmem_limit_bytes=VMEM_BYTES),
        cost_estimate=cost(16),
        name="cross_forward",
    )(mem, table, kv, *queries)
    return out[:parts], out[parts:]


def cross_backward_kernel(parts, tq, blocks, mem_ref, spot_ref, table_ref, kv_ref, m_ref, w_ref, *refs):
    qs, dos, stats = refs[:parts], refs[parts : 2 * parts], refs[2 * parts : 3 * parts]
    keep_ref, send_ref, gw_ref, gb_ref = refs[3 * parts : 3 * parts + 4]
    dqs = refs[3 * parts + 4 : 4 * parts + 4]
    acc_k, acc_v, acc_q, stage, zero, stage_sem, zero_sem = refs[4 * parts + 4 :]
    j = pl.program_id(0)
    last = mem_ref.shape[0] - 2
    steps = mem_ref[last + 1]
    now = mem_ref[j]
    previous = mem_ref[jnp.maximum(j - 1, 0)]
    following = mem_ref[jnp.minimum(j + 1, last)]
    low = lane_mask(tq)
    half = keep_ref.shape[0]

    def to_target(source, spot, sem, wanted, act):
        for target, mine in ((keep_ref, spot < half), (send_ref, spot >= half)):
            copy = pltpu.make_async_copy(source, target.at[spot % half], sem)
            pl.when(wanted & mine)(functools.partial(act, copy))

    start, wait = (lambda copy: copy.start()), (lambda copy: copy.wait())

    def zeros(act):
        for m in range(blocks):
            spot = spot_ref[m]
            to_target(zero, jnp.abs(spot) - 1, zero_sem.at[m], spot < 0, act)

    @pl.when(j == 0)
    def _():
        acc_q[...] = jnp.zeros_like(acc_q)
        gw_ref[...] = jnp.zeros_like(gw_ref)
        gb_ref[...] = jnp.zeros_like(gb_ref)
        zero[...] = jnp.zeros_like(zero)
        zeros(start)

    @pl.when((j == 0) | (now != previous))
    def _():
        acc_k[...] = jnp.zeros_like(acc_k)
        acc_v[...] = jnp.zeros_like(acc_v)

    for part in range(parts):
        first_row = table_ref[j * 2 * parts + 2 * part]
        last_row = table_ref[j * 2 * parts + 2 * part + 1]

        def step(t, carry, part=part, first_row=first_row, last_row=last_row):
            offset = pl.multiple_of(t * tq, tq)
            rows = pl.ds(offset, tq)
            at_row = lax.broadcasted_iota(jnp.int32, (1, tq), 1) + offset
            mine = (at_row >= first_row) & (at_row < last_row)
            for g in range(PAIRS):
                cols = pair_cols(g)
                k, v = kv_ref[0, :, cols], kv_ref[0, :, pair_cols(PAIRS + g)]
                q2, do2 = two(low, qs[part][rows, cols]), two(low, dos[part][rows, cols])

                def stat(base, part=part, g=g):
                    return [stats[part][base + 2 * g + i : base + 2 * g + i + 1, rows] for i in range(2)]

                lse = jnp.concatenate([jnp.where(mine, x, -FILL) for x in stat(0)], axis=1)
                delta = jnp.concatenate(stat(HEADS), axis=1)
                p = jnp.exp(dot_nt(k, q2) - lse)
                ds = (p * (dot_nt(v, do2) - delta)).astype(BF)
                acc_v[:, cols] += dot_nn(p.astype(BF), do2)
                acc_k[:, cols] += dot_nn(ds, q2)
                acc_q[part, rows, cols] += pick(low, dot_tn(ds, k))
            return carry

        lax.fori_loop(first_row // tq, (last_row + tq - 1) // tq, step, 0)

    @pl.when((j == steps - 1) | ((j < steps) & (now != following)))
    def _():
        dk, dv = acc_k[...].astype(BF), acc_v[...].astype(BF)
        spot = spot_ref[now] - 1
        stage[...] = (dot_nn(dk, w_ref[0:D, :]) + dot_nn(dv, w_ref[D : 2 * D, :])).astype(BF)
        to_target(stage, spot, stage_sem, spot >= 0, start)
        gw_ref[0:D, :] += dot_tn(dk, m_ref[0])
        gw_ref[D : 2 * D, :] += dot_tn(dv, m_ref[0])
        gb_ref[0:1, :] += jnp.sum(dv.astype(F32), axis=0, keepdims=True)
        to_target(stage, spot, stage_sem, spot >= 0, wait)

    @pl.when(j == steps - 1)
    def _():
        for part in range(parts):
            dqs[part][...] = (acc_q[part] * SCALE).astype(BF)
        zeros(wait)


def cross_backward(mem, spot, table, kv, rows_of_memory, weights, queries, upstream, stats, tq, cores):
    parts, rows, n = len(queries), queries[0].shape[0], kv.shape[1]
    blocks = kv.shape[0]
    whole = pl.BlockSpec((rows, D), lambda j, *_: (0, 0))
    flat = pl.BlockSpec((2 * HEADS, rows), lambda j, *_: (0, 0))
    by_memory = lambda j, mem, *_: (mem[j], 0, 0)
    anywhere = pl.BlockSpec(memory_space=pl.ANY)
    return pl.pallas_call(
        functools.partial(cross_backward_kernel, parts, tq, blocks),
        grid_spec=pltpu.PrefetchScalarGridSpec(
            num_scalar_prefetch=3,
            grid=(mem.shape[0] - 1,),
            in_specs=[
                pl.BlockSpec((1, n, 2 * D), by_memory),
                pl.BlockSpec((1, n, D), by_memory),
                pl.BlockSpec((2 * D, D), lambda j, *_: (0, 0)),
            ]
            + [whole] * (2 * parts)
            + [flat] * parts,
            out_specs=[
                anywhere,
                anywhere,
                pl.BlockSpec((2 * D, D), lambda j, *_: (0, 0)),
                pl.BlockSpec((8, D), lambda j, *_: (0, 0)),
            ]
            + [whole] * parts,
            scratch_shapes=[
                pltpu.VMEM((n, D), F32),
                pltpu.VMEM((n, D), F32),
                pltpu.VMEM((parts, rows, D), F32),
                pltpu.VMEM((n, D), BF),
                pltpu.VMEM((n, D), BF),
                pltpu.SemaphoreType.DMA,
                pltpu.SemaphoreType.DMA((blocks,)),
            ],
        ),
        out_shape=[jax.ShapeDtypeStruct((blocks // cores, n, D), BF)] * 2
        + [
            jax.ShapeDtypeStruct((2 * D, D), F32),
            jax.ShapeDtypeStruct((8, D), F32),
        ]
        + [jax.ShapeDtypeStruct((rows, D), BF)] * parts,
        compiler_params=pltpu.CompilerParams(vmem_limit_bytes=VMEM_BYTES),
        cost_estimate=cost(32),
        name="cross_backward",
    )(mem, spot, table, kv, rows_of_memory, weights, *queries, *upstream, *stats)


def norm(z):
    centre = z - jnp.mean(z, axis=1, keepdims=True)
    inverse = lax.rsqrt(jnp.mean(centre * centre, axis=1, keepdims=True) + EPSILON)
    return centre * inverse, inverse


def norm_back(upstream, normed, inverse, gain):
    scaled = upstream * gain
    return inverse * (
        scaled
        - jnp.mean(scaled, axis=1, keepdims=True)
        - normed * jnp.mean(scaled * normed, axis=1, keepdims=True)
    )


def total(x):
    return jnp.sum(x, axis=0, keepdims=True)


def head_rows():
    lane = lax.broadcasted_iota(jnp.int32, (HEADS, D), 1) // HD
    return (lane == lax.broadcasted_iota(jnp.int32, (HEADS, D), 0)).astype(F32).astype(BF)


def per_head(product):
    hi, lo = hi_lo(product)
    heads = head_rows()
    return dot_nt(heads, hi) + dot_nt(heads, lo)


def spread(rows):
    hi, lo = hi_lo(rows)
    heads = head_rows()
    return dot_tn(hi, heads) + dot_tn(lo, heads)


def first_kernel(x_ref, att_ref, wo_ref, wq_ref, vec_ref, z_ref, cq_ref):
    z = x_ref[...].astype(F32) + dot_nt(att_ref[...], wo_ref[...]) + vec_ref[5:6, :]
    z_ref[...] = z
    n, _ = norm(z)
    low = (n * vec_ref[0:1, :] + vec_ref[10:11, :]).astype(BF)
    cq_ref[...] = ((dot_nt(low, wq_ref[...]) + vec_ref[6:7, :]).astype(BF) * SCALE).astype(BF)


def first_rows(x, att, wo, wq, vec):
    rows = x.shape[0]
    return pl.pallas_call(
        first_kernel,
        out_shape=[jax.ShapeDtypeStruct((rows, D), F32), jax.ShapeDtypeStruct((rows, D), BF)],
        compiler_params=pltpu.CompilerParams(vmem_limit_bytes=VMEM_BYTES),
        cost_estimate=cost(4),
        name="first_rows",
    )(x, att, wo, wq, vec)


def middle_kernel(parts, chunks, *refs):
    z1_ref, cot_ref = refs[:2]
    outs = refs[2 : 2 + parts]
    lses = refs[2 + parts : 2 + 2 * parts]
    wco_ref, w1_ref, w2_ref, vec_ref, fb_ref = refs[2 + 2 * parts : 7 + 2 * parts]
    (
        y_ref, dz2_ref, dcatt_ref, stat_ref, gwco_ref, gw1_ref, gw2_ref, gvec_ref, hid_ref, slope_ref,
    ) = refs[7 + 2 * parts :]
    vec = lambda i: vec_ref[i : i + 1, :]
    peak = lses[0][...]
    for part in range(1, parts):
        peak = jnp.maximum(peak, lses[part][...])
    mass = 0.0
    for part in range(parts):
        mass = mass + jnp.exp(lses[part][...] - peak)
    lse = peak + jnp.log(mass)
    catt32 = 0.0
    for part in range(parts):
        catt32 = catt32 + spread(jnp.exp(lses[part][...] - lse)) * outs[part][...].astype(F32)
    catt = catt32.astype(BF)
    n1, _ = norm(z1_ref[...])
    h1 = n1 * vec(0) + vec(10)
    z2 = h1 + dot_nt(catt, wco_ref[...]) + vec(8)
    n2, r2 = norm(z2)
    h2 = n2 * vec(1) + vec(11)
    h2_low = h2.astype(BF)
    z3 = h2 + vec(9)
    for c in range(chunks):
        cols = slice(c * D, (c + 1) * D)
        u = dot_nt(h2_low, w1_ref[cols, :]) + fb_ref[:, cols]
        square = u * u
        t = jnp.tanh(GELU_SCALE * (u + 0.044715 * u * square))
        hid = (0.5 * u * (1.0 + t)).astype(BF)
        hid_ref[:, cols] = hid
        slope_ref[:, cols] = 0.5 * (1.0 + t) + 0.5 * u * (1.0 - t * t) * (
            GELU_SCALE * (1.0 + 3.0 * 0.044715 * square)
        )
        z3 = z3 + dot_nt(hid, w2_ref[c])
    n3, r3 = norm(z3)
    y_ref[...] = n3 * vec(2) + vec(12)
    cot = cot_ref[...]
    dz3 = norm_back(cot, n3, r3, vec(2))
    df = dz3.astype(BF)
    sums = [total(cot * n3), total(cot), total(df.astype(F32))]
    hidden_sums = []
    e2 = dz3
    for c in range(chunks):
        cols = slice(c * D, (c + 1) * D)
        hid = hid_ref[:, cols]
        gw2_ref[c] = dot_tn(df, hid).astype(BF)
        du = (dot_nn(df, w2_ref[c]) * slope_ref[:, cols]).astype(BF)
        gw1_ref[cols, :] = dot_tn(du, h2_low).astype(BF)
        hidden_sums.append(total(du.astype(F32)))
        e2 = e2 + dot_nn(du, w1_ref[cols, :])
    dz2 = norm_back(e2, n2, r2, vec(1))
    dz2_ref[...] = dz2
    dca = dz2.astype(BF)
    sums += [total(e2 * n2), total(e2), total(dca.astype(F32))] + hidden_sums
    sums += [jnp.zeros_like(sums[0])] * (-len(sums) % 16)
    gvec_ref[...] = jnp.concatenate(sums, axis=0).astype(BF)
    gwco_ref[...] = dot_tn(dca, catt).astype(BF)
    dcatt = dot_nn(dca, wco_ref[...]).astype(BF)
    dcatt_ref[...] = dcatt
    stat_ref[0:HEADS, :] = lse
    stat_ref[HEADS : 2 * HEADS, :] = per_head(dcatt.astype(F32) * catt32)


def middle_rows(z1, cot, outs, lses, wco, w1, w2, vec, fb):
    rows, parts, chunks = z1.shape[0], len(outs), w2.shape[0]
    hidden = chunks * D
    return pl.pallas_call(
        functools.partial(middle_kernel, parts, chunks),
        out_shape=[
            jax.ShapeDtypeStruct((rows, D), F32),
            jax.ShapeDtypeStruct((rows, D), F32),
            jax.ShapeDtypeStruct((rows, D), BF),
            jax.ShapeDtypeStruct((2 * HEADS, rows), F32),
            jax.ShapeDtypeStruct((D, D), BF),
            jax.ShapeDtypeStruct((hidden, D), BF),
            jax.ShapeDtypeStruct((chunks, D, D), BF),
            jax.ShapeDtypeStruct((6 + chunks + -(6 + chunks) % 16, D), BF),
        ],
        scratch_shapes=[pltpu.VMEM((rows, hidden), BF), pltpu.VMEM((rows, hidden), F32)],
        compiler_params=pltpu.CompilerParams(vmem_limit_bytes=VMEM_BYTES),
        cost_estimate=cost(18),
        name="middle_rows",
    )(z1, cot, *outs, *lses, wco, w1, w2, vec, fb)


def last_kernel(parts, *refs):
    z1_ref, dz2_ref, att_ref = refs[:3]
    dcqs = refs[3 : 3 + parts]
    wq_ref, wo_ref, vec_ref = refs[3 + parts : 6 + parts]
    dz1_ref, datt_ref, delta_ref, gwo_ref, gwq_ref, gvec_ref = refs[6 + parts :]
    dcq = 0.0
    for part in dcqs:
        dcq = dcq + part[...].astype(F32)
    dcq = dcq.astype(BF)
    n1, r1 = norm(z1_ref[...])
    low = (n1 * vec_ref[0:1, :] + vec_ref[10:11, :]).astype(BF)
    e1 = dz2_ref[...] + dot_nn(dcq, wq_ref[...])
    dz1 = norm_back(e1, n1, r1, vec_ref[0:1, :])
    dz1_ref[...] = dz1
    da = dz1.astype(BF)
    datt = dot_nn(da, wo_ref[...]).astype(BF)
    datt_ref[...] = datt
    delta_ref[...] = per_head(datt.astype(F32) * att_ref[...].astype(F32))
    gwo_ref[...] = dot_tn(da, att_ref[...]).astype(BF)
    gwq_ref[...] = dot_tn(dcq, low).astype(BF)
    gvec_ref[...] = jnp.zeros_like(gvec_ref)
    gvec_ref[0:1, :] = total(e1 * n1)
    gvec_ref[1:2, :] = total(e1)
    gvec_ref[2:3, :] = total(da.astype(F32))
    gvec_ref[3:4, :] = total(dcq.astype(F32))


def last_rows(z1, dz2, att, dcqs, wq, wo, vec):
    rows = z1.shape[0]
    return pl.pallas_call(
        functools.partial(last_kernel, len(dcqs)),
        out_shape=[
            jax.ShapeDtypeStruct((rows, D), F32),
            jax.ShapeDtypeStruct((rows, D), BF),
            jax.ShapeDtypeStruct((HEADS, rows), F32),
            jax.ShapeDtypeStruct((D, D), BF),
            jax.ShapeDtypeStruct((D, D), BF),
            jax.ShapeDtypeStruct((8, D), F32),
        ],
        compiler_params=pltpu.CompilerParams(vmem_limit_bytes=VMEM_BYTES),
        cost_estimate=cost(6),
        name="last_rows",
    )(z1, dz2, att, *dcqs, wq, wo, vec)


def self_grads_kernel(*refs):
    dqs, dks, dvs = refs[0:2], refs[2:4], refs[4:6]
    x_ref, ext_ref, w_ref, a_ref, b_ref, dx_ref, back_ref, g_ref, row_ref, acc, sum_v = refs[6:]
    j = pl.program_id(0)
    half = D // 2
    rows = lambda i, first: slice(first + i * half, first + (i + 1) * half)

    @pl.when(j == 0)
    def _():
        dx_ref[...] = sum(dot_nn(dq[...], w_ref[rows(i, 0), :]) for i, dq in enumerate(dqs))
        for i, dq in enumerate(dqs):
            g_ref[rows(i, 0), :] = dot_tn(dq[...], x_ref[...]).astype(BF)
        acc[...] = jnp.zeros_like(acc)
        sum_v[...] = jnp.zeros_like(sum_v)

    ext = ext_ref[...]
    back = 0.0
    for i in range(2):
        dk, dv = dks[i][...], dvs[i][...]
        back = back + dot_nn(dk, w_ref[rows(i, D), :]) + dot_nn(dv, w_ref[rows(i, 2 * D), :])
        acc[rows(i, 0), :] += dot_tn(dk, ext)
        acc[rows(i, D), :] += dot_tn(dv, ext)
        sum_v[0:1, rows(i, 0)] += total(dv.astype(F32))
    back_ref[...] = back.astype(BF)

    @pl.when(j == pl.num_programs(0) - 1)
    def _():
        g_ref[D : 3 * D, :] = acc[...].astype(BF)
        sum_q = jnp.concatenate([total(dq[...].astype(F32)) for dq in dqs], axis=1)
        sums = jnp.concatenate([a_ref[0:4, :], b_ref[0:1, :], sum_q, sum_v[0:1, :], a_ref[0:1, :]], axis=0)
        row_ref[...] = jnp.concatenate([sums, sums], axis=0).astype(BF)


def self_grads(dqs, dks, dvs, x, ext, w, a, b):
    rows, keys = x.shape[0], ext.shape[0]
    tile = 512
    fixed = lambda shape: pl.BlockSpec(shape, lambda j: (0, 0))
    moving = lambda width: pl.BlockSpec((tile, width), lambda j: (j, 0))
    return pl.pallas_call(
        self_grads_kernel,
        grid=(keys // tile,),
        in_specs=[fixed((rows, D // 2))] * 2
        + [moving(D // 2)] * 4
        + [fixed((rows, D)), moving(D), fixed((3 * D, D)), fixed((8, D)), fixed((8, D))],
        out_specs=[fixed((rows, D)), moving(D), fixed((3 * D, D)), fixed((16, D))],
        out_shape=[
            jax.ShapeDtypeStruct((rows, D), F32),
            jax.ShapeDtypeStruct((keys, D), BF),
            jax.ShapeDtypeStruct((3 * D, D), BF),
            jax.ShapeDtypeStruct((16, D), BF),
        ],
        scratch_shapes=[pltpu.VMEM((2 * D, D), F32), pltpu.VMEM((8, D), F32)],
        compiler_params=pltpu.CompilerParams(vmem_limit_bytes=VMEM_BYTES),
        cost_estimate=cost(12),
        name="self_grads",
    )(*dqs, *dks, *dvs, x, ext, w, a, b)


def pack(grid, groups):
    z, x, c, y = (grid.size[d] for d in "zxcy")
    return jnp.concatenate(
        [g.reshape(z, x, c, y, g.shape[0] // grid.count, D).astype(BF) for g in groups], axis=4
    )


def split(grid, summed, groups):
    pieces, start = [], 0
    for g in groups:
        n = g.shape[0] // grid.count
        pieces.append(summed[start : start + n])
        start += n
    return pieces


def one_hot(targets, count):
    return (lax.broadcasted_iota(jnp.int32, (count, targets.shape[0]), 0) == targets[None, :]).astype(BF)


def body(
    tokens,
    memory,
    cotangent,
    deal_order,
    lengths,
    mem_index,
    self_qkv,
    self_out,
    cross_qkv,
    cross_out,
    ffn_in,
    ffn_out,
    norm_gains,
    biases,
    ffn_bias,
):
    grid = Grid()
    heads, blocks = grid.head, grid.blk
    rows = tokens.shape[0]
    block_rows = rows * heads
    mem_rows = memory.shape[0]
    assert mem_rows * heads == MEM
    block = lax.axis_index("blk")
    here = lax.axis_index("head")
    chunks = ffn_out.shape[0] // D

    w_qkv, w_so, w_cqkv, w_co, w_in = (
        w.T for w in (self_qkv, self_out, cross_qkv, cross_out, ffn_in)
    )
    w_out = jnp.transpose(ffn_out.reshape(chunks, D, -1), (0, 2, 1)).reshape(-1, D)
    n_out = w_so.shape[0]
    lanes = norm_gains.shape[1]
    small = jnp.concatenate([norm_gains.reshape(-1), biases.reshape(-1), ffn_bias])
    small = jnp.pad(small[None], ((0, 15), (0, D - small.shape[0])))

    near = [tokens] + grid.others(tokens, "y")
    in_group = deal_order - block * block_rows
    groups = [lax.dynamic_slice_in_dim(in_group, ((here - k) % heads) * rows, rows) for k in range(heads)]
    stream_rows = dot_nn(one_hot(jnp.concatenate(groups), block_rows), jnp.concatenate(near, axis=0)).astype(BF)
    up = [(i, i + heads) for i in range(grid.count - heads)]
    down = [(j, i) for i, j in up]
    before = lax.ppermute(stream_rows, BOTH, up)
    behind = lax.ppermute(stream_rows, BOTH, down)
    ext = jnp.concatenate([before, stream_rows, behind], axis=0)

    urgent = jnp.concatenate([w_qkv, small, w_so, w_cqkv], axis=0)
    urgent_z = along(grid, [(urgent[None], [{}])], "z", True)
    urgent_xy = along(grid, urgent_z, "xy", False)
    held = along(grid, urgent_xy, "c", False)
    wt_qkv, wt_small, wt_so, wt_cqkv = place(grid, held, [w_qkv.shape[0], 16, n_out, w_cqkv.shape[0]])

    late = jnp.concatenate([w_co, w_in, w_out], axis=0)
    late = [late] + grid.others(late, "y")
    late = [late[-k % heads] for k in range(heads)] * 2
    late = lax.dynamic_slice_in_dim(
        jnp.concatenate(late, axis=0), (-here) % heads * late[0].shape[0], heads * late[0].shape[0]
    )
    gathered = lax.all_gather(jnp.concatenate([memory, late], axis=0), "blk", axis=0, tiled=True)
    gathered = gathered.reshape(blocks, -1, D)
    cut = mem_rows * 5 // 8
    smalls = wt_small.reshape(grid.count, 16, D)[:, 0, : 13 * lanes + ffn_bias.shape[0]].astype(F32)
    vec = jnp.transpose(smalls[:, : 13 * lanes].reshape(grid.count, 13, lanes), (1, 0, 2)).reshape(13, D)
    vec = jnp.pad(vec, ((0, 3), (0, 0)))
    hidden_bias = smalls[:, 13 * lanes :].reshape(1, -1)

    place_own = groups[0]
    rank = jnp.sum((place_own[None, :] < place_own[:, None]).astype(jnp.int32), axis=1)
    order = one_hot(rank, rows)
    x = dot_nn(order, tokens).astype(BF)
    cot_hi, cot_lo = hi_lo(cotangent)
    cot = dot_nn(order, cot_hi) + dot_nn(order, cot_lo)
    spot = jnp.sum(jnp.where(rank[None, :] == jnp.arange(rows)[:, None], place_own[None, :], 0), axis=1)
    spot = spot + block_rows
    count = lengths.shape[0]
    tri = jnp.arange(count)[None, :] <= jnp.arange(count)[:, None]
    ends = jnp.sum(jnp.where(tri, lengths[None, :], 0), axis=1)
    starts = ends - lengths
    base = (block - 1) * block_rows
    ext_ends, ext_starts = ends - base, starts - base
    passed = ext_ends[None, :] <= spot[:, None]
    row_begin = jnp.max(jnp.where(passed, ext_ends[None, :], -base), axis=1)
    row_end = jnp.min(jnp.where(passed, jnp.int32(1 << 30), ext_ends[None, :]), axis=1)
    lane = jnp.arange(128)[None, :]
    ranges = jnp.where(lane == 0, row_begin[:, None], row_end[:, None])
    row_ranges = jnp.where(jnp.arange(8)[:, None] == 0, row_begin[None, :], row_end[None, :])
    tq = min(128, rows)
    tk = 256
    lo = jnp.min(row_begin.reshape(-1, tq), axis=1) // tk
    hi = (jnp.max(row_end.reshape(-1, tq), axis=1) + tk - 1) // tk
    lo = jnp.maximum(lo, 0)
    hi = jnp.minimum(hi, 3 * block_rows // tk)

    inside = (ext_starts < 2 * block_rows) & (ext_ends > block_rows)
    number = jnp.arange(count)
    key = jnp.where(inside, mem_index * count + number, blocks * count * 2 + number)
    slot = jnp.sum((key[None, :] < key[:, None]).astype(jnp.int32), axis=1)
    stacked = jnp.stack(groups)
    first = jnp.sum((stacked[None] + block_rows < ext_starts[:, None, None]).astype(jnp.int32), axis=2)
    final = jnp.sum((stacked[None] + block_rows < ext_ends[:, None, None]).astype(jnp.int32), axis=2)
    columns = jnp.concatenate(
        [mem_index[:, None], jnp.stack([first, final], axis=2).reshape(count, -1)], axis=1
    )
    sorted_columns = jnp.sum(
        jnp.where((slot[None, :] == number[:, None])[:, :, None], columns[None], 0), axis=1
    )
    steps = jnp.sum(inside.astype(jnp.int32))
    live = number < steps
    final_mem = jnp.sum(jnp.where(number == steps - 1, sorted_columns[:, 0], 0))
    mem_steps = jnp.where(live, sorted_columns[:, 0], final_mem)
    mem_table = jnp.concatenate([mem_steps, steps[None]])
    memories = jnp.arange(blocks)
    ahead = 0
    for dim, coordinate in (
        ("c", lambda m: m % grid.core),
        ("x", lambda m: m // grid.core % grid.size["x"]),
        ("z", lambda m: m // (grid.core * grid.size["x"])),
    ):
        ahead = ahead * grid.size[dim] + (coordinate(memories) - grid.at[dim]) % grid.size[dim]
    used = jnp.any(inside[:, None] & (mem_index[:, None] == memories[None, :]), axis=0)
    spot_table = jnp.where(used, ahead + 1, -(ahead + 1)).astype(jnp.int32)
    row_table = jnp.where(live[:, None], sorted_columns[:, 1:], 0).reshape(-1)

    bias_q, bias_v = vec[3], vec[4]
    q = ((dot_nt(x, wt_qkv[:D]) + bias_q).astype(BF) * SCALE).astype(BF)
    kv = (dot_nt(ext, wt_qkv[D:]) + jnp.concatenate([jnp.zeros((D,), F32), bias_v])).astype(BF)
    pairs = PAIRS if 3 * block_rows <= 4096 else 1
    att, lse = self_forward(q, kv, ranges, lo, hi, tq, tk, pairs)
    z1, cq = first_rows(x, att, wt_so, wt_cqkv[:D], vec)

    queries = [cq] + grid.others(cq, "y")
    wt_ckv = wt_cqkv[D:]
    bias_kv = jnp.concatenate([jnp.zeros((D,), F32), vec[7]])[None]
    mem_kv = memory_kv(mem_table, gathered, mem_rows, wt_ckv, bias_kv)
    ctq = min(128, rows)
    outs, lses = cross_forward(mem_table, row_table, mem_kv, queries, ctq)
    late = gathered[:, mem_rows:].reshape(grid.count, -1, D)
    late_rows = np.cumsum([0, n_out, w_in.shape[0]] + [n_out] * chunks)
    wt_co, wt_in, *wt_out = (
        late[:, i:j].reshape(-1, D) for i, j in zip(late_rows[:-1], late_rows[1:])
    )
    w2 = jnp.stack(wt_out)
    own_outs = [outs[0]] + [grid.shift(outs[k], y=-k) for k in range(1, heads)]
    own_lses = [lses[0]] + [grid.shift(lses[k], y=-k) for k in range(1, heads)]

    y, dz2, dcatt, stat, g_co, g_in, g_out, rows_1 = middle_rows(
        z1, cot, own_outs, own_lses, wt_co, wt_in, w2, vec, hidden_bias
    )
    upstream = [dcatt] + grid.others(dcatt, "y")
    stats = [stat] + grid.others(stat, "y")
    groups_1 = [g_in, g_co] + [g_out[c] for c in range(chunks)]
    packed_1 = pack(grid, groups_1 + [jnp.tile(rows_1, (grid.count, 1))])
    sum_1 = add(grid.terms(packed_1, 2, "c"))
    upstream, sum_1 = beside(upstream, sum_1)
    outputs = cross_backward(
        mem_table, spot_table, row_table, mem_kv, gathered, wt_ckv, queries, upstream, stats, ctq, grid.core
    )
    outputs, terms_1 = beside(outputs, grid.terms(sum_1, 1, "xy"))
    keep_m, send_m, g_ckv, g_bv, *dcqs = outputs
    own_dcqs = [dcqs[0]] + [grid.shift(dcqs[k], y=-k) for k in range(1, heads)]
    terms_m = [keep_m] if grid.core == 1 else [keep_m, grid.shift(send_m, c=1)]
    terms_1 = grid.terms(add(terms_1), 0, "z")
    dz1, datt, delta, g_so, g_cq, gvec1 = last_rows(z1, dz2, att, own_dcqs, wt_cqkv[:D], wt_so, vec)
    delta = jnp.pad(delta.reshape(PAIRS, 2, rows), ((0, 0), (0, 6), (0, 0)))
    half_pairs = min(pairs, PAIRS // 2)
    backward = lambda datt, half: self_backward(
        q, datt, kv, row_ranges, lse, delta, lo, hi, tq, tk, half_pairs, half
    )
    first_half, (terms_m, terms_1) = beside(backward(datt, 0), (terms_m, terms_1))
    sum_m = add(terms_m).reshape(grid.size["x"], grid.size["z"], mem_rows, D)
    sum_1 = add(terms_1, F32)
    terms_a = grid.ahead(sum_m[:, :, :cut], "x")
    terms_b = grid.ahead(jnp.swapaxes(sum_m[:, :, cut:], 0, 1), "z")
    second_half = backward(after(datt, sum_m), 1)
    dqs, dks, dvs = zip(first_half, second_half)

    outputs = self_grads(dqs, dks, dvs, x, ext, wt_qkv, gvec1, g_bv)
    outputs, (terms_a, terms_b) = beside(outputs, (terms_a, terms_b))
    dxq, back, g_qkv, rows_2 = outputs
    from_next = lax.ppermute(back[:block_rows], BOTH, down)
    from_prior = lax.ppermute(back[2 * block_rows :], BOTH, up)
    shared = (
        back[block_rows : 2 * block_rows].astype(F32) + from_next.astype(F32) + from_prior.astype(F32)
    ).astype(BF)

    def dealt(k):
        picks = lax.broadcasted_iota(jnp.int32, (rows, block_rows), 1) == groups[k][:, None]
        return dot_nn(picks.astype(BF), shared)

    grad_in = dz1 + dxq
    grad_hi, grad_lo = hi_lo(grad_in)
    grad_input = dot_tn(order, grad_hi) + dot_tn(order, grad_lo) + dealt(0)
    for k in range(1, heads):
        grad_input = grad_input + grid.shift(dealt(k).astype(BF), y=-k).astype(F32)
    y_hi, y_lo = hi_lo(y)
    layer_out = dot_tn(order, y_hi) + dot_tn(order, y_lo)
    grad_memory = jnp.concatenate(
        [add(grid.ahead(add(terms_a), "z"), F32), add(grid.ahead(add(terms_b), "x"), F32)], axis=0
    )

    groups_2 = [g_qkv, g_so, jnp.concatenate([g_cq, g_ckv.astype(BF)], axis=0)]
    sum_2 = pack(grid, groups_2 + [jnp.tile(rows_2, (grid.count, 1))])
    sum_2 = add(grid.terms(add(grid.terms(sum_2, 2, "c")), 1, "xy"))
    sum_2 = add(grid.terms(sum_2, 0, "z"), F32)
    s_in, s_co, *s_out = split(grid, sum_1, groups_1)
    s_qkv, s_so, s_cq = split(grid, sum_2, groups_2)
    me = block * heads + here

    def mine(summed, first, count):
        return lax.dynamic_slice(summed, (first, me * lanes), (count, lanes))

    early = sum_1[sum_1.shape[0] - rows_1.shape[0] :]
    final_rows = sum_2[sum_2.shape[0] - 16 :]
    e, f = mine(early, 0, 6), mine(final_rows, 0, 7)
    width = ffn_bias.shape[0]
    s_bias = lax.dynamic_slice(early, (6 + me * width // D, me * width % D), (1, width))[0]
    return (
        layer_out,
        grad_input,
        grad_memory,
        s_qkv.T,
        s_so.T,
        s_cq.T,
        s_co.T,
        s_in.T,
        jnp.concatenate([s.T for s in s_out], axis=0),
        jnp.stack([f[0], e[3], e[0]]),
        jnp.stack([f[5], f[6], f[2], f[3], f[4], e[5], e[2], f[1], e[4], e[1]]),
        s_bias,
    )


def solution(mesh):
    rows = P(BOTH, None)
    cols = P(None, BOTH)
    return jax.shard_map(
        body,
        mesh=mesh,
        in_specs=(rows, rows, rows, P("blk"), P(), P()) + (cols,) * 8 + (P(BOTH),),
        out_specs=(rows,) * 3 + (cols,) * 8 + (P(BOTH),),
        check_vma=False,
    )
```

```python
import functools
import math

import jax
import jax.numpy as jnp
import numpy as np
from jax import lax
from jax.experimental import pallas as pl
from jax.experimental.pallas import tpu as pltpu
from jax.sharding import PartitionSpec as P

D = 512
HEADS = 8
MEM = 1024
HD = D // HEADS
PAIRS = HEADS // 2
SCALE = 1.0 / math.sqrt(HD)
EPSILON = 1e-05
GELU_SCALE = 0.7978845608028654
FILL = -1e30
FLOOR = -1e20
BOTH = ("blk", "head")
BF = jnp.bfloat16
F32 = jnp.float32
VMEM_BYTES = 60 * 1024 * 1024


def dot_nn(a, b):
    return lax.dot_general(a, b, (((1,), (0,)), ((), ())), preferred_element_type=F32)


def dot_nt(a, b):
    return lax.dot_general(a, b, (((1,), (1,)), ((), ())), preferred_element_type=F32)


def dot_tn(a, b):
    return lax.dot_general(a, b, (((0,), (0,)), ((), ())), preferred_element_type=F32)


def hi_lo(x):
    hi = x.astype(BF)
    return hi, (x - hi.astype(F32)).astype(BF)


class Grid:
    def __init__(self):
        self.blk = lax.axis_size("blk")
        self.head = lax.axis_size("head")
        self.core = 2 if self.blk % 2 == 0 else 1
        rest = self.blk // self.core
        major = 4 if rest % 4 == 0 else rest
        self.size = {"z": major, "x": rest // major, "c": self.core, "y": self.head}
        self.stride = {
            "y": 1,
            "c": self.head,
            "x": self.head * self.core,
            "z": self.head * self.core * (rest // major),
        }
        self.count = self.blk * self.head
        b = lax.axis_index("blk")
        self.at = {
            "y": lax.axis_index("head"),
            "c": b % self.core,
            "x": (b // self.core) % self.size["x"],
            "z": b // (self.core * self.size["x"]),
        }

    def shift(self, array, **steps):
        route = []
        for i in range(self.count):
            to = i
            for dim, step in steps.items():
                size, stride = self.size[dim], self.stride[dim]
                at = (i // stride) % size
                to += ((at + step) % size - at) * stride
            route.append((i, to))
        return lax.ppermute(array, BOTH, route)

    def offsets(self, dims):
        out = [{}]
        for dim in dims:
            out = [dict(o, **{dim: k}) for o in out for k in range(self.size[dim])]
        return out[1:]

    def others(self, array, dims):
        return [self.shift(array, **o) for o in self.offsets(dims)]

    def ahead(self, buffer, dims):
        return [buffer[0]] + [self.shift(buffer[k], **o) for k, o in enumerate(self.offsets(dims), 1)]

    def spots(self, order):
        device = jnp.arange(self.count)
        spot = 0
        for dim in order:
            at = device // self.stride[dim] % self.size[dim]
            spot = spot * self.size[dim] + (at - self.at[dim]) % self.size[dim]
        return spot.astype(jnp.int32)


def add(terms, dtype=BF):
    return sum(t.astype(F32) for t in terms).astype(dtype)


def beside(outputs, arrays):
    return lax.optimization_barrier((outputs, arrays))


def after(values, *first):
    return lax.optimization_barrier((values, *first))[0]


def cost(us):
    return pl.CostEstimate(flops=int(us * 1e3), transcendentals=0, bytes_accessed=0)


def along(grid, held, dims, join):
    out = []
    for array, places in held:
        arrays = [array] + grid.others(array, dims)
        tagged = [[dict(p, **o) for p in places] for o in [{}] + grid.offsets(dims)]
        if join:
            out.append((jnp.concatenate(arrays, axis=0), sum(tagged, [])))
        else:
            out += list(zip(arrays, tagged))
    return out


def place_kernel(z_size, rows, index_ref, *refs):
    arrays, outs = refs[: len(refs) - len(rows)], refs[len(refs) - len(rows) :]
    each = arrays[0].shape[0] // z_size
    i = pl.program_id(0)
    for a, array in enumerate(arrays):

        @pl.when(i // each == a)
        def _(array=array):
            for z in range(z_size):
                source = (i % each) * z_size + (index_ref[0] - z + z_size) % z_size
                start = 0
                for out, n in zip(outs, rows):
                    out[z, 0] = array[source, start : start + n, :]
                    start += n


def place(grid, held, rows):
    arrays = [a for a, _ in held]
    z_size = grid.size["z"]
    other = grid.count // z_size
    slot = []
    for _, places in held:
        for p in places[::z_size]:
            at = 0
            for dim in "xcy":
                at = at * grid.size[dim] + (grid.at[dim] - p.get(dim, 0)) % grid.size[dim]
            slot.append(at)
    index = jnp.stack([grid.at["z"]] + slot).astype(jnp.int32)
    outs = pl.pallas_call(
        functools.partial(place_kernel, z_size, rows),
        grid_spec=pltpu.PrefetchScalarGridSpec(
            num_scalar_prefetch=1,
            grid=(other,),
            in_specs=[pl.BlockSpec(a.shape, lambda i, _: (0, 0, 0)) for a in arrays],
            out_specs=[
                pl.BlockSpec((z_size, 1, n, D), lambda i, index: (0, index[i + 1], 0, 0)) for n in rows
            ],
        ),
        out_shape=[jax.ShapeDtypeStruct((z_size, other, n, D), BF) for n in rows],
        compiler_params=pltpu.CompilerParams(vmem_limit_bytes=VMEM_BYTES),
        cost_estimate=cost(5),
        name="place_weights",
    )(index, *arrays)
    return [out.reshape(grid.count * n, D) for out, n in zip(outs, rows)]


def lane_mask(rows):
    return lax.broadcasted_iota(jnp.int32, (rows, 2 * HD), 1) < HD


def two(low, x):
    zero = jnp.zeros_like(x)
    return jnp.concatenate([jnp.where(low, x, zero), jnp.where(low, zero, x)], axis=0)


def pick(low, x):
    half = x.shape[0] // 2
    return jnp.where(low, x[:half], x[half:])


def with_ones(v):
    return jnp.concatenate([v, jnp.ones_like(v)], axis=1)


def pair_cols(g):
    return slice(g * 2 * HD, (g + 1) * 2 * HD)


def self_forward_kernel(
    pairs, tq, tk, lo_ref, hi_ref, q_ref, k_ref, v_ref, range_ref, att_ref, lse_ref, score_ref, top_ref, acc_ref
):
    width = 2 * HD
    low = lane_mask(tq)
    for i in range(q_ref.shape[0] // tq):
        rows = pl.ds(i * tq, tq)
        begin = jnp.concatenate([range_ref[rows, 0:1]] * 2, axis=0)
        end = jnp.concatenate([range_ref[rows, 1:2]] * 2, axis=0)
        first = lo_ref[i]
        top_ref[...] = jnp.full_like(top_ref, FILL)
        acc_ref[...] = jnp.zeros_like(acc_ref)

        def scores(t, carry, i=i):
            keys = pl.ds(pl.multiple_of(t * tk, tk), tk)
            spot = pl.ds(pl.multiple_of((t - first) * tk, tk), tk)
            place = lax.broadcasted_iota(jnp.int32, (2 * tq, tk), 1) + t * tk
            allowed = (place >= begin) & (place < end)
            for g in range(pairs):
                s = dot_nt(two(low, q_ref[pl.ds(i * tq, tq), pair_cols(g)]), k_ref[keys, pair_cols(g)])
                s = jnp.where(allowed, s, FILL)
                score_ref[g, :, spot] = s
                peak = top_ref[g]
                for c in range(tk // width):
                    peak = jnp.maximum(peak, s[:, c * width : (c + 1) * width])
                top_ref[g] = peak
            return carry

        lax.fori_loop(first, hi_ref[i], scores, 0)
        for g in range(pairs):
            peak = jnp.max(top_ref[g], axis=1, keepdims=True)
            top_ref[g] = jnp.broadcast_to(peak, (2 * tq, width))

        def weigh(t, carry):
            keys = pl.ds(pl.multiple_of(t * tk, tk), tk)
            spot = pl.ds(pl.multiple_of((t - first) * tk, tk), tk)
            for g in range(pairs):
                p = jnp.exp(score_ref[g, :, spot] - top_ref[g, :, 0:1]).astype(BF)
                acc_ref[g] += dot_nn(p, with_ones(v_ref[keys, pair_cols(g)]))
            return carry

        lax.fori_loop(first, hi_ref[i], weigh, 0)
        for g in range(pairs):
            mass = acc_ref[g, :, width:]
            att_ref[rows, pair_cols(g)] = pick(low, acc_ref[g, :, :width] / mass).astype(BF)
            flat = (top_ref[g] + jnp.log(mass)).T
            lse_ref[g, 0:1, rows] = flat[0:1, :tq]
            lse_ref[g, 1:2, rows] = flat[0:1, tq:]


def self_forward(q, kv, ranges, lo, hi, tq, tk, pairs):
    rows, keys = q.shape[0], kv.shape[0]
    width = pairs * 2 * HD
    groups = PAIRS // pairs
    return pl.pallas_call(
        functools.partial(self_forward_kernel, pairs, tq, tk),
        grid_spec=pltpu.PrefetchScalarGridSpec(
            num_scalar_prefetch=2,
            grid=(groups,),
            in_specs=[
                pl.BlockSpec((rows, width), lambda g, *_: (0, g)),
                pl.BlockSpec((keys, width), lambda g, *_: (0, g)),
                pl.BlockSpec((keys, width), lambda g, *_: (0, groups + g)),
                pl.BlockSpec((rows, 128), lambda g, *_: (0, 0)),
            ],
            out_specs=[
                pl.BlockSpec((rows, width), lambda g, *_: (0, g)),
                pl.BlockSpec((pairs, 8, rows), lambda g, *_: (g, 0, 0)),
            ],
            scratch_shapes=[
                pltpu.VMEM((pairs, 2 * tq, keys), F32),
                pltpu.VMEM((pairs, 2 * tq, 2 * HD), F32),
                pltpu.VMEM((pairs, 2 * tq, 4 * HD), F32),
            ],
        ),
        out_shape=[
            jax.ShapeDtypeStruct((rows, D), BF),
            jax.ShapeDtypeStruct((PAIRS, 8, rows), F32),
        ],
        compiler_params=pltpu.CompilerParams(vmem_limit_bytes=VMEM_BYTES),
        cost_estimate=cost(20),
        name="self_forward",
    )(lo, hi, q, kv, kv, ranges)


def self_backward_kernel(
    pairs, tq, tk, lo_ref, hi_ref, q_ref, do_ref, k_ref, v_ref, row_ref, lse_ref, delta_ref, dq_ref, dk_ref, dv_ref,
    acc_q, acc_k, acc_v,
):
    low = lane_mask(tq)
    acc_k[...] = jnp.zeros_like(acc_k)
    acc_v[...] = jnp.zeros_like(acc_v)
    for i in range(q_ref.shape[0] // tq):
        rows = pl.ds(i * tq, tq)
        begin = jnp.concatenate([row_ref[0:1, rows]] * 2, axis=1)
        end = jnp.concatenate([row_ref[1:2, rows]] * 2, axis=1)
        acc_q[...] = jnp.zeros_like(acc_q)

        def step(t, carry, i=i):
            rows = pl.ds(i * tq, tq)
            keys = pl.ds(pl.multiple_of(t * tk, tk), tk)
            place = lax.broadcasted_iota(jnp.int32, (tk, 2 * tq), 0) + t * tk
            allowed = (place >= begin) & (place < end)
            for g in range(pairs):
                cols = pair_cols(g)
                k, v = k_ref[keys, cols], v_ref[keys, cols]
                q2, do2 = two(low, q_ref[rows, cols]), two(low, do_ref[rows, cols])
                lse = jnp.concatenate([lse_ref[g, 0:1, rows], lse_ref[g, 1:2, rows]], axis=1)
                delta = jnp.concatenate([delta_ref[g, 0:1, rows], delta_ref[g, 1:2, rows]], axis=1)
                p = jnp.exp(jnp.where(allowed, dot_nt(k, q2) - lse, FILL))
                ds = (p * (dot_nt(v, do2) - delta)).astype(BF)
                acc_v[keys, cols] += dot_nn(p.astype(BF), do2)
                acc_k[keys, cols] += dot_nn(ds, q2)
                acc_q[g] += dot_tn(ds, k)
            return carry

        lax.fori_loop(lo_ref[i], hi_ref[i], step, 0)
        for g in range(pairs):
            dq_ref[rows, pair_cols(g)] = (pick(low, acc_q[g]) * SCALE).astype(BF)
    dk_ref[...] = acc_k[...].astype(BF)
    dv_ref[...] = acc_v[...].astype(BF)


def self_backward(q, do, kv, row_range, lse, delta, lo, hi, tq, tk, pairs):
    rows, keys = q.shape[0], kv.shape[0]
    width = pairs * 2 * HD
    groups = PAIRS // pairs
    return pl.pallas_call(
        functools.partial(self_backward_kernel, pairs, tq, tk),
        grid_spec=pltpu.PrefetchScalarGridSpec(
            num_scalar_prefetch=2,
            grid=(groups,),
            in_specs=[
                pl.BlockSpec((rows, width), lambda g, *_: (0, g)),
                pl.BlockSpec((rows, width), lambda g, *_: (0, g)),
                pl.BlockSpec((keys, width), lambda g, *_: (0, g)),
                pl.BlockSpec((keys, width), lambda g, *_: (0, groups + g)),
                pl.BlockSpec((8, rows), lambda g, *_: (0, 0)),
                pl.BlockSpec((pairs, 8, rows), lambda g, *_: (g, 0, 0)),
                pl.BlockSpec((pairs, 8, rows), lambda g, *_: (g, 0, 0)),
            ],
            out_specs=[
                pl.BlockSpec((rows, width), lambda g, *_: (0, g)),
                pl.BlockSpec((keys, width), lambda g, *_: (0, g)),
                pl.BlockSpec((keys, width), lambda g, *_: (0, g)),
            ],
            scratch_shapes=[
                pltpu.VMEM((pairs, 2 * tq, 2 * HD), F32),
                pltpu.VMEM((keys, width), F32),
                pltpu.VMEM((keys, width), F32),
            ],
        ),
        out_shape=[
            jax.ShapeDtypeStruct((rows, D), BF),
            jax.ShapeDtypeStruct((keys, D), BF),
            jax.ShapeDtypeStruct((keys, D), BF),
        ],
        compiler_params=pltpu.CompilerParams(vmem_limit_bytes=VMEM_BYTES),
        cost_estimate=cost(40),
        name="self_backward",
    )(lo, hi, q, do, kv, kv, row_range, lse, delta)


def memory_kv_kernel(mem_ref, m_ref, w_ref, b_ref, kv_ref):
    j = pl.program_id(0)

    @pl.when((j == 0) | (mem_ref[j] != mem_ref[jnp.maximum(j - 1, 0)]))
    def _():
        kv_ref[0] = (dot_nt(m_ref[0], w_ref[...]) + b_ref[...]).astype(BF)


def memory_kv(mem, gathered, n, weights, bias):
    blocks = gathered.shape[0]
    by_memory = lambda j, mem: (mem[j], 0, 0)
    return pl.pallas_call(
        memory_kv_kernel,
        grid_spec=pltpu.PrefetchScalarGridSpec(
            num_scalar_prefetch=1,
            grid=(mem.shape[0] - 1,),
            in_specs=[
                pl.BlockSpec((1, n, D), by_memory),
                pl.BlockSpec((2 * D, D), lambda j, *_: (0, 0)),
                pl.BlockSpec((1, 2 * D), lambda j, *_: (0, 0)),
            ],
            out_specs=pl.BlockSpec((1, n, 2 * D), by_memory),
        ),
        out_shape=jax.ShapeDtypeStruct((blocks, n, 2 * D), BF),
        compiler_params=pltpu.CompilerParams(vmem_limit_bytes=VMEM_BYTES),
        cost_estimate=cost(6),
        name="memory_kv",
    )(mem, gathered, weights, bias)


def cross_forward_kernel(parts, tq, mem_ref, table_ref, kv_ref, *refs):
    qs, outs, lses = refs[:parts], refs[parts : 2 * parts], refs[2 * parts : 3 * parts]
    width = 2 * HD
    j = pl.program_id(0)
    low = lane_mask(tq)
    for part in range(parts):
        first_row = table_ref[j * 2 * parts + 2 * part]
        last_row = table_ref[j * 2 * parts + 2 * part + 1]

        def step(t, carry, part=part, first_row=first_row, last_row=last_row):
            offset = pl.multiple_of(t * tq, tq)
            rows = pl.ds(offset, tq)
            at = lax.broadcasted_iota(jnp.int32, (tq, width), 0) + offset
            mine = (at >= first_row) & (at < last_row)
            at_row = lax.broadcasted_iota(jnp.int32, (1, tq), 1) + offset
            mine_row = (at_row >= first_row) & (at_row < last_row)
            for g in range(PAIRS):
                cols = pair_cols(g)
                s = dot_nt(two(low, qs[part][rows, cols]), kv_ref[0, :, cols])
                peak = jnp.max(s, axis=1, keepdims=True)
                p = jnp.exp(s - peak).astype(BF)
                acc = dot_nn(p, with_ones(kv_ref[0, :, pair_cols(PAIRS + g)]))
                mass = acc[:, width:]
                new = pick(low, acc[:, :width] / mass).astype(BF)
                outs[part][rows, cols] = jnp.where(mine, new, outs[part][rows, cols])
                flat = (peak + jnp.log(mass)).T
                for i in range(2):
                    head = slice(2 * g + i, 2 * g + i + 1)
                    lses[part][head, rows] = jnp.where(
                        mine_row, flat[0:1, i * tq : (i + 1) * tq], lses[part][head, rows]
                    )
            return carry

        lax.fori_loop(first_row // tq, (last_row + tq - 1) // tq, step, 0)


def cross_forward(mem, table, kv, queries, tq):
    parts, rows, n = len(queries), queries[0].shape[0], kv.shape[1]
    whole = pl.BlockSpec((rows, D), lambda j, *_: (0, 0))
    flat = pl.BlockSpec((HEADS, rows), lambda j, *_: (0, 0))
    out = pl.pallas_call(
        functools.partial(cross_forward_kernel, parts, tq),
        grid_spec=pltpu.PrefetchScalarGridSpec(
            num_scalar_prefetch=2,
            grid=(mem.shape[0] - 1,),
            in_specs=[pl.BlockSpec((1, n, 2 * D), lambda j, mem, _: (mem[j], 0, 0))] + [whole] * parts,
            out_specs=[whole] * parts + [flat] * parts,
        ),
        out_shape=[jax.ShapeDtypeStruct((rows, D), BF)] * parts
        + [jax.ShapeDtypeStruct((HEADS, rows), F32)] * parts,
        compiler_params=pltpu.CompilerParams(vmem_limit_bytes=VMEM_BYTES),
        cost_estimate=cost(16),
        name="cross_forward",
    )(mem, table, kv, *queries)
    return out[:parts], out[parts:]


def cross_backward_kernel(parts, tq, blocks, mem_ref, spot_ref, table_ref, kv_ref, m_ref, w_ref, *refs):
    qs, dos, stats = refs[:parts], refs[parts : 2 * parts], refs[2 * parts : 3 * parts]
    keep_ref, send_ref, gw_ref, gb_ref = refs[3 * parts : 3 * parts + 4]
    dqs = refs[3 * parts + 4 : 4 * parts + 4]
    acc_k, acc_v, acc_q, stage, zero, stage_sem, zero_sem = refs[4 * parts + 4 :]
    j = pl.program_id(0)
    last = mem_ref.shape[0] - 2
    steps = mem_ref[last + 1]
    now = mem_ref[j]
    previous = mem_ref[jnp.maximum(j - 1, 0)]
    following = mem_ref[jnp.minimum(j + 1, last)]
    low = lane_mask(tq)
    half = keep_ref.shape[0]

    def to_target(source, spot, sem, wanted, act):
        for target, mine in ((keep_ref, spot < half), (send_ref, spot >= half)):
            copy = pltpu.make_async_copy(source, target.at[spot % half], sem)
            pl.when(wanted & mine)(functools.partial(act, copy))

    start, wait = (lambda copy: copy.start()), (lambda copy: copy.wait())

    def zeros(act):
        for m in range(blocks):
            spot = spot_ref[m]
            to_target(zero, jnp.abs(spot) - 1, zero_sem.at[m], spot < 0, act)

    @pl.when(j == 0)
    def _():
        acc_q[...] = jnp.zeros_like(acc_q)
        gw_ref[...] = jnp.zeros_like(gw_ref)
        gb_ref[...] = jnp.zeros_like(gb_ref)
        zero[...] = jnp.zeros_like(zero)
        zeros(start)

    @pl.when((j == 0) | (now != previous))
    def _():
        acc_k[...] = jnp.zeros_like(acc_k)
        acc_v[...] = jnp.zeros_like(acc_v)

    for part in range(parts):
        first_row = table_ref[j * 2 * parts + 2 * part]
        last_row = table_ref[j * 2 * parts + 2 * part + 1]

        def step(t, carry, part=part, first_row=first_row, last_row=last_row):
            offset = pl.multiple_of(t * tq, tq)
            rows = pl.ds(offset, tq)
            at_row = lax.broadcasted_iota(jnp.int32, (1, tq), 1) + offset
            mine = (at_row >= first_row) & (at_row < last_row)
            for g in range(PAIRS):
                cols = pair_cols(g)
                k, v = kv_ref[0, :, cols], kv_ref[0, :, pair_cols(PAIRS + g)]
                q2, do2 = two(low, qs[part][rows, cols]), two(low, dos[part][rows, cols])

                def stat(base, part=part, g=g):
                    return [stats[part][base + 2 * g + i : base + 2 * g + i + 1, rows] for i in range(2)]

                lse = jnp.concatenate([jnp.where(mine, x, -FILL) for x in stat(0)], axis=1)
                delta = jnp.concatenate(stat(HEADS), axis=1)
                p = jnp.exp(dot_nt(k, q2) - lse)
                ds = (p * (dot_nt(v, do2) - delta)).astype(BF)
                acc_v[:, cols] += dot_nn(p.astype(BF), do2)
                acc_k[:, cols] += dot_nn(ds, q2)
                acc_q[part, rows, cols] += pick(low, dot_tn(ds, k))
            return carry

        lax.fori_loop(first_row // tq, (last_row + tq - 1) // tq, step, 0)

    @pl.when((j == steps - 1) | ((j < steps) & (now != following)))
    def _():
        dk, dv = acc_k[...].astype(BF), acc_v[...].astype(BF)
        spot = spot_ref[now] - 1
        stage[...] = (dot_nn(dk, w_ref[0:D, :]) + dot_nn(dv, w_ref[D : 2 * D, :])).astype(BF)
        to_target(stage, spot, stage_sem, spot >= 0, start)
        gw_ref[0:D, :] += dot_tn(dk, m_ref[0])
        gw_ref[D : 2 * D, :] += dot_tn(dv, m_ref[0])
        gb_ref[0:1, :] += jnp.sum(dv.astype(F32), axis=0, keepdims=True)
        to_target(stage, spot, stage_sem, spot >= 0, wait)

    @pl.when(j == steps - 1)
    def _():
        for part in range(parts):
            dqs[part][...] = (acc_q[part] * SCALE).astype(BF)
        zeros(wait)


def cross_backward(mem, spot, table, kv, rows_of_memory, weights, queries, upstream, stats, tq, cores):
    parts, rows, n = len(queries), queries[0].shape[0], kv.shape[1]
    blocks = kv.shape[0]
    whole = pl.BlockSpec((rows, D), lambda j, *_: (0, 0))
    flat = pl.BlockSpec((2 * HEADS, rows), lambda j, *_: (0, 0))
    by_memory = lambda j, mem, *_: (mem[j], 0, 0)
    anywhere = pl.BlockSpec(memory_space=pl.ANY)
    return pl.pallas_call(
        functools.partial(cross_backward_kernel, parts, tq, blocks),
        grid_spec=pltpu.PrefetchScalarGridSpec(
            num_scalar_prefetch=3,
            grid=(mem.shape[0] - 1,),
            in_specs=[
                pl.BlockSpec((1, n, 2 * D), by_memory),
                pl.BlockSpec((1, n, D), by_memory),
                pl.BlockSpec((2 * D, D), lambda j, *_: (0, 0)),
            ]
            + [whole] * (2 * parts)
            + [flat] * parts,
            out_specs=[
                anywhere,
                anywhere,
                pl.BlockSpec((2 * D, D), lambda j, *_: (0, 0)),
                pl.BlockSpec((8, D), lambda j, *_: (0, 0)),
            ]
            + [whole] * parts,
            scratch_shapes=[
                pltpu.VMEM((n, D), F32),
                pltpu.VMEM((n, D), F32),
                pltpu.VMEM((parts, rows, D), F32),
                pltpu.VMEM((n, D), BF),
                pltpu.VMEM((n, D), BF),
                pltpu.SemaphoreType.DMA,
                pltpu.SemaphoreType.DMA((blocks,)),
            ],
        ),
        out_shape=[jax.ShapeDtypeStruct((blocks // cores, n, D), BF)] * 2
        + [
            jax.ShapeDtypeStruct((2 * D, D), F32),
            jax.ShapeDtypeStruct((8, D), F32),
        ]
        + [jax.ShapeDtypeStruct((rows, D), BF)] * parts,
        compiler_params=pltpu.CompilerParams(vmem_limit_bytes=VMEM_BYTES),
        cost_estimate=cost(32),
        name="cross_backward",
    )(mem, spot, table, kv, rows_of_memory, weights, *queries, *upstream, *stats)


def norm(z):
    centre = z - jnp.mean(z, axis=1, keepdims=True)
    inverse = lax.rsqrt(jnp.mean(centre * centre, axis=1, keepdims=True) + EPSILON)
    return centre * inverse, inverse


def norm_back(upstream, normed, inverse, gain):
    scaled = upstream * gain
    return inverse * (
        scaled
        - jnp.mean(scaled, axis=1, keepdims=True)
        - normed * jnp.mean(scaled * normed, axis=1, keepdims=True)
    )


def total(x):
    return jnp.sum(x, axis=0, keepdims=True)


def head_rows():
    lane = lax.broadcasted_iota(jnp.int32, (HEADS, D), 1) // HD
    return (lane == lax.broadcasted_iota(jnp.int32, (HEADS, D), 0)).astype(F32).astype(BF)


def per_head(product):
    hi, lo = hi_lo(product)
    heads = head_rows()
    return dot_nt(heads, hi) + dot_nt(heads, lo)


def spread(rows):
    hi, lo = hi_lo(rows)
    heads = head_rows()
    return dot_tn(hi, heads) + dot_tn(lo, heads)


def deal(packed_ref, spot_ref, start, values):
    count = packed_ref.shape[0]
    for value in values:
        n = value.shape[0] // count
        for i in range(count):
            packed_ref[spot_ref[i], start : start + n, :] = value[i * n : (i + 1) * n]
        start += n
    return start


def to_all(packed_ref, start, rows):
    for i in range(packed_ref.shape[0]):
        packed_ref[i, start : start + rows.shape[0], :] = rows


def first_kernel(x_ref, att_ref, wo_ref, wq_ref, vec_ref, z_ref, cq_ref):
    z = x_ref[...].astype(F32) + dot_nt(att_ref[...], wo_ref[...]) + vec_ref[5:6, :]
    z_ref[...] = z
    n, _ = norm(z)
    low = (n * vec_ref[0:1, :] + vec_ref[10:11, :]).astype(BF)
    cq_ref[...] = ((dot_nt(low, wq_ref[...]) + vec_ref[6:7, :]).astype(BF) * SCALE).astype(BF)


def first_rows(x, att, wo, wq, vec):
    rows = x.shape[0]
    return pl.pallas_call(
        first_kernel,
        out_shape=[jax.ShapeDtypeStruct((rows, D), F32), jax.ShapeDtypeStruct((rows, D), BF)],
        compiler_params=pltpu.CompilerParams(vmem_limit_bytes=VMEM_BYTES),
        cost_estimate=cost(4),
        name="first_rows",
    )(x, att, wo, wq, vec)


def middle_kernel(parts, chunks, spot_ref, *refs):
    z1_ref, cot_ref = refs[:2]
    outs = refs[2 : 2 + parts]
    lses = refs[2 + parts : 2 + 2 * parts]
    wco_ref, w1_ref, w2_ref, vec_ref, fb_ref = refs[2 + 2 * parts : 7 + 2 * parts]
    y_ref, dz2_ref, dcatt_ref, stat_ref, packed_ref, hid_ref, slope_ref, gw1_ref = refs[7 + 2 * parts :]
    vec = lambda i: vec_ref[i : i + 1, :]
    peak = lses[0][...]
    for part in range(1, parts):
        peak = jnp.maximum(peak, lses[part][...])
    mass = 0.0
    for part in range(parts):
        mass = mass + jnp.exp(lses[part][...] - peak)
    lse = peak + jnp.log(mass)
    catt32 = 0.0
    for part in range(parts):
        catt32 = catt32 + spread(jnp.exp(lses[part][...] - lse)) * outs[part][...].astype(F32)
    catt = catt32.astype(BF)
    n1, _ = norm(z1_ref[...])
    h1 = n1 * vec(0) + vec(10)
    z2 = h1 + dot_nt(catt, wco_ref[...]) + vec(8)
    n2, r2 = norm(z2)
    h2 = n2 * vec(1) + vec(11)
    h2_low = h2.astype(BF)
    z3 = h2 + vec(9)
    for c in range(chunks):
        cols = slice(c * D, (c + 1) * D)
        u = dot_nt(h2_low, w1_ref[cols, :]) + fb_ref[:, cols]
        square = u * u
        t = jnp.tanh(GELU_SCALE * (u + 0.044715 * u * square))
        hid = (0.5 * u * (1.0 + t)).astype(BF)
        hid_ref[:, cols] = hid
        slope_ref[:, cols] = 0.5 * (1.0 + t) + 0.5 * u * (1.0 - t * t) * (
            GELU_SCALE * (1.0 + 3.0 * 0.044715 * square)
        )
        z3 = z3 + dot_nt(hid, w2_ref[c])
    n3, r3 = norm(z3)
    y_ref[...] = n3 * vec(2) + vec(12)
    cot = cot_ref[...]
    dz3 = norm_back(cot, n3, r3, vec(2))
    df = dz3.astype(BF)
    sums = [total(cot * n3), total(cot), total(df.astype(F32))]
    hidden_sums, g_out = [], []
    e2 = dz3
    for c in range(chunks):
        cols = slice(c * D, (c + 1) * D)
        hid = hid_ref[:, cols]
        g_out.append(dot_tn(df, hid).astype(BF))
        du = (dot_nn(df, w2_ref[c]) * slope_ref[:, cols]).astype(BF)
        gw1_ref[cols, :] = dot_tn(du, h2_low).astype(BF)
        hidden_sums.append(total(du.astype(F32)))
        e2 = e2 + dot_nn(du, w1_ref[cols, :])
    dz2 = norm_back(e2, n2, r2, vec(1))
    dz2_ref[...] = dz2
    dca = dz2.astype(BF)
    sums += [total(e2 * n2), total(e2), total(dca.astype(F32))] + hidden_sums
    sums += [jnp.zeros_like(sums[0])] * (-len(sums) % 16)
    start = deal(packed_ref, spot_ref, 0, [gw1_ref[...], dot_tn(dca, catt).astype(BF)] + g_out)
    to_all(packed_ref, start, jnp.concatenate(sums, axis=0).astype(BF))
    dcatt = dot_nn(dca, wco_ref[...]).astype(BF)
    dcatt_ref[...] = dcatt
    stat_ref[0:HEADS, :] = lse
    stat_ref[HEADS : 2 * HEADS, :] = per_head(dcatt.astype(F32) * catt32)


def middle_rows(spots, z1, cot, outs, lses, wco, w1, w2, vec, fb):
    rows, parts, chunks = z1.shape[0], len(outs), w2.shape[0]
    hidden = chunks * D
    count = spots.shape[0]
    packed = (hidden + (1 + chunks) * D) // count + 6 + chunks + -(6 + chunks) % 16
    operands = [z1, cot, *outs, *lses, wco, w1, w2, vec, fb]
    out_shape = [
        jax.ShapeDtypeStruct((rows, D), F32),
        jax.ShapeDtypeStruct((rows, D), F32),
        jax.ShapeDtypeStruct((rows, D), BF),
        jax.ShapeDtypeStruct((2 * HEADS, rows), F32),
        jax.ShapeDtypeStruct((count, packed, D), BF),
    ]
    whole = pl.BlockSpec(memory_space=pltpu.VMEM)
    return pl.pallas_call(
        functools.partial(middle_kernel, parts, chunks),
        in_specs=[pl.BlockSpec(memory_space=pltpu.SMEM)] + [whole] * len(operands),
        out_specs=[whole] * len(out_shape),
        out_shape=out_shape,
        scratch_shapes=[
            pltpu.VMEM((rows, hidden), BF),
            pltpu.VMEM((rows, hidden), F32),
            pltpu.VMEM((hidden, D), BF),
        ],
        compiler_params=pltpu.CompilerParams(vmem_limit_bytes=VMEM_BYTES),
        cost_estimate=cost(18),
        name="middle_rows",
    )(spots, *operands)


def last_kernel(parts, *refs):
    z1_ref, dz2_ref, att_ref = refs[:3]
    dcqs = refs[3 : 3 + parts]
    wq_ref, wo_ref, vec_ref = refs[3 + parts : 6 + parts]
    dz1_ref, datt_ref, delta_ref, gwo_ref, gwq_ref, gvec_ref = refs[6 + parts :]
    dcq = 0.0
    for part in dcqs:
        dcq = dcq + part[...].astype(F32)
    dcq = dcq.astype(BF)
    n1, r1 = norm(z1_ref[...])
    low = (n1 * vec_ref[0:1, :] + vec_ref[10:11, :]).astype(BF)
    e1 = dz2_ref[...] + dot_nn(dcq, wq_ref[...])
    dz1 = norm_back(e1, n1, r1, vec_ref[0:1, :])
    dz1_ref[...] = dz1
    da = dz1.astype(BF)
    datt = dot_nn(da, wo_ref[...]).astype(BF)
    datt_ref[...] = datt
    delta_ref[...] = per_head(datt.astype(F32) * att_ref[...].astype(F32))
    gwo_ref[...] = dot_tn(da, att_ref[...]).astype(BF)
    gwq_ref[...] = dot_tn(dcq, low).astype(BF)
    gvec_ref[...] = jnp.zeros_like(gvec_ref)
    gvec_ref[0:1, :] = total(e1 * n1)
    gvec_ref[1:2, :] = total(e1)
    gvec_ref[2:3, :] = total(da.astype(F32))
    gvec_ref[3:4, :] = total(dcq.astype(F32))


def last_rows(z1, dz2, att, dcqs, wq, wo, vec):
    rows = z1.shape[0]
    return pl.pallas_call(
        functools.partial(last_kernel, len(dcqs)),
        out_shape=[
            jax.ShapeDtypeStruct((rows, D), F32),
            jax.ShapeDtypeStruct((rows, D), BF),
            jax.ShapeDtypeStruct((HEADS, rows), F32),
            jax.ShapeDtypeStruct((D, D), BF),
            jax.ShapeDtypeStruct((D, D), BF),
            jax.ShapeDtypeStruct((8, D), F32),
        ],
        compiler_params=pltpu.CompilerParams(vmem_limit_bytes=VMEM_BYTES),
        cost_estimate=cost(6),
        name="last_rows",
    )(z1, dz2, att, *dcqs, wq, wo, vec)


def token_grads_kernel(dq_ref, dk_ref, dv_ref, w_ref, dx_ref, back_ref):
    @pl.when(pl.program_id(0) == 0)
    def _():
        dx_ref[...] = dot_nn(dq_ref[...], w_ref[0:D, :])

    back_ref[...] = (
        dot_nn(dk_ref[...], w_ref[D : 2 * D, :]) + dot_nn(dv_ref[...], w_ref[2 * D : 3 * D, :])
    ).astype(BF)


def token_grads(dq, dk, dv, w):
    rows, keys = dq.shape[0], dk.shape[0]
    tile = 512
    fixed = lambda shape: pl.BlockSpec(shape, lambda j: (0, 0))
    moving = pl.BlockSpec((tile, D), lambda j: (j, 0))
    return pl.pallas_call(
        token_grads_kernel,
        grid=(keys // tile,),
        in_specs=[fixed((rows, D)), moving, moving, fixed((3 * D, D))],
        out_specs=[fixed((rows, D)), moving],
        out_shape=[jax.ShapeDtypeStruct((rows, D), F32), jax.ShapeDtypeStruct((keys, D), BF)],
        compiler_params=pltpu.CompilerParams(vmem_limit_bytes=VMEM_BYTES),
        cost_estimate=cost(6),
        name="token_grads",
    )(dq, dk, dv, w)


def weight_grads_kernel(
    spot_ref, dq_ref, dk_ref, dv_ref, x_ref, ext_ref, a_ref, b_ref, so_ref, cq_ref, ckv_ref, packed_ref, acc, sum_v
):
    j = pl.program_id(0)

    @pl.when(j == 0)
    def _():
        acc[...] = jnp.zeros_like(acc)
        acc[0:D, :] = dot_tn(dq_ref[...], x_ref[...])
        sum_v[...] = jnp.zeros_like(sum_v)

    dk, dv, ext = dk_ref[...], dv_ref[...], ext_ref[...]
    acc[D : 2 * D, :] += dot_tn(dk, ext)
    acc[2 * D : 3 * D, :] += dot_tn(dv, ext)
    sum_v[0:1, :] += total(dv.astype(F32))

    @pl.when(j == pl.num_programs(0) - 1)
    def _():
        sum_q = total(dq_ref[...].astype(F32))
        sums = jnp.concatenate([a_ref[0:4, :], b_ref[0:1, :], sum_q, sum_v[0:1, :], a_ref[0:1, :]], axis=0)
        cross = jnp.concatenate([cq_ref[...], ckv_ref[...].astype(BF)], axis=0)
        start = deal(packed_ref, spot_ref, 0, [acc[...].astype(BF), so_ref[...], cross])
        to_all(packed_ref, start, jnp.concatenate([sums, sums], axis=0).astype(BF))


def weight_grads(spots, dq, dk, dv, x, ext, a, b, g_so, g_cq, g_ckv):
    rows, keys = x.shape[0], ext.shape[0]
    tile = 512
    count = spots.shape[0]
    packed = 7 * D // count + 16
    fixed = lambda shape: pl.BlockSpec(shape, lambda j: (0, 0))
    moving = pl.BlockSpec((tile, D), lambda j: (j, 0))
    return pl.pallas_call(
        weight_grads_kernel,
        grid=(keys // tile,),
        in_specs=[pl.BlockSpec(memory_space=pltpu.SMEM), fixed((rows, D)), moving, moving, fixed((rows, D)), moving]
        + [fixed((8, D)), fixed((8, D)), fixed((D, D)), fixed((D, D)), fixed((2 * D, D))],
        out_specs=pl.BlockSpec((count, packed, D), lambda j: (0, 0, 0)),
        out_shape=jax.ShapeDtypeStruct((count, packed, D), BF),
        scratch_shapes=[pltpu.VMEM((3 * D, D), F32), pltpu.VMEM((8, D), F32)],
        compiler_params=pltpu.CompilerParams(vmem_limit_bytes=VMEM_BYTES),
        cost_estimate=cost(9),
        name="weight_grads",
    )(spots, dq, dk, dv, x, ext, a, b, g_so, g_cq, g_ckv)


def split(summed, rows):
    pieces, start = [], 0
    for n in rows:
        pieces.append(summed[start : start + n])
        start += n
    return pieces


def one_hot(targets, count):
    return (lax.broadcasted_iota(jnp.int32, (count, targets.shape[0]), 0) == targets[None, :]).astype(BF)


def body(
    tokens,
    memory,
    cotangent,
    deal_order,
    lengths,
    mem_index,
    self_qkv,
    self_out,
    cross_qkv,
    cross_out,
    ffn_in,
    ffn_out,
    norm_gains,
    biases,
    ffn_bias,
):
    grid = Grid()
    heads, blocks = grid.head, grid.blk
    rows = tokens.shape[0]
    block_rows = rows * heads
    mem_rows = memory.shape[0]
    assert mem_rows * heads == MEM
    block = lax.axis_index("blk")
    here = lax.axis_index("head")
    chunks = ffn_out.shape[0] // D

    w_qkv, w_so, w_cqkv, w_co, w_in = (
        w.T for w in (self_qkv, self_out, cross_qkv, cross_out, ffn_in)
    )
    w_out = jnp.transpose(ffn_out.reshape(chunks, D, -1), (0, 2, 1)).reshape(-1, D)
    n_out = w_so.shape[0]
    lanes = norm_gains.shape[1]
    small = jnp.concatenate([norm_gains.reshape(-1), biases.reshape(-1), ffn_bias])
    small = jnp.pad(small[None], ((0, 15), (0, D - small.shape[0])))

    near = [tokens] + grid.others(tokens, "y")
    in_group = deal_order - block * block_rows
    groups = [lax.dynamic_slice_in_dim(in_group, ((here - k) % heads) * rows, rows) for k in range(heads)]
    stream_rows = dot_nn(one_hot(jnp.concatenate(groups), block_rows), jnp.concatenate(near, axis=0)).astype(BF)
    up = [(i, i + heads) for i in range(grid.count - heads)]
    down = [(j, i) for i, j in up]
    before = lax.ppermute(stream_rows, BOTH, up)
    behind = lax.ppermute(stream_rows, BOTH, down)
    ext = jnp.concatenate([before, stream_rows, behind], axis=0)

    urgent = jnp.concatenate([w_qkv, small, w_so, w_cqkv, w_co], axis=0)
    urgent_z = along(grid, [(urgent[None], [{}])], "z", True)
    urgent_xy = along(grid, urgent_z, "xy", False)
    moved, stream_rows = beside([m for m, _ in urgent_xy], stream_rows)
    urgent_xy = [(m, p) for m, (_, p) in zip(moved, urgent_xy)]
    held = along(grid, urgent_xy, "c", False)
    wt_qkv, wt_small, wt_so, wt_cqkv, wt_co = place(
        grid, held, [w_qkv.shape[0], 16, n_out, w_cqkv.shape[0], n_out]
    )

    late = jnp.concatenate([w_in, w_out], axis=0)
    late = [late] + grid.others(late, "y")
    late = [late[-k % heads] for k in range(heads)] * 2
    late = lax.dynamic_slice_in_dim(
        jnp.concatenate(late, axis=0), (-here) % heads * late[0].shape[0], heads * late[0].shape[0]
    )
    gathered = lax.all_gather(jnp.concatenate([memory, late], axis=0), "blk", axis=0, tiled=True)
    gathered = gathered.reshape(blocks, -1, D)
    cut = mem_rows * 5 // 8
    smalls = wt_small.reshape(grid.count, 16, D)[:, 0, : 13 * lanes + ffn_bias.shape[0]].astype(F32)
    vec = jnp.transpose(smalls[:, : 13 * lanes].reshape(grid.count, 13, lanes), (1, 0, 2)).reshape(13, D)
    vec = jnp.pad(vec, ((0, 3), (0, 0)))
    hidden_bias = smalls[:, 13 * lanes :].reshape(1, -1)

    place_own = groups[0]
    rank = jnp.sum((place_own[None, :] < place_own[:, None]).astype(jnp.int32), axis=1)
    order = one_hot(rank, rows)
    x = dot_nn(order, tokens).astype(BF)
    cot_hi, cot_lo = hi_lo(cotangent)
    cot = dot_nn(order, cot_hi) + dot_nn(order, cot_lo)
    spot = jnp.sum(jnp.where(rank[None, :] == jnp.arange(rows)[:, None], place_own[None, :], 0), axis=1)
    spot = spot + block_rows
    count = lengths.shape[0]
    tri = jnp.arange(count)[None, :] <= jnp.arange(count)[:, None]
    ends = jnp.sum(jnp.where(tri, lengths[None, :], 0), axis=1)
    starts = ends - lengths
    base = (block - 1) * block_rows
    ext_ends, ext_starts = ends - base, starts - base
    passed = ext_ends[None, :] <= spot[:, None]
    row_begin = jnp.max(jnp.where(passed, ext_ends[None, :], -base), axis=1)
    row_end = jnp.min(jnp.where(passed, jnp.int32(1 << 30), ext_ends[None, :]), axis=1)
    lane = jnp.arange(128)[None, :]
    ranges = jnp.where(lane == 0, row_begin[:, None], row_end[:, None])
    row_ranges = jnp.where(jnp.arange(8)[:, None] == 0, row_begin[None, :], row_end[None, :])
    tq = min(128, rows)
    tk = 256
    lo = jnp.min(row_begin.reshape(-1, tq), axis=1) // tk
    hi = (jnp.max(row_end.reshape(-1, tq), axis=1) + tk - 1) // tk
    lo = jnp.maximum(lo, 0)
    hi = jnp.minimum(hi, 3 * block_rows // tk)

    inside = (ext_starts < 2 * block_rows) & (ext_ends > block_rows)
    number = jnp.arange(count)
    key = jnp.where(inside, mem_index * count + number, blocks * count * 2 + number)
    slot = jnp.sum((key[None, :] < key[:, None]).astype(jnp.int32), axis=1)
    stacked = jnp.stack(groups)
    first = jnp.sum((stacked[None] + block_rows < ext_starts[:, None, None]).astype(jnp.int32), axis=2)
    final = jnp.sum((stacked[None] + block_rows < ext_ends[:, None, None]).astype(jnp.int32), axis=2)
    columns = jnp.concatenate(
        [mem_index[:, None], jnp.stack([first, final], axis=2).reshape(count, -1)], axis=1
    )
    sorted_columns = jnp.sum(
        jnp.where((slot[None, :] == number[:, None])[:, :, None], columns[None], 0), axis=1
    )
    steps = jnp.sum(inside.astype(jnp.int32))
    live = number < steps
    final_mem = jnp.sum(jnp.where(number == steps - 1, sorted_columns[:, 0], 0))
    mem_steps = jnp.where(live, sorted_columns[:, 0], final_mem)
    mem_table = jnp.concatenate([mem_steps, steps[None]])
    memories = jnp.arange(blocks)
    ahead = 0
    for dim, coordinate in (
        ("c", lambda m: m % grid.core),
        ("x", lambda m: m // grid.core % grid.size["x"]),
        ("z", lambda m: m // (grid.core * grid.size["x"])),
    ):
        ahead = ahead * grid.size[dim] + (coordinate(memories) - grid.at[dim]) % grid.size[dim]
    used = jnp.any(inside[:, None] & (mem_index[:, None] == memories[None, :]), axis=0)
    spot_table = jnp.where(used, ahead + 1, -(ahead + 1)).astype(jnp.int32)
    row_table = jnp.where(live[:, None], sorted_columns[:, 1:], 0).reshape(-1)

    bias_q, bias_v = vec[3], vec[4]
    q = ((dot_nt(x, wt_qkv[:D]) + bias_q).astype(BF) * SCALE).astype(BF)
    kv = (dot_nt(ext, wt_qkv[D:]) + jnp.concatenate([jnp.zeros((D,), F32), bias_v])).astype(BF)
    pairs = PAIRS if 3 * block_rows <= 4096 else 1
    att, lse = self_forward(q, kv, ranges, lo, hi, tq, tk, pairs)
    z1, cq = first_rows(x, att, wt_so, wt_cqkv[:D], vec)

    queries = [cq] + grid.others(cq, "y")
    wt_ckv = wt_cqkv[D:]
    bias_kv = jnp.concatenate([jnp.zeros((D,), F32), vec[7]])[None]
    mem_kv = memory_kv(mem_table, gathered, mem_rows, wt_ckv, bias_kv)
    ctq = min(128, rows)
    outs, lses = cross_forward(mem_table, row_table, mem_kv, queries, ctq)
    late = gathered[:, mem_rows:].reshape(grid.count, -1, D)
    late_rows = np.cumsum([0, w_in.shape[0]] + [n_out] * chunks)
    wt_in, *wt_out = (
        late[:, i:j].reshape(-1, D) for i, j in zip(late_rows[:-1], late_rows[1:])
    )
    w2 = jnp.stack(wt_out)
    own_outs = [outs[0]] + [grid.shift(outs[k], y=-k) for k in range(1, heads)]
    own_lses = [lses[0]] + [grid.shift(lses[k], y=-k) for k in range(1, heads)]

    spots = grid.spots("cxyz")
    shares = lambda packed: packed.reshape(
        grid.core, grid.size["x"] * grid.size["y"], grid.size["z"], -1, D
    )
    y, dz2, dcatt, stat, packed_1 = middle_rows(
        spots, z1, cot, own_outs, own_lses, wt_co, wt_in, w2, vec, hidden_bias
    )
    upstream = [dcatt] + grid.others(dcatt, "y")
    stats = [stat] + grid.others(stat, "y")
    (upstream, stats), terms_1 = beside((upstream, stats), grid.ahead(shares(packed_1), "c"))
    sum_1 = add(terms_1)
    terms_1 = grid.ahead(sum_1, "xy")
    outputs = cross_backward(
        mem_table,
        spot_table,
        row_table,
        mem_kv,
        gathered,
        wt_ckv,
        queries,
        after(upstream, sum_1),
        stats,
        ctq,
        grid.core,
    )
    outputs, terms_1 = beside(outputs, terms_1)
    keep_m, send_m, g_ckv, g_bv, *dcqs = outputs
    own_dcqs = [dcqs[0]] + [grid.shift(dcqs[k], y=-k) for k in range(1, heads)]
    terms_m = [keep_m] if grid.core == 1 else [keep_m, grid.shift(send_m, c=1)]
    terms_1 = grid.ahead(add(terms_1), "z")
    outputs = last_rows(z1, dz2, att, own_dcqs, wt_cqkv[:D], wt_so, vec)
    outputs, (terms_m, terms_1) = beside(outputs, (terms_m, terms_1))
    dz1, datt, delta, g_so, g_cq, gvec1 = outputs
    delta = jnp.pad(delta.reshape(PAIRS, 2, rows), ((0, 0), (0, 6), (0, 0)))
    sum_m = add(terms_m).reshape(grid.size["x"], grid.size["z"], mem_rows, D)
    terms_a = grid.ahead(sum_m[:, :, :cut], "x")
    terms_b = grid.ahead(jnp.swapaxes(sum_m[:, :, cut:], 0, 1), "z")
    outputs = self_backward(q, after(datt, sum_m), kv, row_ranges, lse, delta, lo, hi, tq, tk, pairs)
    outputs, (terms_a, terms_b) = beside(outputs, (terms_a, terms_b))
    sum_a, sum_b = add(terms_a), add(terms_b)
    dq, dk, dv = after(list(outputs), sum_a, sum_b)
    terms_a, terms_b = grid.ahead(sum_a, "z"), grid.ahead(sum_b, "x")

    outputs, terms_b = beside(token_grads(dq, dk, dv, wt_qkv), terms_b)
    dxq, back = outputs
    from_next = lax.ppermute(back[:block_rows], BOTH, down)
    from_prior = lax.ppermute(back[2 * block_rows :], BOTH, up)
    packed_2 = weight_grads(
        spots, after(dq, back, *terms_b), dk, dv, x, ext, gvec1, g_bv, g_so, g_cq, g_ckv
    )
    packed_2, (terms_a, from_next, from_prior) = beside(packed_2, (terms_a, from_next, from_prior))
    shared = (
        back[block_rows : 2 * block_rows].astype(F32) + from_next.astype(F32) + from_prior.astype(F32)
    ).astype(BF)

    def dealt(k):
        picks = lax.broadcasted_iota(jnp.int32, (rows, block_rows), 1) == groups[k][:, None]
        return dot_nn(picks.astype(BF), shared)

    grad_in = dz1 + dxq
    grad_hi, grad_lo = hi_lo(grad_in)
    grad_input = dot_tn(order, grad_hi) + dot_tn(order, grad_lo) + dealt(0)
    for k in range(1, heads):
        grad_input = grad_input + grid.shift(dealt(k).astype(BF), y=-k).astype(F32)
    y_hi, y_lo = hi_lo(y)
    layer_out = dot_tn(order, y_hi) + dot_tn(order, y_lo)
    grad_memory = jnp.concatenate([add(terms_a, F32), add(terms_b, F32)], axis=0)

    sum_2 = add(grid.ahead(shares(packed_2), "c"))
    sum_2 = add(grid.ahead(sum_2, "xy"))
    sum_2 = add(grid.ahead(sum_2, "z"), F32)
    sum_1 = add(terms_1, F32)
    s_in, s_co, *s_out, early = split(
        sum_1, [w_in.shape[0], n_out] + [n_out] * chunks + [sum_1.shape[0] - w_in.shape[0] - n_out * (1 + chunks)]
    )
    s_qkv, s_so, s_cq, final_rows = split(sum_2, [w_qkv.shape[0], n_out, w_cqkv.shape[0], 16])
    me = block * heads + here

    def mine(summed, first, count):
        return lax.dynamic_slice(summed, (first, me * lanes), (count, lanes))

    e, f = mine(early, 0, 6), mine(final_rows, 0, 7)
    width = ffn_bias.shape[0]
    s_bias = lax.dynamic_slice(early, (6 + me * width // D, me * width % D), (1, width))[0]
    return (
        layer_out,
        grad_input,
        grad_memory,
        s_qkv.T,
        s_so.T,
        s_cq.T,
        s_co.T,
        s_in.T,
        jnp.concatenate([s.T for s in s_out], axis=0),
        jnp.stack([f[0], e[3], e[0]]),
        jnp.stack([f[5], f[6], f[2], f[3], f[4], e[5], e[2], f[1], e[4], e[1]]),
        s_bias,
    )


def solution(mesh):
    rows = P(BOTH, None)
    cols = P(None, BOTH)
    return jax.shard_map(
        body,
        mesh=mesh,
        in_specs=(rows, rows, rows, P("blk"), P(), P()) + (cols,) * 8 + (P(BOTH),),
        out_specs=(rows,) * 3 + (cols,) * 8 + (P(BOTH),),
        check_vma=False,
    )
```

```python
import functools
import math

import jax
import jax.numpy as jnp
import numpy as np
from jax import lax
from jax.experimental import pallas as pl
from jax.experimental.pallas import tpu as pltpu
from jax.sharding import PartitionSpec as P

D = 512
HEADS = 8
MEM = 1024
HD = D // HEADS
PAIRS = HEADS // 2
SCALE = 1.0 / math.sqrt(HD)
EPSILON = 1e-05
GELU_SCALE = 0.7978845608028654
FILL = -1e30
FLOOR = -1e20
BOTH = ("blk", "head")
BF = jnp.bfloat16
F32 = jnp.float32
VMEM_BYTES = 60 * 1024 * 1024


def dot_nn(a, b):
    return lax.dot_general(a, b, (((1,), (0,)), ((), ())), preferred_element_type=F32)


def dot_nt(a, b):
    return lax.dot_general(a, b, (((1,), (1,)), ((), ())), preferred_element_type=F32)


def dot_tn(a, b):
    return lax.dot_general(a, b, (((0,), (0,)), ((), ())), preferred_element_type=F32)


def hi_lo(x):
    hi = x.astype(BF)
    return hi, (x - hi.astype(F32)).astype(BF)


class Grid:
    def __init__(self):
        self.blk = lax.axis_size("blk")
        self.head = lax.axis_size("head")
        self.core = 2 if self.blk % 2 == 0 else 1
        rest = self.blk // self.core
        major = 4 if rest % 4 == 0 else rest
        self.size = {"z": major, "x": rest // major, "c": self.core, "y": self.head}
        self.stride = {
            "y": 1,
            "c": self.head,
            "x": self.head * self.core,
            "z": self.head * self.core * (rest // major),
        }
        self.count = self.blk * self.head
        b = lax.axis_index("blk")
        self.at = {
            "y": lax.axis_index("head"),
            "c": b % self.core,
            "x": (b // self.core) % self.size["x"],
            "z": b // (self.core * self.size["x"]),
        }

    def shift(self, array, **steps):
        route = []
        for i in range(self.count):
            to = i
            for dim, step in steps.items():
                size, stride = self.size[dim], self.stride[dim]
                at = (i // stride) % size
                to += ((at + step) % size - at) * stride
            route.append((i, to))
        return lax.ppermute(array, BOTH, route)

    def offsets(self, dims):
        out = [{}]
        for dim in dims:
            out = [dict(o, **{dim: k}) for o in out for k in range(self.size[dim])]
        return out[1:]

    def others(self, array, dims):
        return [self.shift(array, **o) for o in self.offsets(dims)]

    def ahead(self, buffer, dims):
        return [buffer[0]] + [self.shift(buffer[k], **o) for k, o in enumerate(self.offsets(dims), 1)]

    def spots(self, order):
        device = jnp.arange(self.count)
        spot = 0
        for dim in order:
            at = device // self.stride[dim] % self.size[dim]
            spot = spot * self.size[dim] + (at - self.at[dim]) % self.size[dim]
        return spot.astype(jnp.int32)


def add(terms, dtype=BF):
    return sum(t.astype(F32) for t in terms).astype(dtype)


def beside(outputs, arrays):
    return lax.optimization_barrier((outputs, arrays))


def after(values, *first):
    return lax.optimization_barrier((values, *first))[0]


def cost(us):
    return pl.CostEstimate(flops=int(us * 1e3), transcendentals=0, bytes_accessed=0)


def along(grid, held, dims, join):
    out = []
    for array, places in held:
        arrays = [array] + grid.others(array, dims)
        tagged = [[dict(p, **o) for p in places] for o in [{}] + grid.offsets(dims)]
        if join:
            out.append((jnp.concatenate(arrays, axis=0), sum(tagged, [])))
        else:
            out += list(zip(arrays, tagged))
    return out


def place_kernel(z_size, rows, index_ref, *refs):
    arrays, outs = refs[: len(refs) - len(rows)], refs[len(refs) - len(rows) :]
    each = arrays[0].shape[0] // z_size
    i = pl.program_id(0)
    for a, array in enumerate(arrays):

        @pl.when(i // each == a)
        def _(array=array):
            for z in range(z_size):
                source = (i % each) * z_size + (index_ref[0] - z + z_size) % z_size
                start = 0
                for out, n in zip(outs, rows):
                    out[z, 0] = array[source, start : start + n, :]
                    start += n


def place(grid, held, rows):
    arrays = [a for a, _ in held]
    z_size = grid.size["z"]
    other = grid.count // z_size
    slot = []
    for _, places in held:
        for p in places[::z_size]:
            at = 0
            for dim in "xcy":
                at = at * grid.size[dim] + (grid.at[dim] - p.get(dim, 0)) % grid.size[dim]
            slot.append(at)
    index = jnp.stack([grid.at["z"]] + slot).astype(jnp.int32)
    outs = pl.pallas_call(
        functools.partial(place_kernel, z_size, rows),
        grid_spec=pltpu.PrefetchScalarGridSpec(
            num_scalar_prefetch=1,
            grid=(other,),
            in_specs=[pl.BlockSpec(a.shape, lambda i, _: (0, 0, 0)) for a in arrays],
            out_specs=[
                pl.BlockSpec((z_size, 1, n, D), lambda i, index: (0, index[i + 1], 0, 0)) for n in rows
            ],
        ),
        out_shape=[jax.ShapeDtypeStruct((z_size, other, n, D), BF) for n in rows],
        compiler_params=pltpu.CompilerParams(vmem_limit_bytes=VMEM_BYTES),
        cost_estimate=cost(5),
        name="place_weights",
    )(index, *arrays)
    return [out.reshape(grid.count * n, D) for out, n in zip(outs, rows)]


def lane_mask(rows):
    return lax.broadcasted_iota(jnp.int32, (rows, 2 * HD), 1) < HD


def two(low, x):
    zero = jnp.zeros_like(x)
    return jnp.concatenate([jnp.where(low, x, zero), jnp.where(low, zero, x)], axis=0)


def pick(low, x):
    half = x.shape[0] // 2
    return jnp.where(low, x[:half], x[half:])


def with_ones(v):
    return jnp.concatenate([v, jnp.ones_like(v)], axis=1)


def pair_cols(g):
    return slice(g * 2 * HD, (g + 1) * 2 * HD)


def self_forward_kernel(
    pairs, tq, tk, lo_ref, hi_ref, q_ref, k_ref, v_ref, range_ref, att_ref, lse_ref, score_ref, top_ref, acc_ref
):
    width = 2 * HD
    low = lane_mask(tq)
    for i in range(q_ref.shape[0] // tq):
        rows = pl.ds(i * tq, tq)
        begin = jnp.concatenate([range_ref[rows, 0:1]] * 2, axis=0)
        end = jnp.concatenate([range_ref[rows, 1:2]] * 2, axis=0)
        first = lo_ref[i]
        top_ref[...] = jnp.full_like(top_ref, FILL)
        acc_ref[...] = jnp.zeros_like(acc_ref)

        def scores(t, carry, i=i):
            keys = pl.ds(pl.multiple_of(t * tk, tk), tk)
            spot = pl.ds(pl.multiple_of((t - first) * tk, tk), tk)
            place = lax.broadcasted_iota(jnp.int32, (2 * tq, tk), 1) + t * tk
            allowed = (place >= begin) & (place < end)
            for g in range(pairs):
                s = dot_nt(two(low, q_ref[pl.ds(i * tq, tq), pair_cols(g)]), k_ref[keys, pair_cols(g)])
                s = jnp.where(allowed, s, FILL)
                score_ref[g, :, spot] = s
                peak = top_ref[g]
                for c in range(tk // width):
                    peak = jnp.maximum(peak, s[:, c * width : (c + 1) * width])
                top_ref[g] = peak
            return carry

        lax.fori_loop(first, hi_ref[i], scores, 0)
        for g in range(pairs):
            peak = jnp.max(top_ref[g], axis=1, keepdims=True)
            top_ref[g] = jnp.broadcast_to(peak, (2 * tq, width))

        def weigh(t, carry):
            keys = pl.ds(pl.multiple_of(t * tk, tk), tk)
            spot = pl.ds(pl.multiple_of((t - first) * tk, tk), tk)
            for g in range(pairs):
                p = jnp.exp(score_ref[g, :, spot] - top_ref[g, :, 0:1]).astype(BF)
                acc_ref[g] += dot_nn(p, with_ones(v_ref[keys, pair_cols(g)]))
            return carry

        lax.fori_loop(first, hi_ref[i], weigh, 0)
        for g in range(pairs):
            mass = acc_ref[g, :, width:]
            att_ref[rows, pair_cols(g)] = pick(low, acc_ref[g, :, :width] / mass).astype(BF)
            flat = (top_ref[g] + jnp.log(mass)).T
            lse_ref[g, 0:1, rows] = flat[0:1, :tq]
            lse_ref[g, 1:2, rows] = flat[0:1, tq:]


def self_forward(q, kv, ranges, lo, hi, tq, tk, pairs):
    rows, keys = q.shape[0], kv.shape[0]
    width = pairs * 2 * HD
    groups = PAIRS // pairs
    return pl.pallas_call(
        functools.partial(self_forward_kernel, pairs, tq, tk),
        grid_spec=pltpu.PrefetchScalarGridSpec(
            num_scalar_prefetch=2,
            grid=(groups,),
            in_specs=[
                pl.BlockSpec((rows, width), lambda g, *_: (0, g)),
                pl.BlockSpec((keys, width), lambda g, *_: (0, g)),
                pl.BlockSpec((keys, width), lambda g, *_: (0, groups + g)),
                pl.BlockSpec((rows, 128), lambda g, *_: (0, 0)),
            ],
            out_specs=[
                pl.BlockSpec((rows, width), lambda g, *_: (0, g)),
                pl.BlockSpec((pairs, 8, rows), lambda g, *_: (g, 0, 0)),
            ],
            scratch_shapes=[
                pltpu.VMEM((pairs, 2 * tq, keys), F32),
                pltpu.VMEM((pairs, 2 * tq, 2 * HD), F32),
                pltpu.VMEM((pairs, 2 * tq, 4 * HD), F32),
            ],
        ),
        out_shape=[
            jax.ShapeDtypeStruct((rows, D), BF),
            jax.ShapeDtypeStruct((PAIRS, 8, rows), F32),
        ],
        compiler_params=pltpu.CompilerParams(vmem_limit_bytes=VMEM_BYTES),
        cost_estimate=cost(20),
        name="self_forward",
    )(lo, hi, q, kv, kv, ranges)


def self_backward_kernel(
    pairs, tq, tk, lo_ref, hi_ref, q_ref, do_ref, k_ref, v_ref, row_ref, lse_ref, delta_ref, dq_ref, dk_ref, dv_ref,
    acc_q, acc_k, acc_v,
):
    low = lane_mask(tq)
    acc_k[...] = jnp.zeros_like(acc_k)
    acc_v[...] = jnp.zeros_like(acc_v)
    for i in range(q_ref.shape[0] // tq):
        rows = pl.ds(i * tq, tq)
        begin = jnp.concatenate([row_ref[0:1, rows]] * 2, axis=1)
        end = jnp.concatenate([row_ref[1:2, rows]] * 2, axis=1)
        acc_q[...] = jnp.zeros_like(acc_q)

        def step(t, carry, i=i):
            rows = pl.ds(i * tq, tq)
            keys = pl.ds(pl.multiple_of(t * tk, tk), tk)
            place = lax.broadcasted_iota(jnp.int32, (tk, 2 * tq), 0) + t * tk
            allowed = (place >= begin) & (place < end)
            for g in range(pairs):
                cols = pair_cols(g)
                k, v = k_ref[keys, cols], v_ref[keys, cols]
                q2, do2 = two(low, q_ref[rows, cols]), two(low, do_ref[rows, cols])
                lse = jnp.concatenate([lse_ref[g, 0:1, rows], lse_ref[g, 1:2, rows]], axis=1)
                delta = jnp.concatenate([delta_ref[g, 0:1, rows], delta_ref[g, 1:2, rows]], axis=1)
                p = jnp.exp(jnp.where(allowed, dot_nt(k, q2) - lse, FILL))
                ds = (p * (dot_nt(v, do2) - delta)).astype(BF)
                acc_v[keys, cols] += dot_nn(p.astype(BF), do2)
                acc_k[keys, cols] += dot_nn(ds, q2)
                acc_q[g] += dot_tn(ds, k)
            return carry

        lax.fori_loop(lo_ref[i], hi_ref[i], step, 0)
        for g in range(pairs):
            dq_ref[rows, pair_cols(g)] = (pick(low, acc_q[g]) * SCALE).astype(BF)
    dk_ref[...] = acc_k[...].astype(BF)
    dv_ref[...] = acc_v[...].astype(BF)


def self_backward(q, do, kv, row_range, lse, delta, lo, hi, tq, tk, pairs):
    rows, keys = q.shape[0], kv.shape[0]
    width = pairs * 2 * HD
    groups = PAIRS // pairs
    return pl.pallas_call(
        functools.partial(self_backward_kernel, pairs, tq, tk),
        grid_spec=pltpu.PrefetchScalarGridSpec(
            num_scalar_prefetch=2,
            grid=(groups,),
            in_specs=[
                pl.BlockSpec((rows, width), lambda g, *_: (0, g)),
                pl.BlockSpec((rows, width), lambda g, *_: (0, g)),
                pl.BlockSpec((keys, width), lambda g, *_: (0, g)),
                pl.BlockSpec((keys, width), lambda g, *_: (0, groups + g)),
                pl.BlockSpec((8, rows), lambda g, *_: (0, 0)),
                pl.BlockSpec((pairs, 8, rows), lambda g, *_: (g, 0, 0)),
                pl.BlockSpec((pairs, 8, rows), lambda g, *_: (g, 0, 0)),
            ],
            out_specs=[
                pl.BlockSpec((rows, width), lambda g, *_: (0, g)),
                pl.BlockSpec((keys, width), lambda g, *_: (0, g)),
                pl.BlockSpec((keys, width), lambda g, *_: (0, g)),
            ],
            scratch_shapes=[
                pltpu.VMEM((pairs, 2 * tq, 2 * HD), F32),
                pltpu.VMEM((keys, width), F32),
                pltpu.VMEM((keys, width), F32),
            ],
        ),
        out_shape=[
            jax.ShapeDtypeStruct((rows, D), BF),
            jax.ShapeDtypeStruct((keys, D), BF),
            jax.ShapeDtypeStruct((keys, D), BF),
        ],
        compiler_params=pltpu.CompilerParams(vmem_limit_bytes=VMEM_BYTES),
        cost_estimate=cost(40),
        name="self_backward",
    )(lo, hi, q, do, kv, kv, row_range, lse, delta)


def memory_kv_kernel(mem_ref, m_ref, w_ref, b_ref, kv_ref):
    j = pl.program_id(0)

    @pl.when((j == 0) | (mem_ref[j] != mem_ref[jnp.maximum(j - 1, 0)]))
    def _():
        kv_ref[0] = (dot_nt(m_ref[0], w_ref[...]) + b_ref[...]).astype(BF)


def memory_kv(mem, gathered, n, weights, bias):
    blocks = gathered.shape[0]
    by_memory = lambda j, mem: (mem[j], 0, 0)
    return pl.pallas_call(
        memory_kv_kernel,
        grid_spec=pltpu.PrefetchScalarGridSpec(
            num_scalar_prefetch=1,
            grid=(mem.shape[0] - 1,),
            in_specs=[
                pl.BlockSpec((1, n, D), by_memory),
                pl.BlockSpec((2 * D, D), lambda j, *_: (0, 0)),
                pl.BlockSpec((1, 2 * D), lambda j, *_: (0, 0)),
            ],
            out_specs=pl.BlockSpec((1, n, 2 * D), by_memory),
        ),
        out_shape=jax.ShapeDtypeStruct((blocks, n, 2 * D), BF),
        compiler_params=pltpu.CompilerParams(vmem_limit_bytes=VMEM_BYTES),
        cost_estimate=cost(6),
        name="memory_kv",
    )(mem, gathered, weights, bias)


def cross_forward_kernel(parts, tq, mem_ref, table_ref, kv_ref, *refs):
    qs, outs, lses = refs[:parts], refs[parts : 2 * parts], refs[2 * parts : 3 * parts]
    width = 2 * HD
    j = pl.program_id(0)
    low = lane_mask(tq)
    for part in range(parts):
        first_row = table_ref[j * 2 * parts + 2 * part]
        last_row = table_ref[j * 2 * parts + 2 * part + 1]

        def step(t, carry, part=part, first_row=first_row, last_row=last_row):
            offset = pl.multiple_of(t * tq, tq)
            rows = pl.ds(offset, tq)
            at = lax.broadcasted_iota(jnp.int32, (tq, width), 0) + offset
            mine = (at >= first_row) & (at < last_row)
            at_row = lax.broadcasted_iota(jnp.int32, (1, tq), 1) + offset
            mine_row = (at_row >= first_row) & (at_row < last_row)
            for g in range(PAIRS):
                cols = pair_cols(g)
                s = dot_nt(two(low, qs[part][rows, cols]), kv_ref[0, :, cols])
                peak = jnp.max(s, axis=1, keepdims=True)
                p = jnp.exp(s - peak).astype(BF)
                acc = dot_nn(p, with_ones(kv_ref[0, :, pair_cols(PAIRS + g)]))
                mass = acc[:, width:]
                new = pick(low, acc[:, :width] / mass).astype(BF)
                outs[part][rows, cols] = jnp.where(mine, new, outs[part][rows, cols])
                flat = (peak + jnp.log(mass)).T
                for i in range(2):
                    head = slice(2 * g + i, 2 * g + i + 1)
                    lses[part][head, rows] = jnp.where(
                        mine_row, flat[0:1, i * tq : (i + 1) * tq], lses[part][head, rows]
                    )
            return carry

        lax.fori_loop(first_row // tq, (last_row + tq - 1) // tq, step, 0)


def cross_forward(mem, table, kv, queries, tq):
    parts, rows, n = len(queries), queries[0].shape[0], kv.shape[1]
    whole = pl.BlockSpec((rows, D), lambda j, *_: (0, 0))
    flat = pl.BlockSpec((HEADS, rows), lambda j, *_: (0, 0))
    out = pl.pallas_call(
        functools.partial(cross_forward_kernel, parts, tq),
        grid_spec=pltpu.PrefetchScalarGridSpec(
            num_scalar_prefetch=2,
            grid=(mem.shape[0] - 1,),
            in_specs=[pl.BlockSpec((1, n, 2 * D), lambda j, mem, _: (mem[j], 0, 0))] + [whole] * parts,
            out_specs=[whole] * parts + [flat] * parts,
        ),
        out_shape=[jax.ShapeDtypeStruct((rows, D), BF)] * parts
        + [jax.ShapeDtypeStruct((HEADS, rows), F32)] * parts,
        compiler_params=pltpu.CompilerParams(vmem_limit_bytes=VMEM_BYTES),
        cost_estimate=cost(16),
        name="cross_forward",
    )(mem, table, kv, *queries)
    return out[:parts], out[parts:]


def cross_backward_kernel(parts, tq, blocks, mem_ref, spot_ref, table_ref, kv_ref, m_ref, w_ref, *refs):
    qs, dos, stats = refs[:parts], refs[parts : 2 * parts], refs[2 * parts : 3 * parts]
    keep_ref, send_ref, gw_ref, gb_ref = refs[3 * parts : 3 * parts + 4]
    dqs = refs[3 * parts + 4 : 4 * parts + 4]
    acc_k, acc_v, acc_q, stage, zero, stage_sem, zero_sem = refs[4 * parts + 4 :]
    j = pl.program_id(0)
    last = mem_ref.shape[0] - 2
    steps = mem_ref[last + 1]
    now = mem_ref[j]
    previous = mem_ref[jnp.maximum(j - 1, 0)]
    following = mem_ref[jnp.minimum(j + 1, last)]
    low = lane_mask(tq)
    half = keep_ref.shape[0]

    def to_target(source, spot, sem, wanted, act):
        for target, mine in ((keep_ref, spot < half), (send_ref, spot >= half)):
            copy = pltpu.make_async_copy(source, target.at[spot % half], sem)
            pl.when(wanted & mine)(functools.partial(act, copy))

    start, wait = (lambda copy: copy.start()), (lambda copy: copy.wait())

    def zeros(act):
        for m in range(blocks):
            spot = spot_ref[m]
            to_target(zero, jnp.abs(spot) - 1, zero_sem.at[m], spot < 0, act)

    @pl.when(j == 0)
    def _():
        acc_q[...] = jnp.zeros_like(acc_q)
        gw_ref[...] = jnp.zeros_like(gw_ref)
        gb_ref[...] = jnp.zeros_like(gb_ref)
        zero[...] = jnp.zeros_like(zero)
        zeros(start)

    @pl.when((j == 0) | (now != previous))
    def _():
        acc_k[...] = jnp.zeros_like(acc_k)
        acc_v[...] = jnp.zeros_like(acc_v)

    for part in range(parts):
        first_row = table_ref[j * 2 * parts + 2 * part]
        last_row = table_ref[j * 2 * parts + 2 * part + 1]

        def step(t, carry, part=part, first_row=first_row, last_row=last_row):
            offset = pl.multiple_of(t * tq, tq)
            rows = pl.ds(offset, tq)
            at_row = lax.broadcasted_iota(jnp.int32, (1, tq), 1) + offset
            mine = (at_row >= first_row) & (at_row < last_row)
            for g in range(PAIRS):
                cols = pair_cols(g)
                k, v = kv_ref[0, :, cols], kv_ref[0, :, pair_cols(PAIRS + g)]
                q2, do2 = two(low, qs[part][rows, cols]), two(low, dos[part][rows, cols])

                def stat(base, part=part, g=g):
                    return [stats[part][base + 2 * g + i : base + 2 * g + i + 1, rows] for i in range(2)]

                lse = jnp.concatenate([jnp.where(mine, x, -FILL) for x in stat(0)], axis=1)
                delta = jnp.concatenate(stat(HEADS), axis=1)
                p = jnp.exp(dot_nt(k, q2) - lse)
                ds = (p * (dot_nt(v, do2) - delta)).astype(BF)
                acc_v[:, cols] += dot_nn(p.astype(BF), do2)
                acc_k[:, cols] += dot_nn(ds, q2)
                acc_q[part, rows, cols] += pick(low, dot_tn(ds, k))
            return carry

        lax.fori_loop(first_row // tq, (last_row + tq - 1) // tq, step, 0)

    @pl.when((j == steps - 1) | ((j < steps) & (now != following)))
    def _():
        dk, dv = acc_k[...].astype(BF), acc_v[...].astype(BF)
        spot = spot_ref[now] - 1
        stage[...] = (dot_nn(dk, w_ref[0:D, :]) + dot_nn(dv, w_ref[D : 2 * D, :])).astype(BF)
        to_target(stage, spot, stage_sem, spot >= 0, start)
        gw_ref[0:D, :] += dot_tn(dk, m_ref[0])
        gw_ref[D : 2 * D, :] += dot_tn(dv, m_ref[0])
        gb_ref[0:1, :] += jnp.sum(dv.astype(F32), axis=0, keepdims=True)
        to_target(stage, spot, stage_sem, spot >= 0, wait)

    @pl.when(j == steps - 1)
    def _():
        for part in range(parts):
            dqs[part][...] = (acc_q[part] * SCALE).astype(BF)
        zeros(wait)


def cross_backward(mem, spot, table, kv, rows_of_memory, weights, queries, upstream, stats, tq, cores):
    parts, rows, n = len(queries), queries[0].shape[0], kv.shape[1]
    blocks = kv.shape[0]
    whole = pl.BlockSpec((rows, D), lambda j, *_: (0, 0))
    flat = pl.BlockSpec((2 * HEADS, rows), lambda j, *_: (0, 0))
    by_memory = lambda j, mem, *_: (mem[j], 0, 0)
    anywhere = pl.BlockSpec(memory_space=pl.ANY)
    return pl.pallas_call(
        functools.partial(cross_backward_kernel, parts, tq, blocks),
        grid_spec=pltpu.PrefetchScalarGridSpec(
            num_scalar_prefetch=3,
            grid=(mem.shape[0] - 1,),
            in_specs=[
                pl.BlockSpec((1, n, 2 * D), by_memory),
                pl.BlockSpec((1, n, D), by_memory),
                pl.BlockSpec((2 * D, D), lambda j, *_: (0, 0)),
            ]
            + [whole] * (2 * parts)
            + [flat] * parts,
            out_specs=[
                anywhere,
                anywhere,
                pl.BlockSpec((2 * D, D), lambda j, *_: (0, 0)),
                pl.BlockSpec((8, D), lambda j, *_: (0, 0)),
            ]
            + [whole] * parts,
            scratch_shapes=[
                pltpu.VMEM((n, D), F32),
                pltpu.VMEM((n, D), F32),
                pltpu.VMEM((parts, rows, D), F32),
                pltpu.VMEM((n, D), BF),
                pltpu.VMEM((n, D), BF),
                pltpu.SemaphoreType.DMA,
                pltpu.SemaphoreType.DMA((blocks,)),
            ],
        ),
        out_shape=[jax.ShapeDtypeStruct((blocks // cores, n, D), BF)] * 2
        + [
            jax.ShapeDtypeStruct((2 * D, D), F32),
            jax.ShapeDtypeStruct((8, D), F32),
        ]
        + [jax.ShapeDtypeStruct((rows, D), BF)] * parts,
        compiler_params=pltpu.CompilerParams(vmem_limit_bytes=VMEM_BYTES),
        cost_estimate=cost(32),
        name="cross_backward",
    )(mem, spot, table, kv, rows_of_memory, weights, *queries, *upstream, *stats)


def norm(z):
    centre = z - jnp.mean(z, axis=1, keepdims=True)
    inverse = lax.rsqrt(jnp.mean(centre * centre, axis=1, keepdims=True) + EPSILON)
    return centre * inverse, inverse


def norm_back(upstream, normed, inverse, gain):
    scaled = upstream * gain
    return inverse * (
        scaled
        - jnp.mean(scaled, axis=1, keepdims=True)
        - normed * jnp.mean(scaled * normed, axis=1, keepdims=True)
    )


def total(x):
    return jnp.sum(x, axis=0, keepdims=True)


def head_rows():
    lane = lax.broadcasted_iota(jnp.int32, (HEADS, D), 1) // HD
    return (lane == lax.broadcasted_iota(jnp.int32, (HEADS, D), 0)).astype(F32).astype(BF)


def per_head(product):
    hi, lo = hi_lo(product)
    heads = head_rows()
    return dot_nt(heads, hi) + dot_nt(heads, lo)


def spread(rows):
    hi, lo = hi_lo(rows)
    heads = head_rows()
    return dot_tn(hi, heads) + dot_tn(lo, heads)


def deal(packed_ref, spot_ref, start, values):
    count = packed_ref.shape[0]
    for value in values:
        n = value.shape[0] // count
        for i in range(count):
            packed_ref[spot_ref[i], start : start + n, :] = value[i * n : (i + 1) * n]
        start += n
    return start


def to_all(packed_ref, start, rows):
    for i in range(packed_ref.shape[0]):
        packed_ref[i, start : start + rows.shape[0], :] = rows


def first_kernel(x_ref, att_ref, wo_ref, wq_ref, vec_ref, z_ref, cq_ref):
    z = x_ref[...].astype(F32) + dot_nt(att_ref[...], wo_ref[...]) + vec_ref[5:6, :]
    z_ref[...] = z
    n, _ = norm(z)
    low = (n * vec_ref[0:1, :] + vec_ref[10:11, :]).astype(BF)
    cq_ref[...] = ((dot_nt(low, wq_ref[...]) + vec_ref[6:7, :]).astype(BF) * SCALE).astype(BF)


def first_rows(x, att, wo, wq, vec):
    rows = x.shape[0]
    return pl.pallas_call(
        first_kernel,
        out_shape=[jax.ShapeDtypeStruct((rows, D), F32), jax.ShapeDtypeStruct((rows, D), BF)],
        compiler_params=pltpu.CompilerParams(vmem_limit_bytes=VMEM_BYTES),
        cost_estimate=cost(4),
        name="first_rows",
    )(x, att, wo, wq, vec)


def middle_kernel(parts, chunks, spot_ref, *refs):
    z1_ref, cot_ref = refs[:2]
    outs = refs[2 : 2 + parts]
    lses = refs[2 + parts : 2 + 2 * parts]
    wco_ref, w1_ref, w2_ref, vec_ref, fb_ref = refs[2 + 2 * parts : 7 + 2 * parts]
    y_ref, dz2_ref, dcatt_ref, stat_ref, packed_ref, send_ref, hid_ref, slope_ref, gw1_ref = refs[7 + 2 * parts :]
    vec = lambda i: vec_ref[i : i + 1, :]
    peak = lses[0][...]
    for part in range(1, parts):
        peak = jnp.maximum(peak, lses[part][...])
    mass = 0.0
    for part in range(parts):
        mass = mass + jnp.exp(lses[part][...] - peak)
    lse = peak + jnp.log(mass)
    catt32 = 0.0
    for part in range(parts):
        catt32 = catt32 + spread(jnp.exp(lses[part][...] - lse)) * outs[part][...].astype(F32)
    catt = catt32.astype(BF)
    n1, _ = norm(z1_ref[...])
    h1 = n1 * vec(0) + vec(10)
    z2 = h1 + dot_nt(catt, wco_ref[...]) + vec(8)
    n2, r2 = norm(z2)
    h2 = n2 * vec(1) + vec(11)
    h2_low = h2.astype(BF)
    z3 = h2 + vec(9)
    for c in range(chunks):
        cols = slice(c * D, (c + 1) * D)
        u = dot_nt(h2_low, w1_ref[cols, :]) + fb_ref[:, cols]
        square = u * u
        t = jnp.tanh(GELU_SCALE * (u + 0.044715 * u * square))
        hid = (0.5 * u * (1.0 + t)).astype(BF)
        hid_ref[:, cols] = hid
        slope_ref[:, cols] = 0.5 * (1.0 + t) + 0.5 * u * (1.0 - t * t) * (
            GELU_SCALE * (1.0 + 3.0 * 0.044715 * square)
        )
        z3 = z3 + dot_nt(hid, w2_ref[c])
    n3, r3 = norm(z3)
    y_ref[...] = n3 * vec(2) + vec(12)
    cot = cot_ref[...]
    dz3 = norm_back(cot, n3, r3, vec(2))
    df = dz3.astype(BF)
    sums = [total(cot * n3), total(cot), total(df.astype(F32))]
    hidden_sums, g_out = [], []
    e2 = dz3
    for c in range(chunks):
        cols = slice(c * D, (c + 1) * D)
        hid = hid_ref[:, cols]
        g_out.append(dot_tn(df, hid).astype(BF))
        du = (dot_nn(df, w2_ref[c]) * slope_ref[:, cols]).astype(BF)
        gw1_ref[cols, :] = dot_tn(du, h2_low).astype(BF)
        hidden_sums.append(total(du.astype(F32)))
        e2 = e2 + dot_nn(du, w1_ref[cols, :])
    dz2 = norm_back(e2, n2, r2, vec(1))
    dz2_ref[...] = dz2
    dca = dz2.astype(BF)
    sums += [total(e2 * n2), total(e2), total(dca.astype(F32))] + hidden_sums
    sums += [jnp.zeros_like(sums[0])] * (-len(sums) % 16)
    start = deal(packed_ref, spot_ref, 0, [gw1_ref[...], dot_tn(dca, catt).astype(BF)] + g_out)
    to_all(packed_ref, start, jnp.concatenate(sums, axis=0).astype(BF))
    send_ref[...] = packed_ref[packed_ref.shape[0] - send_ref.shape[0] :]
    dcatt = dot_nn(dca, wco_ref[...]).astype(BF)
    dcatt_ref[...] = dcatt
    stat_ref[0:HEADS, :] = lse
    stat_ref[HEADS : 2 * HEADS, :] = per_head(dcatt.astype(F32) * catt32)


def middle_rows(spots, z1, cot, outs, lses, wco, w1, w2, vec, fb, send):
    rows, parts, chunks = z1.shape[0], len(outs), w2.shape[0]
    hidden = chunks * D
    count = spots.shape[0]
    packed = (hidden + (1 + chunks) * D) // count + 6 + chunks + -(6 + chunks) % 16
    operands = [z1, cot, *outs, *lses, wco, w1, w2, vec, fb]
    out_shape = [
        jax.ShapeDtypeStruct((rows, D), F32),
        jax.ShapeDtypeStruct((rows, D), F32),
        jax.ShapeDtypeStruct((rows, D), BF),
        jax.ShapeDtypeStruct((2 * HEADS, rows), F32),
        jax.ShapeDtypeStruct((count, packed, D), BF),
        jax.ShapeDtypeStruct((send, packed, D), BF),
    ]
    whole = pl.BlockSpec(memory_space=pltpu.VMEM)
    return pl.pallas_call(
        functools.partial(middle_kernel, parts, chunks),
        in_specs=[pl.BlockSpec(memory_space=pltpu.SMEM)] + [whole] * len(operands),
        out_specs=[whole] * len(out_shape),
        out_shape=out_shape,
        scratch_shapes=[
            pltpu.VMEM((rows, hidden), BF),
            pltpu.VMEM((rows, hidden), F32),
            pltpu.VMEM((hidden, D), BF),
        ],
        compiler_params=pltpu.CompilerParams(vmem_limit_bytes=VMEM_BYTES),
        cost_estimate=cost(18),
        name="middle_rows",
    )(spots, *operands)


def last_kernel(parts, *refs):
    z1_ref, dz2_ref, att_ref = refs[:3]
    dcqs = refs[3 : 3 + parts]
    wq_ref, wo_ref, vec_ref = refs[3 + parts : 6 + parts]
    dz1_ref, datt_ref, delta_ref, gwo_ref, gwq_ref, gvec_ref = refs[6 + parts :]
    dcq = 0.0
    for part in dcqs:
        dcq = dcq + part[...].astype(F32)
    dcq = dcq.astype(BF)
    n1, r1 = norm(z1_ref[...])
    low = (n1 * vec_ref[0:1, :] + vec_ref[10:11, :]).astype(BF)
    e1 = dz2_ref[...] + dot_nn(dcq, wq_ref[...])
    dz1 = norm_back(e1, n1, r1, vec_ref[0:1, :])
    dz1_ref[...] = dz1
    da = dz1.astype(BF)
    datt = dot_nn(da, wo_ref[...]).astype(BF)
    datt_ref[...] = datt
    delta_ref[...] = per_head(datt.astype(F32) * att_ref[...].astype(F32))
    gwo_ref[...] = dot_tn(da, att_ref[...]).astype(BF)
    gwq_ref[...] = dot_tn(dcq, low).astype(BF)
    gvec_ref[...] = jnp.zeros_like(gvec_ref)
    gvec_ref[0:1, :] = total(e1 * n1)
    gvec_ref[1:2, :] = total(e1)
    gvec_ref[2:3, :] = total(da.astype(F32))
    gvec_ref[3:4, :] = total(dcq.astype(F32))


def last_rows(z1, dz2, att, dcqs, wq, wo, vec):
    rows = z1.shape[0]
    return pl.pallas_call(
        functools.partial(last_kernel, len(dcqs)),
        out_shape=[
            jax.ShapeDtypeStruct((rows, D), F32),
            jax.ShapeDtypeStruct((rows, D), BF),
            jax.ShapeDtypeStruct((HEADS, rows), F32),
            jax.ShapeDtypeStruct((D, D), BF),
            jax.ShapeDtypeStruct((D, D), BF),
            jax.ShapeDtypeStruct((8, D), F32),
        ],
        compiler_params=pltpu.CompilerParams(vmem_limit_bytes=VMEM_BYTES),
        cost_estimate=cost(6),
        name="last_rows",
    )(z1, dz2, att, *dcqs, wq, wo, vec)


def third(steps, part):
    return lambda j: (jnp.clip(j - part * steps, 0, steps - 1), 0)


def token_grads_kernel(dq_ref, dk_ref, dv_ref, w_ref, dx_ref, *backs):
    j = pl.program_id(0)

    @pl.when(j == 0)
    def _():
        dx_ref[...] = dot_nn(dq_ref[...], w_ref[0:D, :])

    back = (dot_nn(dk_ref[...], w_ref[D : 2 * D, :]) + dot_nn(dv_ref[...], w_ref[2 * D : 3 * D, :])).astype(BF)
    for part, back_ref in enumerate(backs):

        @pl.when(j // (pl.num_programs(0) // 3) == part)
        def _(back_ref=back_ref):
            back_ref[...] = back


def token_grads(dq, dk, dv, w):
    rows, keys = dq.shape[0], dk.shape[0]
    tile = 512
    steps = keys // tile // 3
    fixed = lambda shape: pl.BlockSpec(shape, lambda j: (0, 0))
    moving = pl.BlockSpec((tile, D), lambda j: (j, 0))
    return pl.pallas_call(
        token_grads_kernel,
        grid=(3 * steps,),
        in_specs=[fixed((rows, D)), moving, moving, fixed((3 * D, D))],
        out_specs=[fixed((rows, D))] + [pl.BlockSpec((tile, D), third(steps, part)) for part in range(3)],
        out_shape=[jax.ShapeDtypeStruct((rows, D), F32)] + [jax.ShapeDtypeStruct((keys // 3, D), BF)] * 3,
        compiler_params=pltpu.CompilerParams(vmem_limit_bytes=VMEM_BYTES),
        cost_estimate=cost(6),
        name="token_grads",
    )(dq, dk, dv, w)


def weight_grads_kernel(
    spot_ref, dq_ref, dk_ref, dv_ref, x_ref, before_ref, here_ref, behind_ref, a_ref, b_ref, so_ref, cq_ref, ckv_ref,
    packed_ref, send_ref, acc, sum_v,
):
    j = pl.program_id(0)
    part = j // (pl.num_programs(0) // 3)

    @pl.when(j == 0)
    def _():
        acc[...] = jnp.zeros_like(acc)
        acc[0:D, :] = dot_tn(dq_ref[...], x_ref[...])
        sum_v[...] = jnp.zeros_like(sum_v)

    dk, dv = dk_ref[...], dv_ref[...]
    for i, ext_ref in enumerate((before_ref, here_ref, behind_ref)):

        @pl.when(part == i)
        def _(ext_ref=ext_ref):
            acc[D : 2 * D, :] += dot_tn(dk, ext_ref[...])
            acc[2 * D : 3 * D, :] += dot_tn(dv, ext_ref[...])

    sum_v[0:1, :] += total(dv.astype(F32))

    @pl.when(j == pl.num_programs(0) - 1)
    def _():
        sum_q = total(dq_ref[...].astype(F32))
        sums = jnp.concatenate([a_ref[0:4, :], b_ref[0:1, :], sum_q, sum_v[0:1, :], a_ref[0:1, :]], axis=0)
        cross = jnp.concatenate([cq_ref[...], ckv_ref[...].astype(BF)], axis=0)
        start = deal(packed_ref, spot_ref, 0, [acc[...].astype(BF), so_ref[...], cross])
        to_all(packed_ref, start, jnp.concatenate([sums, sums], axis=0).astype(BF))
        send_ref[...] = packed_ref[packed_ref.shape[0] - send_ref.shape[0] :]


def weight_grads(spots, dq, dk, dv, x, exts, a, b, g_so, g_cq, g_ckv, send):
    rows, keys = x.shape[0], dk.shape[0]
    tile = 512
    steps = keys // tile // 3
    count = spots.shape[0]
    packed = 7 * D // count + 16
    fixed = lambda shape: pl.BlockSpec(shape, lambda j: (0,) * len(shape))
    moving = pl.BlockSpec((tile, D), lambda j: (j, 0))
    return pl.pallas_call(
        weight_grads_kernel,
        grid=(3 * steps,),
        in_specs=[pl.BlockSpec(memory_space=pltpu.SMEM), fixed((rows, D)), moving, moving, fixed((rows, D))]
        + [pl.BlockSpec((tile, D), third(steps, part)) for part in range(3)]
        + [fixed((8, D)), fixed((8, D)), fixed((D, D)), fixed((D, D)), fixed((2 * D, D))],
        out_specs=[fixed((count, packed, D)), fixed((send, packed, D))],
        out_shape=[jax.ShapeDtypeStruct((n, packed, D), BF) for n in (count, send)],
        scratch_shapes=[pltpu.VMEM((3 * D, D), F32), pltpu.VMEM((8, D), F32)],
        compiler_params=pltpu.CompilerParams(vmem_limit_bytes=VMEM_BYTES),
        cost_estimate=cost(9),
        name="weight_grads",
    )(spots, dq, dk, dv, x, *exts, a, b, g_so, g_cq, g_ckv)


def split(summed, rows):
    pieces, start = [], 0
    for n in rows:
        pieces.append(summed[start : start + n])
        start += n
    return pieces


def one_hot(targets, count):
    return (lax.broadcasted_iota(jnp.int32, (count, targets.shape[0]), 0) == targets[None, :]).astype(BF)


def body(
    tokens,
    memory,
    cotangent,
    deal_order,
    lengths,
    mem_index,
    self_qkv,
    self_out,
    cross_qkv,
    cross_out,
    ffn_in,
    ffn_out,
    norm_gains,
    biases,
    ffn_bias,
):
    grid = Grid()
    heads, blocks = grid.head, grid.blk
    rows = tokens.shape[0]
    block_rows = rows * heads
    mem_rows = memory.shape[0]
    assert mem_rows * heads == MEM
    block = lax.axis_index("blk")
    here = lax.axis_index("head")
    chunks = ffn_out.shape[0] // D

    w_qkv, w_so, w_cqkv, w_co, w_in = (
        w.T for w in (self_qkv, self_out, cross_qkv, cross_out, ffn_in)
    )
    w_out = jnp.transpose(ffn_out.reshape(chunks, D, -1), (0, 2, 1)).reshape(-1, D)
    n_out = w_so.shape[0]
    lanes = norm_gains.shape[1]
    small = jnp.concatenate([norm_gains.reshape(-1), biases.reshape(-1), ffn_bias])
    small = jnp.pad(small[None], ((0, 15), (0, D - small.shape[0])))

    near = [tokens] + grid.others(tokens, "y")
    in_group = deal_order - block * block_rows
    groups = [lax.dynamic_slice_in_dim(in_group, ((here - k) % heads) * rows, rows) for k in range(heads)]
    stream_rows = dot_nn(one_hot(jnp.concatenate(groups), block_rows), jnp.concatenate(near, axis=0)).astype(BF)
    up = [(i, i + heads) for i in range(grid.count - heads)]
    down = [(j, i) for i, j in up]
    before = lax.ppermute(stream_rows, BOTH, up)
    behind = lax.ppermute(stream_rows, BOTH, down)
    ext = jnp.concatenate([before, stream_rows, behind], axis=0)

    urgent = jnp.concatenate([w_qkv, small, w_so, w_cqkv, w_co], axis=0)
    urgent_z = along(grid, [(urgent[None], [{}])], "z", True)
    urgent_xy = along(grid, urgent_z, "xy", False)
    moved, stream_rows = beside([m for m, _ in urgent_xy], stream_rows)
    urgent_xy = [(m, p) for m, (_, p) in zip(moved, urgent_xy)]
    held = along(grid, urgent_xy, "c", False)
    wt_qkv, wt_small, wt_so, wt_cqkv, wt_co = place(
        grid, held, [w_qkv.shape[0], 16, n_out, w_cqkv.shape[0], n_out]
    )

    late = jnp.concatenate([w_in, w_out], axis=0)
    late = [late] + grid.others(late, "y")
    late = [late[-k % heads] for k in range(heads)] * 2
    late = lax.dynamic_slice_in_dim(
        jnp.concatenate(late, axis=0), (-here) % heads * late[0].shape[0], heads * late[0].shape[0]
    )
    gathered = lax.all_gather(jnp.concatenate([memory, late], axis=0), "blk", axis=0, tiled=True)
    gathered = gathered.reshape(blocks, -1, D)
    cut = mem_rows * 5 // 8
    smalls = wt_small.reshape(grid.count, 16, D)[:, 0, : 13 * lanes + ffn_bias.shape[0]].astype(F32)
    vec = jnp.transpose(smalls[:, : 13 * lanes].reshape(grid.count, 13, lanes), (1, 0, 2)).reshape(13, D)
    vec = jnp.pad(vec, ((0, 3), (0, 0)))
    hidden_bias = smalls[:, 13 * lanes :].reshape(1, -1)

    place_own = groups[0]
    rank = jnp.sum((place_own[None, :] < place_own[:, None]).astype(jnp.int32), axis=1)
    order = one_hot(rank, rows)
    x = dot_nn(order, tokens).astype(BF)
    cot_hi, cot_lo = hi_lo(cotangent)
    cot = dot_nn(order, cot_hi) + dot_nn(order, cot_lo)
    spot = jnp.sum(jnp.where(rank[None, :] == jnp.arange(rows)[:, None], place_own[None, :], 0), axis=1)
    spot = spot + block_rows
    count = lengths.shape[0]
    tri = jnp.arange(count)[None, :] <= jnp.arange(count)[:, None]
    ends = jnp.sum(jnp.where(tri, lengths[None, :], 0), axis=1)
    starts = ends - lengths
    base = (block - 1) * block_rows
    ext_ends, ext_starts = ends - base, starts - base
    passed = ext_ends[None, :] <= spot[:, None]
    row_begin = jnp.max(jnp.where(passed, ext_ends[None, :], -base), axis=1)
    row_end = jnp.min(jnp.where(passed, jnp.int32(1 << 30), ext_ends[None, :]), axis=1)
    lane = jnp.arange(128)[None, :]
    ranges = jnp.where(lane == 0, row_begin[:, None], row_end[:, None])
    row_ranges = jnp.where(jnp.arange(8)[:, None] == 0, row_begin[None, :], row_end[None, :])
    tq = min(128, rows)
    tk = 256
    lo = jnp.min(row_begin.reshape(-1, tq), axis=1) // tk
    hi = (jnp.max(row_end.reshape(-1, tq), axis=1) + tk - 1) // tk
    lo = jnp.maximum(lo, 0)
    hi = jnp.minimum(hi, 3 * block_rows // tk)

    inside = (ext_starts < 2 * block_rows) & (ext_ends > block_rows)
    number = jnp.arange(count)
    key = jnp.where(inside, mem_index * count + number, blocks * count * 2 + number)
    slot = jnp.sum((key[None, :] < key[:, None]).astype(jnp.int32), axis=1)
    stacked = jnp.stack(groups)
    first = jnp.sum((stacked[None] + block_rows < ext_starts[:, None, None]).astype(jnp.int32), axis=2)
    final = jnp.sum((stacked[None] + block_rows < ext_ends[:, None, None]).astype(jnp.int32), axis=2)
    columns = jnp.concatenate(
        [mem_index[:, None], jnp.stack([first, final], axis=2).reshape(count, -1)], axis=1
    )
    sorted_columns = jnp.sum(
        jnp.where((slot[None, :] == number[:, None])[:, :, None], columns[None], 0), axis=1
    )
    steps = jnp.sum(inside.astype(jnp.int32))
    live = number < steps
    final_mem = jnp.sum(jnp.where(number == steps - 1, sorted_columns[:, 0], 0))
    mem_steps = jnp.where(live, sorted_columns[:, 0], final_mem)
    mem_table = jnp.concatenate([mem_steps, steps[None]])
    memories = jnp.arange(blocks)
    ahead = 0
    for dim, coordinate in (
        ("c", lambda m: m % grid.core),
        ("x", lambda m: m // grid.core % grid.size["x"]),
        ("z", lambda m: m // (grid.core * grid.size["x"])),
    ):
        ahead = ahead * grid.size[dim] + (coordinate(memories) - grid.at[dim]) % grid.size[dim]
    used = jnp.any(inside[:, None] & (mem_index[:, None] == memories[None, :]), axis=0)
    spot_table = jnp.where(used, ahead + 1, -(ahead + 1)).astype(jnp.int32)
    row_table = jnp.where(live[:, None], sorted_columns[:, 1:], 0).reshape(-1)

    bias_q, bias_v = vec[3], vec[4]
    q = ((dot_nt(x, wt_qkv[:D]) + bias_q).astype(BF) * SCALE).astype(BF)
    kv = (dot_nt(ext, wt_qkv[D:]) + jnp.concatenate([jnp.zeros((D,), F32), bias_v])).astype(BF)
    pairs = PAIRS if 3 * block_rows <= 4096 else 1
    att, lse = self_forward(q, kv, ranges, lo, hi, tq, tk, pairs)
    z1, cq = first_rows(x, att, wt_so, wt_cqkv[:D], vec)

    queries = [cq] + grid.others(cq, "y")
    wt_ckv = wt_cqkv[D:]
    bias_kv = jnp.concatenate([jnp.zeros((D,), F32), vec[7]])[None]
    mem_kv = memory_kv(mem_table, gathered, mem_rows, wt_ckv, bias_kv)
    ctq = min(128, rows)
    outs, lses = cross_forward(mem_table, row_table, mem_kv, queries, ctq)
    late = gathered[:, mem_rows:].reshape(grid.count, -1, D)
    late_rows = np.cumsum([0, w_in.shape[0]] + [n_out] * chunks)
    wt_in, *wt_out = (
        late[:, i:j].reshape(-1, D) for i, j in zip(late_rows[:-1], late_rows[1:])
    )
    w2 = jnp.stack(wt_out)
    own_outs = [outs[0]] + [grid.shift(outs[k], y=-k) for k in range(1, heads)]
    own_lses = [lses[0]] + [grid.shift(lses[k], y=-k) for k in range(1, heads)]

    spots = grid.spots("cxyz")
    send = grid.count - grid.count // grid.core

    def over_cores(packed, sent):
        shape = (grid.core, grid.size["x"] * grid.size["y"], grid.size["z"], -1, D)
        own = packed.reshape(shape)[0]
        if grid.core == 1:
            return [own]
        return [own, grid.shift(sent.reshape(shape[1:]), c=1)]

    y, dz2, dcatt, stat, packed_1, sent_1 = middle_rows(
        spots, z1, cot, own_outs, own_lses, wt_co, wt_in, w2, vec, hidden_bias, max(send, 1)
    )
    upstream = [dcatt] + grid.others(dcatt, "y")
    stats = [stat] + grid.others(stat, "y")
    (upstream, stats), terms_1 = beside((upstream, stats), over_cores(packed_1, sent_1))
    sum_1 = add(terms_1)
    terms_1 = grid.ahead(sum_1, "xy")
    outputs = cross_backward(
        mem_table,
        spot_table,
        row_table,
        mem_kv,
        gathered,
        wt_ckv,
        queries,
        after(upstream, sum_1),
        stats,
        ctq,
        grid.core,
    )
    outputs, terms_1 = beside(outputs, terms_1)
    keep_m, send_m, g_ckv, g_bv, *dcqs = outputs
    own_dcqs = [dcqs[0]] + [grid.shift(dcqs[k], y=-k) for k in range(1, heads)]
    terms_m = [keep_m] if grid.core == 1 else [keep_m, grid.shift(send_m, c=1)]
    terms_1 = grid.ahead(add(terms_1), "z")
    outputs = last_rows(z1, dz2, att, own_dcqs, wt_cqkv[:D], wt_so, vec)
    outputs, (terms_m, terms_1) = beside(outputs, (terms_m, terms_1))
    dz1, datt, delta, g_so, g_cq, gvec1 = outputs
    delta = jnp.pad(delta.reshape(PAIRS, 2, rows), ((0, 0), (0, 6), (0, 0)))
    terms_m = [t.reshape(grid.size["x"], grid.size["z"], mem_rows, D) for t in terms_m]
    sends_a = [add([t[k, :, :cut] for t in terms_m]) for k in range(1, grid.size["x"])]
    sends_b = [add([t[:, k, cut:] for t in terms_m]) for k in range(1, grid.size["z"])]
    terms_a = [grid.shift(a, x=k) for k, a in enumerate(sends_a, 1)]
    terms_b = [grid.shift(b, z=k) for k, b in enumerate(sends_b, 1)]
    outputs = self_backward(
        q, after(datt, *sends_a, *sends_b), kv, row_ranges, lse, delta, lo, hi, tq, tk, pairs
    )
    outputs, (terms_a, terms_b) = beside(outputs, (terms_a, terms_b))
    sum_a = add([t[0, :, :cut] for t in terms_m] + terms_a)
    sum_b = add([t[:, 0, cut:] for t in terms_m] + terms_b)
    dq, dk, dv = after(list(outputs), sum_a, sum_b)
    terms_a, terms_b = grid.ahead(sum_a, "z"), grid.ahead(sum_b, "x")

    outputs, terms_b = beside(token_grads(dq, dk, dv, wt_qkv), terms_b)
    dxq, back_before, back_here, back_behind = outputs
    from_next = lax.ppermute(back_before, BOTH, down)
    from_prior = lax.ppermute(back_behind, BOTH, up)
    packed_2 = weight_grads(
        spots,
        after(dq, back_here, *terms_b),
        dk,
        dv,
        x,
        (before, stream_rows, behind),
        gvec1,
        g_bv,
        g_so,
        g_cq,
        g_ckv,
        max(send, 1),
    )
    packed_2, (terms_a, from_next, from_prior) = beside(packed_2, (terms_a, from_next, from_prior))
    shared = (
        back_here.astype(F32) + from_next.astype(F32) + from_prior.astype(F32)
    ).astype(BF)

    def dealt(k):
        picks = lax.broadcasted_iota(jnp.int32, (rows, block_rows), 1) == groups[k][:, None]
        return dot_nn(picks.astype(BF), shared)

    grad_in = dz1 + dxq
    grad_hi, grad_lo = hi_lo(grad_in)
    grad_input = dot_tn(order, grad_hi) + dot_tn(order, grad_lo) + dealt(0)
    for k in range(1, heads):
        grad_input = grad_input + grid.shift(dealt(k).astype(BF), y=-k).astype(F32)
    y_hi, y_lo = hi_lo(y)
    layer_out = dot_tn(order, y_hi) + dot_tn(order, y_lo)
    grad_memory = jnp.concatenate([add(terms_a, F32), add(terms_b, F32)], axis=0)

    sum_2 = add(over_cores(*packed_2))
    sum_2 = add(grid.ahead(sum_2, "xy"))
    sum_2 = add(grid.ahead(sum_2, "z"), F32)
    sum_1 = add(terms_1, F32)
    s_in, s_co, *s_out, early = split(
        sum_1, [w_in.shape[0], n_out] + [n_out] * chunks + [sum_1.shape[0] - w_in.shape[0] - n_out * (1 + chunks)]
    )
    s_qkv, s_so, s_cq, final_rows = split(sum_2, [w_qkv.shape[0], n_out, w_cqkv.shape[0], 16])
    me = block * heads + here

    def mine(summed, first, count):
        return lax.dynamic_slice(summed, (first, me * lanes), (count, lanes))

    e, f = mine(early, 0, 6), mine(final_rows, 0, 7)
    width = ffn_bias.shape[0]
    s_bias = lax.dynamic_slice(early, (6 + me * width // D, me * width % D), (1, width))[0]
    return (
        layer_out,
        grad_input,
        grad_memory,
        s_qkv.T,
        s_so.T,
        s_cq.T,
        s_co.T,
        s_in.T,
        jnp.concatenate([s.T for s in s_out], axis=0),
        jnp.stack([f[0], e[3], e[0]]),
        jnp.stack([f[5], f[6], f[2], f[3], f[4], e[5], e[2], f[1], e[4], e[1]]),
        s_bias,
    )


def solution(mesh):
    rows = P(BOTH, None)
    cols = P(None, BOTH)
    return jax.shard_map(
        body,
        mesh=mesh,
        in_specs=(rows, rows, rows, P("blk"), P(), P()) + (cols,) * 8 + (P(BOTH),),
        out_specs=(rows,) * 3 + (cols,) * 8 + (P(BOTH),),
        check_vma=False,
    )
```

```python
import functools
import math

import jax
import jax.numpy as jnp
import numpy as np
from jax import lax
from jax.experimental import pallas as pl
from jax.experimental.pallas import tpu as pltpu
from jax.sharding import PartitionSpec as P

D = 512
HEADS = 8
MEM = 1024
HD = D // HEADS
PAIRS = HEADS // 2
SCALE = 1.0 / math.sqrt(HD)
EPSILON = 1e-05
GELU_SCALE = 0.7978845608028654
FILL = -1e30
FLOOR = -1e20
BOTH = ("blk", "head")
BF = jnp.bfloat16
F32 = jnp.float32
VMEM_BYTES = 60 * 1024 * 1024


def dot_nn(a, b):
    return lax.dot_general(a, b, (((1,), (0,)), ((), ())), preferred_element_type=F32)


def dot_nt(a, b):
    return lax.dot_general(a, b, (((1,), (1,)), ((), ())), preferred_element_type=F32)


def dot_tn(a, b):
    return lax.dot_general(a, b, (((0,), (0,)), ((), ())), preferred_element_type=F32)


def hi_lo(x):
    hi = x.astype(BF)
    return hi, (x - hi.astype(F32)).astype(BF)


class Grid:
    def __init__(self):
        self.blk = lax.axis_size("blk")
        self.head = lax.axis_size("head")
        self.core = 2 if self.blk % 2 == 0 else 1
        rest = self.blk // self.core
        major = 4 if rest % 4 == 0 else rest
        self.size = {"z": major, "x": rest // major, "c": self.core, "y": self.head}
        self.stride = {
            "y": 1,
            "c": self.head,
            "x": self.head * self.core,
            "z": self.head * self.core * (rest // major),
        }
        self.count = self.blk * self.head
        b = lax.axis_index("blk")
        self.at = {
            "y": lax.axis_index("head"),
            "c": b % self.core,
            "x": (b // self.core) % self.size["x"],
            "z": b // (self.core * self.size["x"]),
        }

    def shift(self, array, **steps):
        route = []
        for i in range(self.count):
            to = i
            for dim, step in steps.items():
                size, stride = self.size[dim], self.stride[dim]
                at = (i // stride) % size
                to += ((at + step) % size - at) * stride
            route.append((i, to))
        return lax.ppermute(array, BOTH, route)

    def offsets(self, dims):
        out = [{}]
        for dim in dims:
            out = [dict(o, **{dim: k}) for o in out for k in range(self.size[dim])]
        return out[1:]

    def others(self, array, dims):
        return [self.shift(array, **o) for o in self.offsets(dims)]

    def ahead(self, buffer, dims):
        return [buffer[0]] + [self.shift(buffer[k], **o) for k, o in enumerate(self.offsets(dims), 1)]

    def spots(self, order):
        device = jnp.arange(self.count)
        spot = 0
        for dim in order:
            at = device // self.stride[dim] % self.size[dim]
            spot = spot * self.size[dim] + (at - self.at[dim]) % self.size[dim]
        return spot.astype(jnp.int32)


def add(terms, dtype=BF):
    return sum(t.astype(F32) for t in terms).astype(dtype)


def beside(outputs, arrays):
    return lax.optimization_barrier((outputs, arrays))


def after(values, *first):
    return lax.optimization_barrier((values, *first))[0]


def cost(us):
    return pl.CostEstimate(flops=int(us * 1e3), transcendentals=0, bytes_accessed=0)


def along(grid, held, dims, join):
    out = []
    for array, places in held:
        arrays = [array] + grid.others(array, dims)
        tagged = [[dict(p, **o) for p in places] for o in [{}] + grid.offsets(dims)]
        if join:
            out.append((jnp.concatenate(arrays, axis=0), sum(tagged, [])))
        else:
            out += list(zip(arrays, tagged))
    return out


def place_kernel(z_size, rows, index_ref, *refs):
    arrays, outs = refs[: len(refs) - len(rows)], refs[len(refs) - len(rows) :]
    each = arrays[0].shape[0] // z_size
    i = pl.program_id(0)
    for a, array in enumerate(arrays):

        @pl.when(i // each == a)
        def _(array=array):
            for z in range(z_size):
                source = (i % each) * z_size + (index_ref[0] - z + z_size) % z_size
                start = 0
                for out, n in zip(outs, rows):
                    out[z, 0] = array[source, start : start + n, :]
                    start += n


def place(grid, held, rows):
    arrays = [a for a, _ in held]
    z_size = grid.size["z"]
    other = grid.count // z_size
    slot = []
    for _, places in held:
        for p in places[::z_size]:
            at = 0
            for dim in "xcy":
                at = at * grid.size[dim] + (grid.at[dim] - p.get(dim, 0)) % grid.size[dim]
            slot.append(at)
    index = jnp.stack([grid.at["z"]] + slot).astype(jnp.int32)
    outs = pl.pallas_call(
        functools.partial(place_kernel, z_size, rows),
        grid_spec=pltpu.PrefetchScalarGridSpec(
            num_scalar_prefetch=1,
            grid=(other,),
            in_specs=[pl.BlockSpec(a.shape, lambda i, _: (0, 0, 0)) for a in arrays],
            out_specs=[
                pl.BlockSpec((z_size, 1, n, D), lambda i, index: (0, index[i + 1], 0, 0)) for n in rows
            ],
        ),
        out_shape=[jax.ShapeDtypeStruct((z_size, other, n, D), BF) for n in rows],
        compiler_params=pltpu.CompilerParams(vmem_limit_bytes=VMEM_BYTES),
        cost_estimate=cost(5),
        name="place_weights",
    )(index, *arrays)
    return [out.reshape(grid.count * n, D) for out, n in zip(outs, rows)]


def lane_mask(rows):
    return lax.broadcasted_iota(jnp.int32, (rows, 2 * HD), 1) < HD


def two(low, x):
    zero = jnp.zeros_like(x)
    return jnp.concatenate([jnp.where(low, x, zero), jnp.where(low, zero, x)], axis=0)


def pick(low, x):
    half = x.shape[0] // 2
    return jnp.where(low, x[:half], x[half:])


def with_ones(v):
    return jnp.concatenate([v, jnp.ones_like(v)], axis=1)


def pair_cols(g):
    return slice(g * 2 * HD, (g + 1) * 2 * HD)


def self_forward_kernel(
    pairs, tq, tk, lo_ref, hi_ref, q_ref, k_ref, v_ref, range_ref, att_ref, lse_ref, score_ref, top_ref, acc_ref
):
    width = 2 * HD
    low = lane_mask(tq)
    for i in range(q_ref.shape[0] // tq):
        rows = pl.ds(i * tq, tq)
        begin = jnp.concatenate([range_ref[rows, 0:1]] * 2, axis=0)
        end = jnp.concatenate([range_ref[rows, 1:2]] * 2, axis=0)
        first = lo_ref[i]
        top_ref[...] = jnp.full_like(top_ref, FILL)
        acc_ref[...] = jnp.zeros_like(acc_ref)

        def scores(t, carry, i=i):
            keys = pl.ds(pl.multiple_of(t * tk, tk), tk)
            spot = pl.ds(pl.multiple_of((t - first) * tk, tk), tk)
            place = lax.broadcasted_iota(jnp.int32, (2 * tq, tk), 1) + t * tk
            allowed = (place >= begin) & (place < end)
            for g in range(pairs):
                s = dot_nt(two(low, q_ref[pl.ds(i * tq, tq), pair_cols(g)]), k_ref[keys, pair_cols(g)])
                s = jnp.where(allowed, s, FILL)
                score_ref[g, :, spot] = s
                peak = top_ref[g]
                for c in range(tk // width):
                    peak = jnp.maximum(peak, s[:, c * width : (c + 1) * width])
                top_ref[g] = peak
            return carry

        lax.fori_loop(first, hi_ref[i], scores, 0)
        for g in range(pairs):
            peak = jnp.max(top_ref[g], axis=1, keepdims=True)
            top_ref[g] = jnp.broadcast_to(peak, (2 * tq, width))

        def weigh(t, carry):
            keys = pl.ds(pl.multiple_of(t * tk, tk), tk)
            spot = pl.ds(pl.multiple_of((t - first) * tk, tk), tk)
            for g in range(pairs):
                p = jnp.exp(score_ref[g, :, spot] - top_ref[g, :, 0:1]).astype(BF)
                acc_ref[g] += dot_nn(p, with_ones(v_ref[keys, pair_cols(g)]))
            return carry

        lax.fori_loop(first, hi_ref[i], weigh, 0)
        for g in range(pairs):
            mass = acc_ref[g, :, width:]
            att_ref[rows, pair_cols(g)] = pick(low, acc_ref[g, :, :width] / mass).astype(BF)
            flat = (top_ref[g] + jnp.log(mass)).T
            lse_ref[g, 0:1, rows] = flat[0:1, :tq]
            lse_ref[g, 1:2, rows] = flat[0:1, tq:]


def self_forward(q, kv, ranges, lo, hi, tq, tk, pairs):
    rows, keys = q.shape[0], kv.shape[0]
    width = pairs * 2 * HD
    groups = PAIRS // pairs
    return pl.pallas_call(
        functools.partial(self_forward_kernel, pairs, tq, tk),
        grid_spec=pltpu.PrefetchScalarGridSpec(
            num_scalar_prefetch=2,
            grid=(groups,),
            in_specs=[
                pl.BlockSpec((rows, width), lambda g, *_: (0, g)),
                pl.BlockSpec((keys, width), lambda g, *_: (0, g)),
                pl.BlockSpec((keys, width), lambda g, *_: (0, groups + g)),
                pl.BlockSpec((rows, 128), lambda g, *_: (0, 0)),
            ],
            out_specs=[
                pl.BlockSpec((rows, width), lambda g, *_: (0, g)),
                pl.BlockSpec((pairs, 8, rows), lambda g, *_: (g, 0, 0)),
            ],
            scratch_shapes=[
                pltpu.VMEM((pairs, 2 * tq, keys), F32),
                pltpu.VMEM((pairs, 2 * tq, 2 * HD), F32),
                pltpu.VMEM((pairs, 2 * tq, 4 * HD), F32),
            ],
        ),
        out_shape=[
            jax.ShapeDtypeStruct((rows, D), BF),
            jax.ShapeDtypeStruct((PAIRS, 8, rows), F32),
        ],
        compiler_params=pltpu.CompilerParams(vmem_limit_bytes=VMEM_BYTES),
        cost_estimate=cost(20),
        name="self_forward",
    )(lo, hi, q, kv, kv, ranges)


def self_backward_kernel(
    pairs, tq, tk, lo_ref, hi_ref, q_ref, do_ref, k_ref, v_ref, row_ref, lse_ref, delta_ref, dq_ref, dk_ref, dv_ref,
    acc_q, acc_k, acc_v,
):
    low = lane_mask(tq)
    acc_k[...] = jnp.zeros_like(acc_k)
    acc_v[...] = jnp.zeros_like(acc_v)
    for i in range(q_ref.shape[0] // tq):
        rows = pl.ds(i * tq, tq)
        begin = jnp.concatenate([row_ref[0:1, rows]] * 2, axis=1)
        end = jnp.concatenate([row_ref[1:2, rows]] * 2, axis=1)
        acc_q[...] = jnp.zeros_like(acc_q)

        def step(t, carry, i=i):
            rows = pl.ds(i * tq, tq)
            keys = pl.ds(pl.multiple_of(t * tk, tk), tk)
            place = lax.broadcasted_iota(jnp.int32, (tk, 2 * tq), 0) + t * tk
            allowed = (place >= begin) & (place < end)
            for g in range(pairs):
                cols = pair_cols(g)
                k, v = k_ref[keys, cols], v_ref[keys, cols]
                q2, do2 = two(low, q_ref[rows, cols]), two(low, do_ref[rows, cols])
                lse = jnp.concatenate([lse_ref[g, 0:1, rows], lse_ref[g, 1:2, rows]], axis=1)
                delta = jnp.concatenate([delta_ref[g, 0:1, rows], delta_ref[g, 1:2, rows]], axis=1)
                p = jnp.exp(jnp.where(allowed, dot_nt(k, q2) - lse, FILL))
                ds = (p * (dot_nt(v, do2) - delta)).astype(BF)
                acc_v[keys, cols] += dot_nn(p.astype(BF), do2)
                acc_k[keys, cols] += dot_nn(ds, q2)
                acc_q[g] += dot_tn(ds, k)
            return carry

        lax.fori_loop(lo_ref[i], hi_ref[i], step, 0)
        for g in range(pairs):
            dq_ref[rows, pair_cols(g)] = (pick(low, acc_q[g]) * SCALE).astype(BF)
    dk_ref[...] = acc_k[...].astype(BF)
    dv_ref[...] = acc_v[...].astype(BF)


def self_backward(q, do, kv, row_range, lse, delta, lo, hi, tq, tk, pairs):
    rows, keys = q.shape[0], kv.shape[0]
    width = pairs * 2 * HD
    groups = PAIRS // pairs
    return pl.pallas_call(
        functools.partial(self_backward_kernel, pairs, tq, tk),
        grid_spec=pltpu.PrefetchScalarGridSpec(
            num_scalar_prefetch=2,
            grid=(groups,),
            in_specs=[
                pl.BlockSpec((rows, width), lambda g, *_: (0, g)),
                pl.BlockSpec((rows, width), lambda g, *_: (0, g)),
                pl.BlockSpec((keys, width), lambda g, *_: (0, g)),
                pl.BlockSpec((keys, width), lambda g, *_: (0, groups + g)),
                pl.BlockSpec((8, rows), lambda g, *_: (0, 0)),
                pl.BlockSpec((pairs, 8, rows), lambda g, *_: (g, 0, 0)),
                pl.BlockSpec((pairs, 8, rows), lambda g, *_: (g, 0, 0)),
            ],
            out_specs=[
                pl.BlockSpec((rows, width), lambda g, *_: (0, g)),
                pl.BlockSpec((keys, width), lambda g, *_: (0, g)),
                pl.BlockSpec((keys, width), lambda g, *_: (0, g)),
            ],
            scratch_shapes=[
                pltpu.VMEM((pairs, 2 * tq, 2 * HD), F32),
                pltpu.VMEM((keys, width), F32),
                pltpu.VMEM((keys, width), F32),
            ],
        ),
        out_shape=[
            jax.ShapeDtypeStruct((rows, D), BF),
            jax.ShapeDtypeStruct((keys, D), BF),
            jax.ShapeDtypeStruct((keys, D), BF),
        ],
        compiler_params=pltpu.CompilerParams(vmem_limit_bytes=VMEM_BYTES),
        cost_estimate=cost(40),
        name="self_backward",
    )(lo, hi, q, do, kv, kv, row_range, lse, delta)


def memory_kv_kernel(mem_ref, m_ref, w_ref, b_ref, kv_ref):
    j = pl.program_id(0)

    @pl.when((j == 0) | (mem_ref[j] != mem_ref[jnp.maximum(j - 1, 0)]))
    def _():
        kv_ref[0] = (dot_nt(m_ref[0], w_ref[...]) + b_ref[...]).astype(BF)


def memory_kv(mem, gathered, n, weights, bias):
    blocks = gathered.shape[0]
    by_memory = lambda j, mem: (mem[j], 0, 0)
    return pl.pallas_call(
        memory_kv_kernel,
        grid_spec=pltpu.PrefetchScalarGridSpec(
            num_scalar_prefetch=1,
            grid=(mem.shape[0] - 1,),
            in_specs=[
                pl.BlockSpec((1, n, D), by_memory),
                pl.BlockSpec((2 * D, D), lambda j, *_: (0, 0)),
                pl.BlockSpec((1, 2 * D), lambda j, *_: (0, 0)),
            ],
            out_specs=pl.BlockSpec((1, n, 2 * D), by_memory),
        ),
        out_shape=jax.ShapeDtypeStruct((blocks, n, 2 * D), BF),
        compiler_params=pltpu.CompilerParams(vmem_limit_bytes=VMEM_BYTES),
        cost_estimate=cost(6),
        name="memory_kv",
    )(mem, gathered, weights, bias)


def cross_forward_kernel(parts, tq, mem_ref, table_ref, kv_ref, *refs):
    qs, outs, lses = refs[:parts], refs[parts : 2 * parts], refs[2 * parts : 3 * parts]
    width = 2 * HD
    j = pl.program_id(0)
    low = lane_mask(tq)
    for part in range(parts):
        first_row = table_ref[j * 2 * parts + 2 * part]
        last_row = table_ref[j * 2 * parts + 2 * part + 1]

        def step(t, carry, part=part, first_row=first_row, last_row=last_row):
            offset = pl.multiple_of(t * tq, tq)
            rows = pl.ds(offset, tq)
            at = lax.broadcasted_iota(jnp.int32, (tq, width), 0) + offset
            mine = (at >= first_row) & (at < last_row)
            at_row = lax.broadcasted_iota(jnp.int32, (1, tq), 1) + offset
            mine_row = (at_row >= first_row) & (at_row < last_row)
            for g in range(PAIRS):
                cols = pair_cols(g)
                s = dot_nt(two(low, qs[part][rows, cols]), kv_ref[0, :, cols])
                peak = jnp.max(s, axis=1, keepdims=True)
                p = jnp.exp(s - peak).astype(BF)
                acc = dot_nn(p, with_ones(kv_ref[0, :, pair_cols(PAIRS + g)]))
                mass = acc[:, width:]
                new = pick(low, acc[:, :width] / mass).astype(BF)
                outs[part][rows, cols] = jnp.where(mine, new, outs[part][rows, cols])
                flat = (peak + jnp.log(mass)).T
                for i in range(2):
                    head = slice(2 * g + i, 2 * g + i + 1)
                    lses[part][head, rows] = jnp.where(
                        mine_row, flat[0:1, i * tq : (i + 1) * tq], lses[part][head, rows]
                    )
            return carry

        lax.fori_loop(first_row // tq, (last_row + tq - 1) // tq, step, 0)


def cross_forward(mem, table, kv, queries, tq):
    parts, rows, n = len(queries), queries[0].shape[0], kv.shape[1]
    whole = pl.BlockSpec((rows, D), lambda j, *_: (0, 0))
    flat = pl.BlockSpec((HEADS, rows), lambda j, *_: (0, 0))
    out = pl.pallas_call(
        functools.partial(cross_forward_kernel, parts, tq),
        grid_spec=pltpu.PrefetchScalarGridSpec(
            num_scalar_prefetch=2,
            grid=(mem.shape[0] - 1,),
            in_specs=[pl.BlockSpec((1, n, 2 * D), lambda j, mem, _: (mem[j], 0, 0))] + [whole] * parts,
            out_specs=[whole] * parts + [flat] * parts,
        ),
        out_shape=[jax.ShapeDtypeStruct((rows, D), BF)] * parts
        + [jax.ShapeDtypeStruct((HEADS, rows), F32)] * parts,
        compiler_params=pltpu.CompilerParams(vmem_limit_bytes=VMEM_BYTES),
        cost_estimate=cost(16),
        name="cross_forward",
    )(mem, table, kv, *queries)
    return out[:parts], out[parts:]


def gradient_step(tq, kv_ref, q_ref, do_ref, stat_ref, first_row, last_row, add_k, add_v, add_q):
    low = lane_mask(tq)

    def step(t, carry):
        rows = pl.ds(pl.multiple_of(t * tq, tq), tq)
        at_row = lax.broadcasted_iota(jnp.int32, (1, tq), 1) + t * tq
        mine = (at_row >= first_row) & (at_row < last_row)
        for g in range(PAIRS):
            cols = pair_cols(g)
            k, v = kv_ref[0, :, cols], kv_ref[0, :, pair_cols(PAIRS + g)]
            q2, do2 = two(low, q_ref[rows, cols]), two(low, do_ref[rows, cols])

            def stat(base, g=g):
                return [stat_ref[base + 2 * g + i : base + 2 * g + i + 1, rows] for i in range(2)]

            lse = jnp.concatenate([jnp.where(mine, x, -FILL) for x in stat(0)], axis=1)
            delta = jnp.concatenate(stat(HEADS), axis=1)
            p = jnp.exp(dot_nt(k, q2) - lse)
            ds = (p * (dot_nt(v, do2) - delta)).astype(BF)
            add_v(cols, dot_nn(p.astype(BF), do2))
            add_k(cols, dot_nn(ds, q2))
            add_q(rows, cols, pick(low, dot_tn(ds, k)))
        return carry

    lax.fori_loop(first_row // tq, (last_row + tq - 1) // tq, step, 0)


def cross_begin_kernel(tq, mem_ref, table_ref, kv_ref, q_ref, do_ref, stat_ref, dkv_ref, dq_ref, acc_q):
    j = pl.program_id(0)

    @pl.when(j == 0)
    def _():
        acc_q[...] = jnp.zeros_like(acc_q)

    @pl.when((j == 0) | (mem_ref[j] != mem_ref[jnp.maximum(j - 1, 0)]))
    def _():
        dkv_ref[...] = jnp.zeros_like(dkv_ref)

    def add_k(cols, x):
        dkv_ref[0, :, cols] += x

    def add_v(cols, x):
        dkv_ref[0, :, D + cols.start : D + cols.stop] += x

    def add_q(rows, cols, x):
        acc_q[rows, cols] += x

    gradient_step(
        tq, kv_ref, q_ref, do_ref, stat_ref, table_ref[2 * j], table_ref[2 * j + 1], add_k, add_v, add_q
    )

    @pl.when(j == pl.num_programs(0) - 1)
    def _():
        dq_ref[...] = (acc_q[...] * SCALE).astype(BF)


def cross_begin(mem, table, kv, query, upstream, stat, tq):
    rows, n, blocks = query.shape[0], kv.shape[1], kv.shape[0]
    whole = pl.BlockSpec((rows, D), lambda j, *_: (0, 0))
    by_memory = pl.BlockSpec((1, n, 2 * D), lambda j, mem, *_: (mem[j], 0, 0))
    return pl.pallas_call(
        functools.partial(cross_begin_kernel, tq),
        grid_spec=pltpu.PrefetchScalarGridSpec(
            num_scalar_prefetch=2,
            grid=(mem.shape[0] - 1,),
            in_specs=[by_memory, whole, whole, pl.BlockSpec((2 * HEADS, rows), lambda j, *_: (0, 0))],
            out_specs=[by_memory, whole],
            scratch_shapes=[pltpu.VMEM((rows, D), F32)],
        ),
        out_shape=[jax.ShapeDtypeStruct((blocks, n, 2 * D), F32), jax.ShapeDtypeStruct((rows, D), BF)],
        compiler_params=pltpu.CompilerParams(vmem_limit_bytes=VMEM_BYTES),
        cost_estimate=cost(16),
        name="cross_begin",
    )(mem, table, kv, query, upstream, stat)


def cross_backward_kernel(parts, tq, blocks, mem_ref, spot_ref, table_ref, kv_ref, m_ref, w_ref, begun_ref, *refs):
    qs, dos, stats = refs[:parts], refs[parts : 2 * parts], refs[2 * parts : 3 * parts]
    keep_ref, send_ref, gw_ref, gb_ref = refs[3 * parts : 3 * parts + 4]
    dqs = refs[3 * parts + 4 : 4 * parts + 4]
    acc, acc_q, stage, zero, stage_sem, zero_sem = refs[4 * parts + 4 :]
    j = pl.program_id(0)
    last = mem_ref.shape[0] - 2
    steps = mem_ref[last + 1]
    now = mem_ref[j]
    previous = mem_ref[jnp.maximum(j - 1, 0)]
    following = mem_ref[jnp.minimum(j + 1, last)]
    half = keep_ref.shape[0]

    def to_target(source, spot, sem, wanted, act):
        for target, mine in ((keep_ref, spot < half), (send_ref, spot >= half)):
            copy = pltpu.make_async_copy(source, target.at[spot % half], sem)
            pl.when(wanted & mine)(functools.partial(act, copy))

    start, wait = (lambda copy: copy.start()), (lambda copy: copy.wait())

    def zeros(act):
        for m in range(blocks):
            spot = spot_ref[m]
            to_target(zero, jnp.abs(spot) - 1, zero_sem.at[m], spot < 0, act)

    @pl.when(j == 0)
    def _():
        acc_q[...] = jnp.zeros_like(acc_q)
        gw_ref[...] = jnp.zeros_like(gw_ref)
        gb_ref[...] = jnp.zeros_like(gb_ref)
        zero[...] = jnp.zeros_like(zero)
        zeros(start)

    @pl.when((j == 0) | (now != previous))
    def _():
        acc[...] = begun_ref[0]

    def add_k(cols, x):
        acc[:, cols] += x

    def add_v(cols, x):
        acc[:, D + cols.start : D + cols.stop] += x

    for part in range(parts):

        def add_q(rows, cols, x, part=part):
            acc_q[part, rows, cols] += x

        at = j * 2 * parts + 2 * part
        gradient_step(
            tq, kv_ref, qs[part], dos[part], stats[part], table_ref[at], table_ref[at + 1], add_k, add_v, add_q
        )

    @pl.when((j == steps - 1) | ((j < steps) & (now != following)))
    def _():
        dk, dv = acc[:, :D].astype(BF), acc[:, D:].astype(BF)
        spot = spot_ref[now] - 1
        stage[...] = (dot_nn(dk, w_ref[0:D, :]) + dot_nn(dv, w_ref[D : 2 * D, :])).astype(BF)
        to_target(stage, spot, stage_sem, spot >= 0, start)
        gw_ref[0:D, :] += dot_tn(dk, m_ref[0])
        gw_ref[D : 2 * D, :] += dot_tn(dv, m_ref[0])
        gb_ref[0:1, :] += jnp.sum(dv.astype(F32), axis=0, keepdims=True)
        to_target(stage, spot, stage_sem, spot >= 0, wait)

    @pl.when(j == steps - 1)
    def _():
        for part in range(parts):
            dqs[part][...] = (acc_q[part] * SCALE).astype(BF)
        zeros(wait)


def cross_backward(mem, spot, table, kv, gathered, weights, begun, queries, upstream, stats, tq, cores):
    parts, rows, n = len(queries), queries[0].shape[0], kv.shape[1]
    blocks = kv.shape[0]
    whole = pl.BlockSpec((rows, D), lambda j, *_: (0, 0))
    flat = pl.BlockSpec((2 * HEADS, rows), lambda j, *_: (0, 0))
    by_memory = lambda j, mem, *_: (mem[j], 0, 0)
    anywhere = pl.BlockSpec(memory_space=pl.ANY)
    return pl.pallas_call(
        functools.partial(cross_backward_kernel, parts, tq, blocks),
        grid_spec=pltpu.PrefetchScalarGridSpec(
            num_scalar_prefetch=3,
            grid=(mem.shape[0] - 1,),
            in_specs=[
                pl.BlockSpec((1, n, 2 * D), by_memory),
                pl.BlockSpec((1, n, D), by_memory),
                pl.BlockSpec((2 * D, D), lambda j, *_: (0, 0)),
                pl.BlockSpec((1, n, 2 * D), by_memory),
            ]
            + [whole] * (2 * parts)
            + [flat] * parts,
            out_specs=[
                anywhere,
                anywhere,
                pl.BlockSpec((2 * D, D), lambda j, *_: (0, 0)),
                pl.BlockSpec((8, D), lambda j, *_: (0, 0)),
            ]
            + [whole] * parts,
            scratch_shapes=[
                pltpu.VMEM((n, 2 * D), F32),
                pltpu.VMEM((parts, rows, D), F32),
                pltpu.VMEM((n, D), BF),
                pltpu.VMEM((n, D), BF),
                pltpu.SemaphoreType.DMA,
                pltpu.SemaphoreType.DMA((blocks,)),
            ],
        ),
        out_shape=[jax.ShapeDtypeStruct((blocks // cores, n, D), BF)] * 2
        + [
            jax.ShapeDtypeStruct((2 * D, D), F32),
            jax.ShapeDtypeStruct((8, D), F32),
        ]
        + [jax.ShapeDtypeStruct((rows, D), BF)] * parts,
        compiler_params=pltpu.CompilerParams(vmem_limit_bytes=VMEM_BYTES),
        cost_estimate=cost(20),
        name="cross_backward",
    )(mem, spot, table, kv, gathered, weights, begun, *queries, *upstream, *stats)


def norm(z):
    centre = z - jnp.mean(z, axis=1, keepdims=True)
    inverse = lax.rsqrt(jnp.mean(centre * centre, axis=1, keepdims=True) + EPSILON)
    return centre * inverse, inverse


def norm_back(upstream, normed, inverse, gain):
    scaled = upstream * gain
    return inverse * (
        scaled
        - jnp.mean(scaled, axis=1, keepdims=True)
        - normed * jnp.mean(scaled * normed, axis=1, keepdims=True)
    )


def total(x):
    return jnp.sum(x, axis=0, keepdims=True)


def head_rows():
    lane = lax.broadcasted_iota(jnp.int32, (HEADS, D), 1) // HD
    return (lane == lax.broadcasted_iota(jnp.int32, (HEADS, D), 0)).astype(F32).astype(BF)


def per_head(product):
    hi, lo = hi_lo(product)
    heads = head_rows()
    return dot_nt(heads, hi) + dot_nt(heads, lo)


def spread(rows):
    hi, lo = hi_lo(rows)
    heads = head_rows()
    return dot_tn(hi, heads) + dot_tn(lo, heads)


def deal(packed_ref, spot_ref, start, values):
    count = packed_ref.shape[0]
    for value in values:
        n = value.shape[0] // count
        for i in range(count):
            packed_ref[spot_ref[i], start : start + n, :] = value[i * n : (i + 1) * n]
        start += n
    return start


def to_all(packed_ref, start, rows):
    for i in range(packed_ref.shape[0]):
        packed_ref[i, start : start + rows.shape[0], :] = rows


def first_kernel(x_ref, att_ref, wo_ref, wq_ref, vec_ref, z_ref, cq_ref):
    z = x_ref[...].astype(F32) + dot_nt(att_ref[...], wo_ref[...]) + vec_ref[5:6, :]
    z_ref[...] = z
    n, _ = norm(z)
    low = (n * vec_ref[0:1, :] + vec_ref[10:11, :]).astype(BF)
    cq_ref[...] = ((dot_nt(low, wq_ref[...]) + vec_ref[6:7, :]).astype(BF) * SCALE).astype(BF)


def first_rows(x, att, wo, wq, vec):
    rows = x.shape[0]
    return pl.pallas_call(
        first_kernel,
        out_shape=[jax.ShapeDtypeStruct((rows, D), F32), jax.ShapeDtypeStruct((rows, D), BF)],
        compiler_params=pltpu.CompilerParams(vmem_limit_bytes=VMEM_BYTES),
        cost_estimate=cost(4),
        name="first_rows",
    )(x, att, wo, wq, vec)


def middle_kernel(parts, chunks, spot_ref, *refs):
    z1_ref, cot_ref = refs[:2]
    outs = refs[2 : 2 + parts]
    lses = refs[2 + parts : 2 + 2 * parts]
    wco_ref, w1_ref, w2_ref, vec_ref, fb_ref = refs[2 + 2 * parts : 7 + 2 * parts]
    y_ref, dz2_ref, dcatt_ref, stat_ref, packed_ref, send_ref, hid_ref, slope_ref, gw1_ref = refs[7 + 2 * parts :]
    vec = lambda i: vec_ref[i : i + 1, :]
    peak = lses[0][...]
    for part in range(1, parts):
        peak = jnp.maximum(peak, lses[part][...])
    mass = 0.0
    for part in range(parts):
        mass = mass + jnp.exp(lses[part][...] - peak)
    lse = peak + jnp.log(mass)
    catt32 = 0.0
    for part in range(parts):
        catt32 = catt32 + spread(jnp.exp(lses[part][...] - lse)) * outs[part][...].astype(F32)
    catt = catt32.astype(BF)
    n1, _ = norm(z1_ref[...])
    h1 = n1 * vec(0) + vec(10)
    z2 = h1 + dot_nt(catt, wco_ref[...]) + vec(8)
    n2, r2 = norm(z2)
    h2 = n2 * vec(1) + vec(11)
    h2_low = h2.astype(BF)
    z3 = h2 + vec(9)
    for c in range(chunks):
        cols = slice(c * D, (c + 1) * D)
        u = dot_nt(h2_low, w1_ref[cols, :]) + fb_ref[:, cols]
        square = u * u
        t = jnp.tanh(GELU_SCALE * (u + 0.044715 * u * square))
        hid = (0.5 * u * (1.0 + t)).astype(BF)
        hid_ref[:, cols] = hid
        slope_ref[:, cols] = 0.5 * (1.0 + t) + 0.5 * u * (1.0 - t * t) * (
            GELU_SCALE * (1.0 + 3.0 * 0.044715 * square)
        )
        z3 = z3 + dot_nt(hid, w2_ref[c])
    n3, r3 = norm(z3)
    y_ref[...] = n3 * vec(2) + vec(12)
    cot = cot_ref[...]
    dz3 = norm_back(cot, n3, r3, vec(2))
    df = dz3.astype(BF)
    sums = [total(cot * n3), total(cot), total(df.astype(F32))]
    hidden_sums, g_out = [], []
    e2 = dz3
    for c in range(chunks):
        cols = slice(c * D, (c + 1) * D)
        hid = hid_ref[:, cols]
        g_out.append(dot_tn(df, hid).astype(BF))
        du = (dot_nn(df, w2_ref[c]) * slope_ref[:, cols]).astype(BF)
        gw1_ref[cols, :] = dot_tn(du, h2_low).astype(BF)
        hidden_sums.append(total(du.astype(F32)))
        e2 = e2 + dot_nn(du, w1_ref[cols, :])
    dz2 = norm_back(e2, n2, r2, vec(1))
    dz2_ref[...] = dz2
    dca = dz2.astype(BF)
    sums += [total(e2 * n2), total(e2), total(dca.astype(F32))] + hidden_sums
    sums += [jnp.zeros_like(sums[0])] * (-len(sums) % 16)
    start = deal(packed_ref, spot_ref, 0, [gw1_ref[...], dot_tn(dca, catt).astype(BF)] + g_out)
    to_all(packed_ref, start, jnp.concatenate(sums, axis=0).astype(BF))
    send_ref[...] = packed_ref[packed_ref.shape[0] - send_ref.shape[0] :]
    dcatt = dot_nn(dca, wco_ref[...]).astype(BF)
    dcatt_ref[...] = dcatt
    stat_ref[0:HEADS, :] = lse
    stat_ref[HEADS : 2 * HEADS, :] = per_head(dcatt.astype(F32) * catt32)


def middle_rows(spots, z1, cot, outs, lses, wco, w1, w2, vec, fb, send):
    rows, parts, chunks = z1.shape[0], len(outs), w2.shape[0]
    hidden = chunks * D
    count = spots.shape[0]
    packed = (hidden + (1 + chunks) * D) // count + 6 + chunks + -(6 + chunks) % 16
    operands = [z1, cot, *outs, *lses, wco, w1, w2, vec, fb]
    out_shape = [
        jax.ShapeDtypeStruct((rows, D), F32),
        jax.ShapeDtypeStruct((rows, D), F32),
        jax.ShapeDtypeStruct((rows, D), BF),
        jax.ShapeDtypeStruct((2 * HEADS, rows), F32),
        jax.ShapeDtypeStruct((count, packed, D), BF),
        jax.ShapeDtypeStruct((send, packed, D), BF),
    ]
    whole = pl.BlockSpec(memory_space=pltpu.VMEM)
    return pl.pallas_call(
        functools.partial(middle_kernel, parts, chunks),
        in_specs=[pl.BlockSpec(memory_space=pltpu.SMEM)] + [whole] * len(operands),
        out_specs=[whole] * len(out_shape),
        out_shape=out_shape,
        scratch_shapes=[
            pltpu.VMEM((rows, hidden), BF),
            pltpu.VMEM((rows, hidden), F32),
            pltpu.VMEM((hidden, D), BF),
        ],
        compiler_params=pltpu.CompilerParams(vmem_limit_bytes=VMEM_BYTES),
        cost_estimate=cost(18),
        name="middle_rows",
    )(spots, *operands)


def last_kernel(parts, *refs):
    z1_ref, dz2_ref, att_ref = refs[:3]
    dcqs = refs[3 : 3 + parts]
    wq_ref, wo_ref, vec_ref = refs[3 + parts : 6 + parts]
    dz1_ref, datt_ref, delta_ref, gwo_ref, gwq_ref, gvec_ref = refs[6 + parts :]
    dcq = 0.0
    for part in dcqs:
        dcq = dcq + part[...].astype(F32)
    dcq = dcq.astype(BF)
    n1, r1 = norm(z1_ref[...])
    low = (n1 * vec_ref[0:1, :] + vec_ref[10:11, :]).astype(BF)
    e1 = dz2_ref[...] + dot_nn(dcq, wq_ref[...])
    dz1 = norm_back(e1, n1, r1, vec_ref[0:1, :])
    dz1_ref[...] = dz1
    da = dz1.astype(BF)
    datt = dot_nn(da, wo_ref[...]).astype(BF)
    datt_ref[...] = datt
    delta_ref[...] = per_head(datt.astype(F32) * att_ref[...].astype(F32))
    gwo_ref[...] = dot_tn(da, att_ref[...]).astype(BF)
    gwq_ref[...] = dot_tn(dcq, low).astype(BF)
    gvec_ref[...] = jnp.zeros_like(gvec_ref)
    gvec_ref[0:1, :] = total(e1 * n1)
    gvec_ref[1:2, :] = total(e1)
    gvec_ref[2:3, :] = total(da.astype(F32))
    gvec_ref[3:4, :] = total(dcq.astype(F32))


def last_rows(z1, dz2, att, dcqs, wq, wo, vec):
    rows = z1.shape[0]
    return pl.pallas_call(
        functools.partial(last_kernel, len(dcqs)),
        out_shape=[
            jax.ShapeDtypeStruct((rows, D), F32),
            jax.ShapeDtypeStruct((rows, D), BF),
            jax.ShapeDtypeStruct((HEADS, rows), F32),
            jax.ShapeDtypeStruct((D, D), BF),
            jax.ShapeDtypeStruct((D, D), BF),
            jax.ShapeDtypeStruct((8, D), F32),
        ],
        compiler_params=pltpu.CompilerParams(vmem_limit_bytes=VMEM_BYTES),
        cost_estimate=cost(6),
        name="last_rows",
    )(z1, dz2, att, *dcqs, wq, wo, vec)


def third(steps, part):
    return lambda j: (jnp.clip(j - part * steps, 0, steps - 1), 0)


def token_grads_kernel(dq_ref, dk_ref, dv_ref, w_ref, dx_ref, *backs):
    j = pl.program_id(0)

    @pl.when(j == 0)
    def _():
        dx_ref[...] = dot_nn(dq_ref[...], w_ref[0:D, :])

    back = (dot_nn(dk_ref[...], w_ref[D : 2 * D, :]) + dot_nn(dv_ref[...], w_ref[2 * D : 3 * D, :])).astype(BF)
    for part, back_ref in enumerate(backs):

        @pl.when(j // (pl.num_programs(0) // 3) == part)
        def _(back_ref=back_ref):
            back_ref[...] = back


def token_grads(dq, dk, dv, w):
    rows, keys = dq.shape[0], dk.shape[0]
    tile = 512
    steps = keys // tile // 3
    fixed = lambda shape: pl.BlockSpec(shape, lambda j: (0, 0))
    moving = pl.BlockSpec((tile, D), lambda j: (j, 0))
    return pl.pallas_call(
        token_grads_kernel,
        grid=(3 * steps,),
        in_specs=[fixed((rows, D)), moving, moving, fixed((3 * D, D))],
        out_specs=[fixed((rows, D))] + [pl.BlockSpec((tile, D), third(steps, part)) for part in range(3)],
        out_shape=[jax.ShapeDtypeStruct((rows, D), F32)] + [jax.ShapeDtypeStruct((keys // 3, D), BF)] * 3,
        compiler_params=pltpu.CompilerParams(vmem_limit_bytes=VMEM_BYTES),
        cost_estimate=cost(6),
        name="token_grads",
    )(dq, dk, dv, w)


def weight_grads_kernel(
    spot_ref, dq_ref, dk_ref, dv_ref, x_ref, before_ref, here_ref, behind_ref, a_ref, b_ref, so_ref, cq_ref, ckv_ref,
    packed_ref, send_ref, acc, sum_v,
):
    j = pl.program_id(0)
    part = j // (pl.num_programs(0) // 3)

    @pl.when(j == 0)
    def _():
        acc[...] = jnp.zeros_like(acc)
        acc[0:D, :] = dot_tn(dq_ref[...], x_ref[...])
        sum_v[...] = jnp.zeros_like(sum_v)

    dk, dv = dk_ref[...], dv_ref[...]
    for i, ext_ref in enumerate((before_ref, here_ref, behind_ref)):

        @pl.when(part == i)
        def _(ext_ref=ext_ref):
            acc[D : 2 * D, :] += dot_tn(dk, ext_ref[...])
            acc[2 * D : 3 * D, :] += dot_tn(dv, ext_ref[...])

    sum_v[0:1, :] += total(dv.astype(F32))

    @pl.when(j == pl.num_programs(0) - 1)
    def _():
        sum_q = total(dq_ref[...].astype(F32))
        sums = jnp.concatenate([a_ref[0:4, :], b_ref[0:1, :], sum_q, sum_v[0:1, :], a_ref[0:1, :]], axis=0)
        cross = jnp.concatenate([cq_ref[...], ckv_ref[...].astype(BF)], axis=0)
        start = deal(packed_ref, spot_ref, 0, [acc[...].astype(BF), so_ref[...], cross])
        to_all(packed_ref, start, jnp.concatenate([sums, sums], axis=0).astype(BF))
        send_ref[...] = packed_ref[packed_ref.shape[0] - send_ref.shape[0] :]


def weight_grads(spots, dq, dk, dv, x, exts, a, b, g_so, g_cq, g_ckv, send):
    rows, keys = x.shape[0], dk.shape[0]
    tile = 512
    steps = keys // tile // 3
    count = spots.shape[0]
    packed = 7 * D // count + 16
    fixed = lambda shape: pl.BlockSpec(shape, lambda j: (0,) * len(shape))
    moving = pl.BlockSpec((tile, D), lambda j: (j, 0))
    return pl.pallas_call(
        weight_grads_kernel,
        grid=(3 * steps,),
        in_specs=[pl.BlockSpec(memory_space=pltpu.SMEM), fixed((rows, D)), moving, moving, fixed((rows, D))]
        + [pl.BlockSpec((tile, D), third(steps, part)) for part in range(3)]
        + [fixed((8, D)), fixed((8, D)), fixed((D, D)), fixed((D, D)), fixed((2 * D, D))],
        out_specs=[fixed((count, packed, D)), fixed((send, packed, D))],
        out_shape=[jax.ShapeDtypeStruct((n, packed, D), BF) for n in (count, send)],
        scratch_shapes=[pltpu.VMEM((3 * D, D), F32), pltpu.VMEM((8, D), F32)],
        compiler_params=pltpu.CompilerParams(vmem_limit_bytes=VMEM_BYTES),
        cost_estimate=cost(9),
        name="weight_grads",
    )(spots, dq, dk, dv, x, *exts, a, b, g_so, g_cq, g_ckv)


def split(summed, rows):
    pieces, start = [], 0
    for n in rows:
        pieces.append(summed[start : start + n])
        start += n
    return pieces


def one_hot(targets, count):
    return (lax.broadcasted_iota(jnp.int32, (count, targets.shape[0]), 0) == targets[None, :]).astype(BF)


def body(
    tokens,
    memory,
    cotangent,
    deal_order,
    lengths,
    mem_index,
    self_qkv,
    self_out,
    cross_qkv,
    cross_out,
    ffn_in,
    ffn_out,
    norm_gains,
    biases,
    ffn_bias,
):
    grid = Grid()
    heads, blocks = grid.head, grid.blk
    rows = tokens.shape[0]
    block_rows = rows * heads
    mem_rows = memory.shape[0]
    assert mem_rows * heads == MEM
    block = lax.axis_index("blk")
    here = lax.axis_index("head")
    chunks = ffn_out.shape[0] // D

    w_qkv, w_so, w_cqkv, w_co, w_in = (
        w.T for w in (self_qkv, self_out, cross_qkv, cross_out, ffn_in)
    )
    w_out = jnp.transpose(ffn_out.reshape(chunks, D, -1), (0, 2, 1)).reshape(-1, D)
    n_out = w_so.shape[0]
    lanes = norm_gains.shape[1]
    small = jnp.concatenate([norm_gains.reshape(-1), biases.reshape(-1), ffn_bias])
    small = jnp.pad(small[None], ((0, 15), (0, D - small.shape[0])))

    near = [tokens] + grid.others(tokens, "y")
    in_group = deal_order - block * block_rows
    groups = [lax.dynamic_slice_in_dim(in_group, ((here - k) % heads) * rows, rows) for k in range(heads)]
    stream_rows = dot_nn(one_hot(jnp.concatenate(groups), block_rows), jnp.concatenate(near, axis=0)).astype(BF)
    up = [(i, i + heads) for i in range(grid.count - heads)]
    down = [(j, i) for i, j in up]
    before = lax.ppermute(stream_rows, BOTH, up)
    behind = lax.ppermute(stream_rows, BOTH, down)
    ext = jnp.concatenate([before, stream_rows, behind], axis=0)

    urgent = jnp.concatenate([w_qkv, small, w_so, w_cqkv, w_co], axis=0)
    urgent_z = along(grid, [(urgent[None], [{}])], "z", True)
    urgent_xy = along(grid, urgent_z, "xy", False)
    moved, stream_rows = beside([m for m, _ in urgent_xy], stream_rows)
    urgent_xy = [(m, p) for m, (_, p) in zip(moved, urgent_xy)]
    held = along(grid, urgent_xy, "c", False)
    wt_qkv, wt_small, wt_so, wt_cqkv, wt_co = place(
        grid, held, [w_qkv.shape[0], 16, n_out, w_cqkv.shape[0], n_out]
    )

    late = jnp.concatenate([w_in, w_out], axis=0)
    late = [late] + grid.others(late, "y")
    late = [late[-k % heads] for k in range(heads)] * 2
    late = lax.dynamic_slice_in_dim(
        jnp.concatenate(late, axis=0), (-here) % heads * late[0].shape[0], heads * late[0].shape[0]
    )
    gathered = lax.all_gather(jnp.concatenate([memory, late], axis=0), "blk", axis=0, tiled=True)
    gathered = gathered.reshape(blocks, -1, D)
    cut = mem_rows * 5 // 8
    smalls = wt_small.reshape(grid.count, 16, D)[:, 0, : 13 * lanes + ffn_bias.shape[0]].astype(F32)
    vec = jnp.transpose(smalls[:, : 13 * lanes].reshape(grid.count, 13, lanes), (1, 0, 2)).reshape(13, D)
    vec = jnp.pad(vec, ((0, 3), (0, 0)))
    hidden_bias = smalls[:, 13 * lanes :].reshape(1, -1)

    place_own = groups[0]
    rank = jnp.sum((place_own[None, :] < place_own[:, None]).astype(jnp.int32), axis=1)
    order = one_hot(rank, rows)
    x = dot_nn(order, tokens).astype(BF)
    cot_hi, cot_lo = hi_lo(cotangent)
    cot = dot_nn(order, cot_hi) + dot_nn(order, cot_lo)
    spot = jnp.sum(jnp.where(rank[None, :] == jnp.arange(rows)[:, None], place_own[None, :], 0), axis=1)
    spot = spot + block_rows
    count = lengths.shape[0]
    tri = jnp.arange(count)[None, :] <= jnp.arange(count)[:, None]
    ends = jnp.sum(jnp.where(tri, lengths[None, :], 0), axis=1)
    starts = ends - lengths
    base = (block - 1) * block_rows
    ext_ends, ext_starts = ends - base, starts - base
    passed = ext_ends[None, :] <= spot[:, None]
    row_begin = jnp.max(jnp.where(passed, ext_ends[None, :], -base), axis=1)
    row_end = jnp.min(jnp.where(passed, jnp.int32(1 << 30), ext_ends[None, :]), axis=1)
    lane = jnp.arange(128)[None, :]
    ranges = jnp.where(lane == 0, row_begin[:, None], row_end[:, None])
    row_ranges = jnp.where(jnp.arange(8)[:, None] == 0, row_begin[None, :], row_end[None, :])
    tq = min(128, rows)
    tk = 256
    lo = jnp.min(row_begin.reshape(-1, tq), axis=1) // tk
    hi = (jnp.max(row_end.reshape(-1, tq), axis=1) + tk - 1) // tk
    lo = jnp.maximum(lo, 0)
    hi = jnp.minimum(hi, 3 * block_rows // tk)

    inside = (ext_starts < 2 * block_rows) & (ext_ends > block_rows)
    number = jnp.arange(count)
    key = jnp.where(inside, mem_index * count + number, blocks * count * 2 + number)
    slot = jnp.sum((key[None, :] < key[:, None]).astype(jnp.int32), axis=1)
    stacked = jnp.stack(groups)
    first = jnp.sum((stacked[None] + block_rows < ext_starts[:, None, None]).astype(jnp.int32), axis=2)
    final = jnp.sum((stacked[None] + block_rows < ext_ends[:, None, None]).astype(jnp.int32), axis=2)
    columns = jnp.concatenate(
        [mem_index[:, None], jnp.stack([first, final], axis=2).reshape(count, -1)], axis=1
    )
    sorted_columns = jnp.sum(
        jnp.where((slot[None, :] == number[:, None])[:, :, None], columns[None], 0), axis=1
    )
    steps = jnp.sum(inside.astype(jnp.int32))
    live = number < steps
    final_mem = jnp.sum(jnp.where(number == steps - 1, sorted_columns[:, 0], 0))
    mem_steps = jnp.where(live, sorted_columns[:, 0], final_mem)
    mem_table = jnp.concatenate([mem_steps, steps[None]])
    memories = jnp.arange(blocks)
    ahead = 0
    for dim, coordinate in (
        ("c", lambda m: m % grid.core),
        ("x", lambda m: m // grid.core % grid.size["x"]),
        ("z", lambda m: m // (grid.core * grid.size["x"])),
    ):
        ahead = ahead * grid.size[dim] + (coordinate(memories) - grid.at[dim]) % grid.size[dim]
    used = jnp.any(inside[:, None] & (mem_index[:, None] == memories[None, :]), axis=0)
    spot_table = jnp.where(used, ahead + 1, -(ahead + 1)).astype(jnp.int32)
    row_table = jnp.where(live[:, None], sorted_columns[:, 1:], 0)
    own_table, other_table = row_table[:, :2].reshape(-1), row_table[:, 2:].reshape(-1)

    bias_q, bias_v = vec[3], vec[4]
    q = ((dot_nt(x, wt_qkv[:D]) + bias_q).astype(BF) * SCALE).astype(BF)
    kv = (dot_nt(ext, wt_qkv[D:]) + jnp.concatenate([jnp.zeros((D,), F32), bias_v])).astype(BF)
    pairs = PAIRS if 3 * block_rows <= 4096 else 1
    att, lse = self_forward(q, kv, ranges, lo, hi, tq, tk, pairs)
    z1, cq = first_rows(x, att, wt_so, wt_cqkv[:D], vec)

    queries = [cq] + grid.others(cq, "y")
    wt_ckv = wt_cqkv[D:]
    bias_kv = jnp.concatenate([jnp.zeros((D,), F32), vec[7]])[None]
    mem_kv = memory_kv(mem_table, gathered, mem_rows, wt_ckv, bias_kv)
    ctq = min(128, rows)
    outs, lses = cross_forward(mem_table, row_table.reshape(-1), mem_kv, queries, ctq)
    own_outs = [outs[0]] + [grid.shift(outs[k], y=-k) for k in range(1, heads)]
    own_lses = [lses[0]] + [grid.shift(lses[k], y=-k) for k in range(1, heads)]
    late = gathered[:, mem_rows:].reshape(grid.count, -1, D)
    late_rows = np.cumsum([0, w_in.shape[0]] + [n_out] * chunks)
    wt_in, *wt_out = (
        late[:, i:j].reshape(-1, D) for i, j in zip(late_rows[:-1], late_rows[1:])
    )
    w2 = jnp.stack(wt_out)
    spots = grid.spots("cxyz")
    send = grid.count - grid.count // grid.core

    def over_cores(packed, sent):
        shape = (grid.core, grid.size["x"] * grid.size["y"], grid.size["z"], -1, D)
        own = packed.reshape(shape)[0]
        if grid.core == 1:
            return [own]
        return [own, grid.shift(sent.reshape(shape[1:]), c=1)]

    y, dz2, dcatt, stat, packed_1, sent_1 = middle_rows(
        spots, z1, cot, own_outs, own_lses, wt_co, wt_in, w2, vec, hidden_bias, max(send, 1)
    )
    upstream = grid.others(dcatt, "y")
    stats = grid.others(stat, "y")
    terms_1 = over_cores(packed_1, sent_1)
    begun = cross_begin(mem_table, own_table, mem_kv, queries[0], dcatt, stat, ctq)
    (begun, own_dcq), (upstream, stats, terms_1) = beside(begun, (upstream, stats, terms_1))
    sum_1 = add(terms_1)
    terms_1 = grid.ahead(sum_1, "xy")
    outputs = cross_backward(
        mem_table,
        spot_table,
        other_table,
        mem_kv,
        gathered,
        wt_ckv,
        begun,
        queries[1:],
        after(upstream, sum_1),
        stats,
        ctq,
        grid.core,
    )
    outputs, terms_1 = beside(outputs, terms_1)
    keep_m, send_m, g_ckv, g_bv, *dcqs = outputs
    own_dcqs = [own_dcq] + [grid.shift(x, y=-k) for k, x in enumerate(dcqs, 1)]
    terms_m = [keep_m] if grid.core == 1 else [keep_m, grid.shift(send_m, c=1)]
    terms_1 = grid.ahead(add(terms_1), "z")
    outputs = last_rows(z1, dz2, att, own_dcqs, wt_cqkv[:D], wt_so, vec)
    outputs, (terms_m, terms_1) = beside(outputs, (terms_m, terms_1))
    dz1, datt, delta, g_so, g_cq, gvec1 = outputs
    delta = jnp.pad(delta.reshape(PAIRS, 2, rows), ((0, 0), (0, 6), (0, 0)))
    terms_m = [t.reshape(grid.size["x"], grid.size["z"], mem_rows, D) for t in terms_m]
    sends_a = [add([t[k, :, :cut] for t in terms_m]) for k in range(1, grid.size["x"])]
    sends_b = [add([t[:, k, cut:] for t in terms_m]) for k in range(1, grid.size["z"])]
    terms_a = [grid.shift(a, x=k) for k, a in enumerate(sends_a, 1)]
    terms_b = [grid.shift(b, z=k) for k, b in enumerate(sends_b, 1)]
    outputs = self_backward(
        q, after(datt, *sends_a, *sends_b), kv, row_ranges, lse, delta, lo, hi, tq, tk, pairs
    )
    outputs, (terms_a, terms_b) = beside(outputs, (terms_a, terms_b))
    sum_a = add([t[0, :, :cut] for t in terms_m] + terms_a)
    sum_b = add([t[:, 0, cut:] for t in terms_m] + terms_b)
    dq, dk, dv = after(list(outputs), sum_a, sum_b)
    terms_a, terms_b = grid.ahead(sum_a, "z"), grid.ahead(sum_b, "x")

    outputs, terms_b = beside(token_grads(dq, dk, dv, wt_qkv), terms_b)
    dxq, back_before, back_here, back_behind = outputs
    from_next = lax.ppermute(back_before, BOTH, down)
    from_prior = lax.ppermute(back_behind, BOTH, up)
    packed_2 = weight_grads(
        spots,
        after(dq, back_here, *terms_b),
        dk,
        dv,
        x,
        (before, stream_rows, behind),
        gvec1,
        g_bv,
        g_so,
        g_cq,
        g_ckv,
        max(send, 1),
    )
    packed_2, (terms_a, from_next, from_prior) = beside(packed_2, (terms_a, from_next, from_prior))
    shared = (
        back_here.astype(F32) + from_next.astype(F32) + from_prior.astype(F32)
    ).astype(BF)

    def dealt(k):
        picks = lax.broadcasted_iota(jnp.int32, (rows, block_rows), 1) == groups[k][:, None]
        return dot_nn(picks.astype(BF), shared)

    grad_in = dz1 + dxq
    grad_hi, grad_lo = hi_lo(grad_in)
    grad_input = dot_tn(order, grad_hi) + dot_tn(order, grad_lo) + dealt(0)
    for k in range(1, heads):
        grad_input = grad_input + grid.shift(dealt(k).astype(BF), y=-k).astype(F32)
    y_hi, y_lo = hi_lo(y)
    layer_out = dot_tn(order, y_hi) + dot_tn(order, y_lo)
    grad_memory = jnp.concatenate([add(terms_a, F32), add(terms_b, F32)], axis=0)

    sum_2 = add(over_cores(*packed_2))
    sum_2 = add(grid.ahead(sum_2, "xy"))
    sum_2 = add(grid.ahead(sum_2, "z"), F32)
    sum_1 = add(terms_1, F32)
    s_in, s_co, *s_out, early = split(
        sum_1, [w_in.shape[0], n_out] + [n_out] * chunks + [sum_1.shape[0] - w_in.shape[0] - n_out * (1 + chunks)]
    )
    s_qkv, s_so, s_cq, final_rows = split(sum_2, [w_qkv.shape[0], n_out, w_cqkv.shape[0], 16])
    me = block * heads + here

    def mine(summed, first, count):
        return lax.dynamic_slice(summed, (first, me * lanes), (count, lanes))

    e, f = mine(early, 0, 6), mine(final_rows, 0, 7)
    width = ffn_bias.shape[0]
    s_bias = lax.dynamic_slice(early, (6 + me * width // D, me * width % D), (1, width))[0]
    return (
        layer_out,
        grad_input,
        grad_memory,
        s_qkv.T,
        s_so.T,
        s_cq.T,
        s_co.T,
        s_in.T,
        jnp.concatenate([s.T for s in s_out], axis=0),
        jnp.stack([f[0], e[3], e[0]]),
        jnp.stack([f[5], f[6], f[2], f[3], f[4], e[5], e[2], f[1], e[4], e[1]]),
        s_bias,
    )


def solution(mesh):
    rows = P(BOTH, None)
    cols = P(None, BOTH)
    return jax.shard_map(
        body,
        mesh=mesh,
        in_specs=(rows, rows, rows, P("blk"), P(), P()) + (cols,) * 8 + (P(BOTH),),
        out_specs=(rows,) * 3 + (cols,) * 8 + (P(BOTH),),
        check_vma=False,
    )
```

```python
import functools
import math

import jax
import jax.numpy as jnp
import numpy as np
from jax import lax
from jax.experimental import pallas as pl
from jax.experimental.pallas import tpu as pltpu
from jax.sharding import PartitionSpec as P

D = 512
HEADS = 8
MEM = 1024
HD = D // HEADS
PAIRS = HEADS // 2
SCALE = 1.0 / math.sqrt(HD)
EPSILON = 1e-05
GELU_SCALE = 0.7978845608028654
FILL = -1e30
FLOOR = -1e20
BOTH = ("blk", "head")
BF = jnp.bfloat16
F32 = jnp.float32
VMEM_BYTES = 60 * 1024 * 1024


def dot_nn(a, b):
    return lax.dot_general(a, b, (((1,), (0,)), ((), ())), preferred_element_type=F32)


def dot_nt(a, b):
    return lax.dot_general(a, b, (((1,), (1,)), ((), ())), preferred_element_type=F32)


def dot_tn(a, b):
    return lax.dot_general(a, b, (((0,), (0,)), ((), ())), preferred_element_type=F32)


def hi_lo(x):
    hi = x.astype(BF)
    return hi, (x - hi.astype(F32)).astype(BF)


class Grid:
    def __init__(self):
        self.blk = lax.axis_size("blk")
        self.head = lax.axis_size("head")
        self.core = 2 if self.blk % 2 == 0 else 1
        rest = self.blk // self.core
        major = 4 if rest % 4 == 0 else rest
        self.size = {"z": major, "x": rest // major, "c": self.core, "y": self.head}
        self.stride = {
            "y": 1,
            "c": self.head,
            "x": self.head * self.core,
            "z": self.head * self.core * (rest // major),
        }
        self.count = self.blk * self.head
        b = lax.axis_index("blk")
        self.at = {
            "y": lax.axis_index("head"),
            "c": b % self.core,
            "x": (b // self.core) % self.size["x"],
            "z": b // (self.core * self.size["x"]),
        }

    def shift(self, array, **steps):
        route = []
        for i in range(self.count):
            to = i
            for dim, step in steps.items():
                size, stride = self.size[dim], self.stride[dim]
                at = (i // stride) % size
                to += ((at + step) % size - at) * stride
            route.append((i, to))
        return lax.ppermute(array, BOTH, route)

    def offsets(self, dims):
        out = [{}]
        for dim in dims:
            out = [dict(o, **{dim: k}) for o in out for k in range(self.size[dim])]
        return out[1:]

    def others(self, array, dims):
        return [self.shift(array, **o) for o in self.offsets(dims)]

    def ahead(self, buffer, dims):
        return [buffer[0]] + [self.shift(buffer[k], **o) for k, o in enumerate(self.offsets(dims), 1)]

    def spots(self, order):
        device = jnp.arange(self.count)
        spot = 0
        for dim in order:
            at = device // self.stride[dim] % self.size[dim]
            spot = spot * self.size[dim] + (at - self.at[dim]) % self.size[dim]
        return spot.astype(jnp.int32)


def add(terms, dtype=BF):
    return sum(t.astype(F32) for t in terms).astype(dtype)


def beside(outputs, arrays):
    return lax.optimization_barrier((outputs, arrays))


def after(values, *first):
    return lax.optimization_barrier((values, *first))[0]


def cost(us):
    return pl.CostEstimate(flops=int(us * 1e3), transcendentals=0, bytes_accessed=0)


def along(grid, held, dims, join):
    out = []
    for array, places in held:
        arrays = [array] + grid.others(array, dims)
        tagged = [[dict(p, **o) for p in places] for o in [{}] + grid.offsets(dims)]
        if join:
            out.append((jnp.concatenate(arrays, axis=0), sum(tagged, [])))
        else:
            out += list(zip(arrays, tagged))
    return out


def place_kernel(z_size, rows, index_ref, *refs):
    arrays, outs = refs[: len(refs) - len(rows)], refs[len(refs) - len(rows) :]
    each = arrays[0].shape[0] // z_size
    i = pl.program_id(0)
    for a, array in enumerate(arrays):

        @pl.when(i // each == a)
        def _(array=array):
            for z in range(z_size):
                source = (i % each) * z_size + (index_ref[0] - z + z_size) % z_size
                start = 0
                for out, n in zip(outs, rows):
                    out[z, 0] = array[source, start : start + n, :]
                    start += n


def place(grid, held, rows):
    arrays = [a for a, _ in held]
    z_size = grid.size["z"]
    other = grid.count // z_size
    slot = []
    for _, places in held:
        for p in places[::z_size]:
            at = 0
            for dim in "xcy":
                at = at * grid.size[dim] + (grid.at[dim] - p.get(dim, 0)) % grid.size[dim]
            slot.append(at)
    index = jnp.stack([grid.at["z"]] + slot).astype(jnp.int32)
    outs = pl.pallas_call(
        functools.partial(place_kernel, z_size, rows),
        grid_spec=pltpu.PrefetchScalarGridSpec(
            num_scalar_prefetch=1,
            grid=(other,),
            in_specs=[pl.BlockSpec(a.shape, lambda i, _: (0, 0, 0)) for a in arrays],
            out_specs=[
                pl.BlockSpec((z_size, 1, n, D), lambda i, index: (0, index[i + 1], 0, 0)) for n in rows
            ],
        ),
        out_shape=[jax.ShapeDtypeStruct((z_size, other, n, D), BF) for n in rows],
        compiler_params=pltpu.CompilerParams(vmem_limit_bytes=VMEM_BYTES),
        cost_estimate=cost(5),
        name="place_weights",
    )(index, *arrays)
    return [out.reshape(grid.count * n, D) for out, n in zip(outs, rows)]


def lane_mask(rows):
    return lax.broadcasted_iota(jnp.int32, (rows, 2 * HD), 1) < HD


def two(low, x):
    zero = jnp.zeros_like(x)
    return jnp.concatenate([jnp.where(low, x, zero), jnp.where(low, zero, x)], axis=0)


def pick(low, x):
    half = x.shape[0] // 2
    return jnp.where(low, x[:half], x[half:])


def with_ones(v):
    return jnp.concatenate([v, jnp.ones_like(v)], axis=1)


def pair_cols(g):
    return slice(g * 2 * HD, (g + 1) * 2 * HD)


def self_forward_kernel(
    pairs, tq, tk, lo_ref, hi_ref, q_ref, k_ref, v_ref, range_ref, att_ref, lse_ref, score_ref, top_ref, acc_ref
):
    width = 2 * HD
    low = lane_mask(tq)
    for i in range(q_ref.shape[0] // tq):
        rows = pl.ds(i * tq, tq)
        begin = jnp.concatenate([range_ref[rows, 0:1]] * 2, axis=0)
        end = jnp.concatenate([range_ref[rows, 1:2]] * 2, axis=0)
        first = lo_ref[i]
        top_ref[...] = jnp.full_like(top_ref, FILL)
        acc_ref[...] = jnp.zeros_like(acc_ref)

        def scores(t, carry, i=i):
            keys = pl.ds(pl.multiple_of(t * tk, tk), tk)
            spot = pl.ds(pl.multiple_of((t - first) * tk, tk), tk)
            place = lax.broadcasted_iota(jnp.int32, (2 * tq, tk), 1) + t * tk
            allowed = (place >= begin) & (place < end)
            for g in range(pairs):
                s = dot_nt(two(low, q_ref[pl.ds(i * tq, tq), pair_cols(g)]), k_ref[keys, pair_cols(g)])
                s = jnp.where(allowed, s, FILL)
                score_ref[g, :, spot] = s
                peak = top_ref[g]
                for c in range(tk // width):
                    peak = jnp.maximum(peak, s[:, c * width : (c + 1) * width])
                top_ref[g] = peak
            return carry

        lax.fori_loop(first, hi_ref[i], scores, 0)
        for g in range(pairs):
            peak = jnp.max(top_ref[g], axis=1, keepdims=True)
            top_ref[g] = jnp.broadcast_to(peak, (2 * tq, width))

        def weigh(t, carry):
            keys = pl.ds(pl.multiple_of(t * tk, tk), tk)
            spot = pl.ds(pl.multiple_of((t - first) * tk, tk), tk)
            for g in range(pairs):
                p = jnp.exp(score_ref[g, :, spot] - top_ref[g, :, 0:1]).astype(BF)
                acc_ref[g] += dot_nn(p, with_ones(v_ref[keys, pair_cols(g)]))
            return carry

        lax.fori_loop(first, hi_ref[i], weigh, 0)
        for g in range(pairs):
            mass = acc_ref[g, :, width:]
            att_ref[rows, pair_cols(g)] = pick(low, acc_ref[g, :, :width] / mass).astype(BF)
            flat = (top_ref[g] + jnp.log(mass)).T
            lse_ref[g, 0:1, rows] = flat[0:1, :tq]
            lse_ref[g, 1:2, rows] = flat[0:1, tq:]


def self_forward(q, kv, ranges, lo, hi, tq, tk, pairs):
    rows, keys = q.shape[0], kv.shape[0]
    width = pairs * 2 * HD
    groups = PAIRS // pairs
    return pl.pallas_call(
        functools.partial(self_forward_kernel, pairs, tq, tk),
        grid_spec=pltpu.PrefetchScalarGridSpec(
            num_scalar_prefetch=2,
            grid=(groups,),
            in_specs=[
                pl.BlockSpec((rows, width), lambda g, *_: (0, g)),
                pl.BlockSpec((keys, width), lambda g, *_: (0, g)),
                pl.BlockSpec((keys, width), lambda g, *_: (0, groups + g)),
                pl.BlockSpec((rows, 128), lambda g, *_: (0, 0)),
            ],
            out_specs=[
                pl.BlockSpec((rows, width), lambda g, *_: (0, g)),
                pl.BlockSpec((pairs, 8, rows), lambda g, *_: (g, 0, 0)),
            ],
            scratch_shapes=[
                pltpu.VMEM((pairs, 2 * tq, keys), F32),
                pltpu.VMEM((pairs, 2 * tq, 2 * HD), F32),
                pltpu.VMEM((pairs, 2 * tq, 4 * HD), F32),
            ],
        ),
        out_shape=[
            jax.ShapeDtypeStruct((rows, D), BF),
            jax.ShapeDtypeStruct((PAIRS, 8, rows), F32),
        ],
        compiler_params=pltpu.CompilerParams(vmem_limit_bytes=VMEM_BYTES),
        cost_estimate=cost(20),
        name="self_forward",
    )(lo, hi, q, kv, kv, ranges)


def self_backward_kernel(
    pairs, tq, tk, lo_ref, hi_ref, q_ref, do_ref, k_ref, v_ref, row_ref, lse_ref, delta_ref, dq_ref, dk_ref, dv_ref,
    acc_q, acc_k, acc_v,
):
    low = lane_mask(tq)
    acc_k[...] = jnp.zeros_like(acc_k)
    acc_v[...] = jnp.zeros_like(acc_v)
    for i in range(q_ref.shape[0] // tq):
        rows = pl.ds(i * tq, tq)
        begin = jnp.concatenate([row_ref[0:1, rows]] * 2, axis=1)
        end = jnp.concatenate([row_ref[1:2, rows]] * 2, axis=1)
        acc_q[...] = jnp.zeros_like(acc_q)

        def step(t, carry, i=i):
            rows = pl.ds(i * tq, tq)
            keys = pl.ds(pl.multiple_of(t * tk, tk), tk)
            place = lax.broadcasted_iota(jnp.int32, (tk, 2 * tq), 0) + t * tk
            allowed = (place >= begin) & (place < end)
            for g in range(pairs):
                cols = pair_cols(g)
                k, v = k_ref[keys, cols], v_ref[keys, cols]
                q2, do2 = two(low, q_ref[rows, cols]), two(low, do_ref[rows, cols])
                lse = jnp.concatenate([lse_ref[g, 0:1, rows], lse_ref[g, 1:2, rows]], axis=1)
                delta = jnp.concatenate([delta_ref[g, 0:1, rows], delta_ref[g, 1:2, rows]], axis=1)
                p = jnp.exp(jnp.where(allowed, dot_nt(k, q2) - lse, FILL))
                ds = (p * (dot_nt(v, do2) - delta)).astype(BF)
                acc_v[keys, cols] += dot_nn(p.astype(BF), do2)
                acc_k[keys, cols] += dot_nn(ds, q2)
                acc_q[g] += dot_tn(ds, k)
            return carry

        lax.fori_loop(lo_ref[i], hi_ref[i], step, 0)
        for g in range(pairs):
            dq_ref[rows, pair_cols(g)] = (pick(low, acc_q[g]) * SCALE).astype(BF)
    dk_ref[...] = acc_k[...].astype(BF)
    dv_ref[...] = acc_v[...].astype(BF)


def self_backward(q, do, kv, row_range, lse, delta, lo, hi, tq, tk, pairs):
    rows, keys = q.shape[0], kv.shape[0]
    width = pairs * 2 * HD
    groups = PAIRS // pairs
    return pl.pallas_call(
        functools.partial(self_backward_kernel, pairs, tq, tk),
        grid_spec=pltpu.PrefetchScalarGridSpec(
            num_scalar_prefetch=2,
            grid=(groups,),
            in_specs=[
                pl.BlockSpec((rows, width), lambda g, *_: (0, g)),
                pl.BlockSpec((rows, width), lambda g, *_: (0, g)),
                pl.BlockSpec((keys, width), lambda g, *_: (0, g)),
                pl.BlockSpec((keys, width), lambda g, *_: (0, groups + g)),
                pl.BlockSpec((8, rows), lambda g, *_: (0, 0)),
                pl.BlockSpec((pairs, 8, rows), lambda g, *_: (g, 0, 0)),
                pl.BlockSpec((pairs, 8, rows), lambda g, *_: (g, 0, 0)),
            ],
            out_specs=[
                pl.BlockSpec((rows, width), lambda g, *_: (0, g)),
                pl.BlockSpec((keys, width), lambda g, *_: (0, g)),
                pl.BlockSpec((keys, width), lambda g, *_: (0, g)),
            ],
            scratch_shapes=[
                pltpu.VMEM((pairs, 2 * tq, 2 * HD), F32),
                pltpu.VMEM((keys, width), F32),
                pltpu.VMEM((keys, width), F32),
            ],
        ),
        out_shape=[
            jax.ShapeDtypeStruct((rows, D), BF),
            jax.ShapeDtypeStruct((keys, D), BF),
            jax.ShapeDtypeStruct((keys, D), BF),
        ],
        compiler_params=pltpu.CompilerParams(vmem_limit_bytes=VMEM_BYTES),
        cost_estimate=cost(40),
        name="self_backward",
    )(lo, hi, q, do, kv, kv, row_range, lse, delta)


def memory_kv_kernel(mem_ref, m_ref, w_ref, b_ref, kv_ref):
    j = pl.program_id(0)

    @pl.when((j == 0) | (mem_ref[j] != mem_ref[jnp.maximum(j - 1, 0)]))
    def _():
        kv_ref[0] = (dot_nt(m_ref[0], w_ref[...]) + b_ref[...]).astype(BF)


def memory_kv(mem, gathered, n, weights, bias):
    blocks = gathered.shape[0]
    by_memory = lambda j, mem: (mem[j], 0, 0)
    return pl.pallas_call(
        memory_kv_kernel,
        grid_spec=pltpu.PrefetchScalarGridSpec(
            num_scalar_prefetch=1,
            grid=(mem.shape[0] - 1,),
            in_specs=[
                pl.BlockSpec((1, n, D), by_memory),
                pl.BlockSpec((2 * D, D), lambda j, *_: (0, 0)),
                pl.BlockSpec((1, 2 * D), lambda j, *_: (0, 0)),
            ],
            out_specs=pl.BlockSpec((1, n, 2 * D), by_memory),
        ),
        out_shape=jax.ShapeDtypeStruct((blocks, n, 2 * D), BF),
        compiler_params=pltpu.CompilerParams(vmem_limit_bytes=VMEM_BYTES),
        cost_estimate=cost(6),
        name="memory_kv",
    )(mem, gathered, weights, bias)


def cross_forward_kernel(parts, tq, mem_ref, table_ref, kv_ref, *refs):
    qs, outs, lses = refs[:parts], refs[parts : 2 * parts], refs[2 * parts : 3 * parts]
    width = 2 * HD
    j = pl.program_id(0)
    low = lane_mask(tq)
    for part in range(parts):
        first_row = table_ref[j * 2 * parts + 2 * part]
        last_row = table_ref[j * 2 * parts + 2 * part + 1]

        def step(t, carry, part=part, first_row=first_row, last_row=last_row):
            offset = pl.multiple_of(t * tq, tq)
            rows = pl.ds(offset, tq)
            at = lax.broadcasted_iota(jnp.int32, (tq, width), 0) + offset
            mine = (at >= first_row) & (at < last_row)
            at_row = lax.broadcasted_iota(jnp.int32, (1, tq), 1) + offset
            mine_row = (at_row >= first_row) & (at_row < last_row)
            for g in range(PAIRS):
                cols = pair_cols(g)
                s = dot_nt(two(low, qs[part][rows, cols]), kv_ref[0, :, cols])
                peak = jnp.max(s, axis=1, keepdims=True)
                p = jnp.exp(s - peak).astype(BF)
                acc = dot_nn(p, with_ones(kv_ref[0, :, pair_cols(PAIRS + g)]))
                mass = acc[:, width:]
                new = pick(low, acc[:, :width] / mass).astype(BF)
                outs[part][rows, cols] = jnp.where(mine, new, outs[part][rows, cols])
                flat = (peak + jnp.log(mass)).T
                for i in range(2):
                    head = slice(2 * g + i, 2 * g + i + 1)
                    lses[part][head, rows] = jnp.where(
                        mine_row, flat[0:1, i * tq : (i + 1) * tq], lses[part][head, rows]
                    )
            return carry

        lax.fori_loop(first_row // tq, (last_row + tq - 1) // tq, step, 0)


def cross_forward(mem, table, kv, queries, tq):
    parts, rows, n = len(queries), queries[0].shape[0], kv.shape[1]
    whole = pl.BlockSpec((rows, D), lambda j, *_: (0, 0))
    flat = pl.BlockSpec((HEADS, rows), lambda j, *_: (0, 0))
    out = pl.pallas_call(
        functools.partial(cross_forward_kernel, parts, tq),
        grid_spec=pltpu.PrefetchScalarGridSpec(
            num_scalar_prefetch=2,
            grid=(mem.shape[0] - 1,),
            in_specs=[pl.BlockSpec((1, n, 2 * D), lambda j, mem, _: (mem[j], 0, 0))] + [whole] * parts,
            out_specs=[whole] * parts + [flat] * parts,
        ),
        out_shape=[jax.ShapeDtypeStruct((rows, D), BF)] * parts
        + [jax.ShapeDtypeStruct((HEADS, rows), F32)] * parts,
        compiler_params=pltpu.CompilerParams(vmem_limit_bytes=VMEM_BYTES),
        cost_estimate=cost(16),
        name="cross_forward",
    )(mem, table, kv, *queries)
    return out[:parts], out[parts:]


def gradient_step(tq, kv_ref, q_ref, do_ref, stat_ref, first_row, last_row, add_k, add_v, add_q):
    low = lane_mask(tq)

    def step(t, carry):
        rows = pl.ds(pl.multiple_of(t * tq, tq), tq)
        at_row = lax.broadcasted_iota(jnp.int32, (1, tq), 1) + t * tq
        mine = (at_row >= first_row) & (at_row < last_row)
        for g in range(PAIRS):
            cols = pair_cols(g)
            k, v = kv_ref[0, :, cols], kv_ref[0, :, pair_cols(PAIRS + g)]
            q2, do2 = two(low, q_ref[rows, cols]), two(low, do_ref[rows, cols])

            def stat(base, g=g):
                return [stat_ref[base + 2 * g + i : base + 2 * g + i + 1, rows] for i in range(2)]

            lse = jnp.concatenate([jnp.where(mine, x, -FILL) for x in stat(0)], axis=1)
            delta = jnp.concatenate(stat(HEADS), axis=1)
            p = jnp.exp(dot_nt(k, q2) - lse)
            ds = (p * (dot_nt(v, do2) - delta)).astype(BF)
            add_v(cols, dot_nn(p.astype(BF), do2))
            add_k(cols, dot_nn(ds, q2))
            add_q(rows, cols, pick(low, dot_tn(ds, k)))
        return carry

    lax.fori_loop(first_row // tq, (last_row + tq - 1) // tq, step, 0)


def cross_begin_kernel(tq, mem_ref, table_ref, kv_ref, q_ref, do_ref, stat_ref, dkv_ref, dq_ref, acc_q):
    j = pl.program_id(0)

    @pl.when(j == 0)
    def _():
        acc_q[...] = jnp.zeros_like(acc_q)

    @pl.when((j == 0) | (mem_ref[j] != mem_ref[jnp.maximum(j - 1, 0)]))
    def _():
        dkv_ref[...] = jnp.zeros_like(dkv_ref)

    def add_k(cols, x):
        dkv_ref[0, :, cols] += x

    def add_v(cols, x):
        dkv_ref[0, :, D + cols.start : D + cols.stop] += x

    def add_q(rows, cols, x):
        acc_q[rows, cols] += x

    gradient_step(
        tq, kv_ref, q_ref, do_ref, stat_ref, table_ref[2 * j], table_ref[2 * j + 1], add_k, add_v, add_q
    )

    @pl.when(j == pl.num_programs(0) - 1)
    def _():
        dq_ref[...] = (acc_q[...] * SCALE).astype(BF)


def cross_begin(mem, table, kv, query, upstream, stat, tq):
    rows, n, blocks = query.shape[0], kv.shape[1], kv.shape[0]
    whole = pl.BlockSpec((rows, D), lambda j, *_: (0, 0))
    by_memory = pl.BlockSpec((1, n, 2 * D), lambda j, mem, *_: (mem[j], 0, 0))
    return pl.pallas_call(
        functools.partial(cross_begin_kernel, tq),
        grid_spec=pltpu.PrefetchScalarGridSpec(
            num_scalar_prefetch=2,
            grid=(mem.shape[0] - 1,),
            in_specs=[by_memory, whole, whole, pl.BlockSpec((2 * HEADS, rows), lambda j, *_: (0, 0))],
            out_specs=[by_memory, whole],
            scratch_shapes=[pltpu.VMEM((rows, D), F32)],
        ),
        out_shape=[jax.ShapeDtypeStruct((blocks, n, 2 * D), F32), jax.ShapeDtypeStruct((rows, D), BF)],
        compiler_params=pltpu.CompilerParams(vmem_limit_bytes=VMEM_BYTES),
        cost_estimate=cost(16),
        name="cross_begin",
    )(mem, table, kv, query, upstream, stat)


def cross_backward_kernel(parts, tq, blocks, mem_ref, spot_ref, table_ref, kv_ref, m_ref, w_ref, begun_ref, *refs):
    qs, dos, stats = refs[:parts], refs[parts : 2 * parts], refs[2 * parts : 3 * parts]
    keep_ref, send_ref, gw_ref, gb_ref = refs[3 * parts : 3 * parts + 4]
    dqs = refs[3 * parts + 4 : 4 * parts + 4]
    acc, acc_q, stage, zero, stage_sem, zero_sem = refs[4 * parts + 4 :]
    j = pl.program_id(0)
    last = mem_ref.shape[0] - 2
    steps = mem_ref[last + 1]
    now = mem_ref[j]
    previous = mem_ref[jnp.maximum(j - 1, 0)]
    following = mem_ref[jnp.minimum(j + 1, last)]
    half = keep_ref.shape[0]

    def to_target(source, spot, sem, wanted, act):
        for target, mine in ((keep_ref, spot < half), (send_ref, spot >= half)):
            copy = pltpu.make_async_copy(source, target.at[spot % half], sem)
            pl.when(wanted & mine)(functools.partial(act, copy))

    start, wait = (lambda copy: copy.start()), (lambda copy: copy.wait())

    def zeros(act):
        for m in range(blocks):
            spot = spot_ref[m]
            to_target(zero, jnp.abs(spot) - 1, zero_sem.at[m], spot < 0, act)

    @pl.when(j == 0)
    def _():
        acc_q[...] = jnp.zeros_like(acc_q)
        gw_ref[...] = jnp.zeros_like(gw_ref)
        gb_ref[...] = jnp.zeros_like(gb_ref)
        zero[...] = jnp.zeros_like(zero)
        zeros(start)

    @pl.when((j == 0) | (now != previous))
    def _():
        acc[...] = begun_ref[0]

    def add_k(cols, x):
        acc[:, cols] += x

    def add_v(cols, x):
        acc[:, D + cols.start : D + cols.stop] += x

    for part in range(parts):

        def add_q(rows, cols, x, part=part):
            acc_q[part, rows, cols] += x

        at = j * 2 * parts + 2 * part
        gradient_step(
            tq, kv_ref, qs[part], dos[part], stats[part], table_ref[at], table_ref[at + 1], add_k, add_v, add_q
        )

    @pl.when((j == steps - 1) | ((j < steps) & (now != following)))
    def _():
        dk, dv = acc[:, :D].astype(BF), acc[:, D:].astype(BF)
        spot = spot_ref[now] - 1
        stage[...] = (dot_nn(dk, w_ref[0:D, :]) + dot_nn(dv, w_ref[D : 2 * D, :])).astype(BF)
        to_target(stage, spot, stage_sem, spot >= 0, start)
        gw_ref[0:D, :] += dot_tn(dk, m_ref[0])
        gw_ref[D : 2 * D, :] += dot_tn(dv, m_ref[0])
        gb_ref[0:1, :] += jnp.sum(dv.astype(F32), axis=0, keepdims=True)
        to_target(stage, spot, stage_sem, spot >= 0, wait)

    @pl.when(j == steps - 1)
    def _():
        for part in range(parts):
            dqs[part][...] = (acc_q[part] * SCALE).astype(BF)
        zeros(wait)


def cross_backward(mem, spot, table, kv, gathered, weights, begun, queries, upstream, stats, tq, cores):
    parts, rows, n = len(queries), queries[0].shape[0], kv.shape[1]
    blocks = kv.shape[0]
    whole = pl.BlockSpec((rows, D), lambda j, *_: (0, 0))
    flat = pl.BlockSpec((2 * HEADS, rows), lambda j, *_: (0, 0))
    by_memory = lambda j, mem, *_: (mem[j], 0, 0)
    anywhere = pl.BlockSpec(memory_space=pl.ANY)
    return pl.pallas_call(
        functools.partial(cross_backward_kernel, parts, tq, blocks),
        grid_spec=pltpu.PrefetchScalarGridSpec(
            num_scalar_prefetch=3,
            grid=(mem.shape[0] - 1,),
            in_specs=[
                pl.BlockSpec((1, n, 2 * D), by_memory),
                pl.BlockSpec((1, n, D), by_memory),
                pl.BlockSpec((2 * D, D), lambda j, *_: (0, 0)),
                pl.BlockSpec((1, n, 2 * D), by_memory),
            ]
            + [whole] * (2 * parts)
            + [flat] * parts,
            out_specs=[
                anywhere,
                anywhere,
                pl.BlockSpec((2 * D, D), lambda j, *_: (0, 0)),
                pl.BlockSpec((8, D), lambda j, *_: (0, 0)),
            ]
            + [whole] * parts,
            scratch_shapes=[
                pltpu.VMEM((n, 2 * D), F32),
                pltpu.VMEM((parts, rows, D), F32),
                pltpu.VMEM((n, D), BF),
                pltpu.VMEM((n, D), BF),
                pltpu.SemaphoreType.DMA,
                pltpu.SemaphoreType.DMA((blocks,)),
            ],
        ),
        out_shape=[jax.ShapeDtypeStruct((blocks // cores, n, D), BF)] * 2
        + [
            jax.ShapeDtypeStruct((2 * D, D), F32),
            jax.ShapeDtypeStruct((8, D), F32),
        ]
        + [jax.ShapeDtypeStruct((rows, D), BF)] * parts,
        compiler_params=pltpu.CompilerParams(vmem_limit_bytes=VMEM_BYTES),
        cost_estimate=cost(20),
        name="cross_backward",
    )(mem, spot, table, kv, gathered, weights, begun, *queries, *upstream, *stats)


def norm(z):
    centre = z - jnp.mean(z, axis=1, keepdims=True)
    inverse = lax.rsqrt(jnp.mean(centre * centre, axis=1, keepdims=True) + EPSILON)
    return centre * inverse, inverse


def norm_back(upstream, normed, inverse, gain):
    scaled = upstream * gain
    return inverse * (
        scaled
        - jnp.mean(scaled, axis=1, keepdims=True)
        - normed * jnp.mean(scaled * normed, axis=1, keepdims=True)
    )


def total(x):
    return jnp.sum(x, axis=0, keepdims=True)


def head_rows():
    lane = lax.broadcasted_iota(jnp.int32, (HEADS, D), 1) // HD
    return (lane == lax.broadcasted_iota(jnp.int32, (HEADS, D), 0)).astype(F32).astype(BF)


def per_head(product):
    hi, lo = hi_lo(product)
    heads = head_rows()
    return dot_nt(heads, hi) + dot_nt(heads, lo)


def spread(rows):
    hi, lo = hi_lo(rows)
    heads = head_rows()
    return dot_tn(hi, heads) + dot_tn(lo, heads)


def deal(packed_ref, spot_ref, start, values):
    count = packed_ref.shape[0]
    for value in values:
        n = value.shape[0] // count
        for i in range(count):
            packed_ref[spot_ref[i], start : start + n, :] = value[i * n : (i + 1) * n]
        start += n
    return start


def to_all(packed_ref, start, rows):
    for i in range(packed_ref.shape[0]):
        packed_ref[i, start : start + rows.shape[0], :] = rows


def first_kernel(x_ref, att_ref, wo_ref, wq_ref, vec_ref, z_ref, cq_ref):
    z = x_ref[...].astype(F32) + dot_nt(att_ref[...], wo_ref[...]) + vec_ref[5:6, :]
    z_ref[...] = z
    n, _ = norm(z)
    low = (n * vec_ref[0:1, :] + vec_ref[10:11, :]).astype(BF)
    cq_ref[...] = ((dot_nt(low, wq_ref[...]) + vec_ref[6:7, :]).astype(BF) * SCALE).astype(BF)


def first_rows(x, att, wo, wq, vec):
    rows = x.shape[0]
    return pl.pallas_call(
        first_kernel,
        out_shape=[jax.ShapeDtypeStruct((rows, D), F32), jax.ShapeDtypeStruct((rows, D), BF)],
        compiler_params=pltpu.CompilerParams(vmem_limit_bytes=VMEM_BYTES),
        cost_estimate=cost(4),
        name="first_rows",
    )(x, att, wo, wq, vec)


def middle_kernel(parts, chunks, spot_ref, *refs):
    z1_ref, cot_ref = refs[:2]
    outs = refs[2 : 2 + parts]
    lses = refs[2 + parts : 2 + 2 * parts]
    wco_ref, w1_ref, w2_ref, vec_ref, fb_ref = refs[2 + 2 * parts : 7 + 2 * parts]
    y_ref, dz2_ref, dcatt_ref, stat_ref, packed_ref, send_ref, hid_ref, slope_ref, gw1_ref = refs[7 + 2 * parts :]
    vec = lambda i: vec_ref[i : i + 1, :]
    peak = lses[0][...]
    for part in range(1, parts):
        peak = jnp.maximum(peak, lses[part][...])
    mass = 0.0
    for part in range(parts):
        mass = mass + jnp.exp(lses[part][...] - peak)
    lse = peak + jnp.log(mass)
    catt32 = 0.0
    for part in range(parts):
        catt32 = catt32 + spread(jnp.exp(lses[part][...] - lse)) * outs[part][...].astype(F32)
    catt = catt32.astype(BF)
    n1, _ = norm(z1_ref[...])
    h1 = n1 * vec(0) + vec(10)
    z2 = h1 + dot_nt(catt, wco_ref[...]) + vec(8)
    n2, r2 = norm(z2)
    h2 = n2 * vec(1) + vec(11)
    h2_low = h2.astype(BF)
    z3 = h2 + vec(9)
    for c in range(chunks):
        cols = slice(c * D, (c + 1) * D)
        u = dot_nt(h2_low, w1_ref[cols, :]) + fb_ref[:, cols]
        square = u * u
        t = jnp.tanh(GELU_SCALE * (u + 0.044715 * u * square))
        hid = (0.5 * u * (1.0 + t)).astype(BF)
        hid_ref[:, cols] = hid
        slope_ref[:, cols] = 0.5 * (1.0 + t) + 0.5 * u * (1.0 - t * t) * (
            GELU_SCALE * (1.0 + 3.0 * 0.044715 * square)
        )
        z3 = z3 + dot_nt(hid, w2_ref[c])
    n3, r3 = norm(z3)
    y_ref[...] = n3 * vec(2) + vec(12)
    cot = cot_ref[...]
    dz3 = norm_back(cot, n3, r3, vec(2))
    df = dz3.astype(BF)
    sums = [total(cot * n3), total(cot), total(df.astype(F32))]
    hidden_sums, g_out = [], []
    e2 = dz3
    for c in range(chunks):
        cols = slice(c * D, (c + 1) * D)
        hid = hid_ref[:, cols]
        g_out.append(dot_tn(df, hid).astype(BF))
        du = (dot_nn(df, w2_ref[c]) * slope_ref[:, cols]).astype(BF)
        gw1_ref[cols, :] = dot_tn(du, h2_low).astype(BF)
        hidden_sums.append(total(du.astype(F32)))
        e2 = e2 + dot_nn(du, w1_ref[cols, :])
    dz2 = norm_back(e2, n2, r2, vec(1))
    dz2_ref[...] = dz2
    dca = dz2.astype(BF)
    sums += [total(e2 * n2), total(e2), total(dca.astype(F32))] + hidden_sums
    sums += [jnp.zeros_like(sums[0])] * (-len(sums) % 16)
    start = deal(packed_ref, spot_ref, 0, [gw1_ref[...], dot_tn(dca, catt).astype(BF)] + g_out)
    to_all(packed_ref, start, jnp.concatenate(sums, axis=0).astype(BF))
    send_ref[...] = packed_ref[packed_ref.shape[0] - send_ref.shape[0] :]
    dcatt = dot_nn(dca, wco_ref[...]).astype(BF)
    dcatt_ref[...] = dcatt
    stat_ref[0:HEADS, :] = lse
    stat_ref[HEADS : 2 * HEADS, :] = per_head(dcatt.astype(F32) * catt32)


def middle_rows(spots, z1, cot, outs, lses, wco, w1, w2, vec, fb, send):
    rows, parts, chunks = z1.shape[0], len(outs), w2.shape[0]
    hidden = chunks * D
    count = spots.shape[0]
    packed = (hidden + (1 + chunks) * D) // count + 6 + chunks + -(6 + chunks) % 16
    operands = [z1, cot, *outs, *lses, wco, w1, w2, vec, fb]
    out_shape = [
        jax.ShapeDtypeStruct((rows, D), F32),
        jax.ShapeDtypeStruct((rows, D), F32),
        jax.ShapeDtypeStruct((rows, D), BF),
        jax.ShapeDtypeStruct((2 * HEADS, rows), F32),
        jax.ShapeDtypeStruct((count, packed, D), BF),
        jax.ShapeDtypeStruct((send, packed, D), BF),
    ]
    whole = pl.BlockSpec(memory_space=pltpu.VMEM)
    return pl.pallas_call(
        functools.partial(middle_kernel, parts, chunks),
        in_specs=[pl.BlockSpec(memory_space=pltpu.SMEM)] + [whole] * len(operands),
        out_specs=[whole] * len(out_shape),
        out_shape=out_shape,
        scratch_shapes=[
            pltpu.VMEM((rows, hidden), BF),
            pltpu.VMEM((rows, hidden), F32),
            pltpu.VMEM((hidden, D), BF),
        ],
        compiler_params=pltpu.CompilerParams(vmem_limit_bytes=VMEM_BYTES),
        cost_estimate=cost(18),
        name="middle_rows",
    )(spots, *operands)


def last_kernel(parts, *refs):
    z1_ref, dz2_ref, att_ref = refs[:3]
    dcqs = refs[3 : 3 + parts]
    wq_ref, wo_ref, vec_ref = refs[3 + parts : 6 + parts]
    dz1_ref, datt_ref, delta_ref, gwo_ref, gwq_ref, gvec_ref = refs[6 + parts :]
    dcq = 0.0
    for part in dcqs:
        dcq = dcq + part[...].astype(F32)
    dcq = dcq.astype(BF)
    n1, r1 = norm(z1_ref[...])
    low = (n1 * vec_ref[0:1, :] + vec_ref[10:11, :]).astype(BF)
    e1 = dz2_ref[...] + dot_nn(dcq, wq_ref[...])
    dz1 = norm_back(e1, n1, r1, vec_ref[0:1, :])
    dz1_ref[...] = dz1
    da = dz1.astype(BF)
    datt = dot_nn(da, wo_ref[...]).astype(BF)
    datt_ref[...] = datt
    delta_ref[...] = per_head(datt.astype(F32) * att_ref[...].astype(F32))
    gwo_ref[...] = dot_tn(da, att_ref[...]).astype(BF)
    gwq_ref[...] = dot_tn(dcq, low).astype(BF)
    gvec_ref[...] = jnp.zeros_like(gvec_ref)
    gvec_ref[0:1, :] = total(e1 * n1)
    gvec_ref[1:2, :] = total(e1)
    gvec_ref[2:3, :] = total(da.astype(F32))
    gvec_ref[3:4, :] = total(dcq.astype(F32))


def last_rows(z1, dz2, att, dcqs, wq, wo, vec):
    rows = z1.shape[0]
    return pl.pallas_call(
        functools.partial(last_kernel, len(dcqs)),
        out_shape=[
            jax.ShapeDtypeStruct((rows, D), F32),
            jax.ShapeDtypeStruct((rows, D), BF),
            jax.ShapeDtypeStruct((HEADS, rows), F32),
            jax.ShapeDtypeStruct((D, D), BF),
            jax.ShapeDtypeStruct((D, D), BF),
            jax.ShapeDtypeStruct((8, D), F32),
        ],
        compiler_params=pltpu.CompilerParams(vmem_limit_bytes=VMEM_BYTES),
        cost_estimate=cost(6),
        name="last_rows",
    )(z1, dz2, att, *dcqs, wq, wo, vec)


def third(steps, part):
    return lambda j: (jnp.clip(j - part * steps, 0, steps - 1), 0)


def token_grads_kernel(dq_ref, dk_ref, dv_ref, w_ref, dx_ref, *backs):
    j = pl.program_id(0)

    @pl.when(j == 0)
    def _():
        dx_ref[...] = dot_nn(dq_ref[...], w_ref[0:D, :])

    back = (dot_nn(dk_ref[...], w_ref[D : 2 * D, :]) + dot_nn(dv_ref[...], w_ref[2 * D : 3 * D, :])).astype(BF)
    for part, back_ref in enumerate(backs):

        @pl.when(j // (pl.num_programs(0) // 3) == part)
        def _(back_ref=back_ref):
            back_ref[...] = back


def token_grads(dq, dk, dv, w):
    rows, keys = dq.shape[0], dk.shape[0]
    tile = 512
    steps = keys // tile // 3
    fixed = lambda shape: pl.BlockSpec(shape, lambda j: (0, 0))
    moving = pl.BlockSpec((tile, D), lambda j: (j, 0))
    return pl.pallas_call(
        token_grads_kernel,
        grid=(3 * steps,),
        in_specs=[fixed((rows, D)), moving, moving, fixed((3 * D, D))],
        out_specs=[fixed((rows, D))] + [pl.BlockSpec((tile, D), third(steps, part)) for part in range(3)],
        out_shape=[jax.ShapeDtypeStruct((rows, D), F32)] + [jax.ShapeDtypeStruct((keys // 3, D), BF)] * 3,
        compiler_params=pltpu.CompilerParams(vmem_limit_bytes=VMEM_BYTES),
        cost_estimate=cost(6),
        name="token_grads",
    )(dq, dk, dv, w)


def weight_grads_kernel(
    spot_ref, dq_ref, dk_ref, dv_ref, x_ref, before_ref, here_ref, behind_ref, a_ref, b_ref, so_ref, cq_ref, ckv_ref,
    packed_ref, send_ref, acc, sum_v,
):
    j = pl.program_id(0)
    part = j // (pl.num_programs(0) // 3)

    @pl.when(j == 0)
    def _():
        acc[...] = jnp.zeros_like(acc)
        acc[0:D, :] = dot_tn(dq_ref[...], x_ref[...])
        sum_v[...] = jnp.zeros_like(sum_v)

    dk, dv = dk_ref[...], dv_ref[...]
    for i, ext_ref in enumerate((before_ref, here_ref, behind_ref)):

        @pl.when(part == i)
        def _(ext_ref=ext_ref):
            acc[D : 2 * D, :] += dot_tn(dk, ext_ref[...])
            acc[2 * D : 3 * D, :] += dot_tn(dv, ext_ref[...])

    sum_v[0:1, :] += total(dv.astype(F32))

    @pl.when(j == pl.num_programs(0) - 1)
    def _():
        sum_q = total(dq_ref[...].astype(F32))
        sums = jnp.concatenate([a_ref[0:4, :], b_ref[0:1, :], sum_q, sum_v[0:1, :], a_ref[0:1, :]], axis=0)
        cross = jnp.concatenate([cq_ref[...], ckv_ref[...].astype(BF)], axis=0)
        start = deal(packed_ref, spot_ref, 0, [acc[...].astype(BF), so_ref[...], cross])
        to_all(packed_ref, start, jnp.concatenate([sums, sums], axis=0).astype(BF))
        send_ref[...] = packed_ref[packed_ref.shape[0] - send_ref.shape[0] :]


def weight_grads(spots, dq, dk, dv, x, exts, a, b, g_so, g_cq, g_ckv, send):
    rows, keys = x.shape[0], dk.shape[0]
    tile = 512
    steps = keys // tile // 3
    count = spots.shape[0]
    packed = 7 * D // count + 16
    fixed = lambda shape: pl.BlockSpec(shape, lambda j: (0,) * len(shape))
    moving = pl.BlockSpec((tile, D), lambda j: (j, 0))
    return pl.pallas_call(
        weight_grads_kernel,
        grid=(3 * steps,),
        in_specs=[pl.BlockSpec(memory_space=pltpu.SMEM), fixed((rows, D)), moving, moving, fixed((rows, D))]
        + [pl.BlockSpec((tile, D), third(steps, part)) for part in range(3)]
        + [fixed((8, D)), fixed((8, D)), fixed((D, D)), fixed((D, D)), fixed((2 * D, D))],
        out_specs=[fixed((count, packed, D)), fixed((send, packed, D))],
        out_shape=[jax.ShapeDtypeStruct((n, packed, D), BF) for n in (count, send)],
        scratch_shapes=[pltpu.VMEM((3 * D, D), F32), pltpu.VMEM((8, D), F32)],
        compiler_params=pltpu.CompilerParams(vmem_limit_bytes=VMEM_BYTES),
        cost_estimate=cost(9),
        name="weight_grads",
    )(spots, dq, dk, dv, x, *exts, a, b, g_so, g_cq, g_ckv)


def split(summed, rows):
    pieces, start = [], 0
    for n in rows:
        pieces.append(summed[start : start + n])
        start += n
    return pieces


def one_hot(targets, count):
    return (lax.broadcasted_iota(jnp.int32, (count, targets.shape[0]), 0) == targets[None, :]).astype(BF)


def body(
    tokens,
    memory,
    cotangent,
    deal_order,
    lengths,
    mem_index,
    self_qkv,
    self_out,
    cross_qkv,
    cross_out,
    ffn_in,
    ffn_out,
    norm_gains,
    biases,
    ffn_bias,
):
    grid = Grid()
    heads, blocks = grid.head, grid.blk
    rows = tokens.shape[0]
    block_rows = rows * heads
    mem_rows = memory.shape[0]
    assert mem_rows * heads == MEM
    block = lax.axis_index("blk")
    here = lax.axis_index("head")
    chunks = ffn_out.shape[0] // D

    w_qkv, w_so, w_cqkv, w_co, w_in = (
        w.T for w in (self_qkv, self_out, cross_qkv, cross_out, ffn_in)
    )
    w_out = jnp.transpose(ffn_out.reshape(chunks, D, -1), (0, 2, 1)).reshape(-1, D)
    n_out = w_so.shape[0]
    lanes = norm_gains.shape[1]
    small = jnp.concatenate([norm_gains.reshape(-1), biases.reshape(-1), ffn_bias])
    small = jnp.pad(small[None], ((0, 15), (0, D - small.shape[0])))

    near = [tokens] + grid.others(tokens, "y")
    in_group = deal_order - block * block_rows
    groups = [lax.dynamic_slice_in_dim(in_group, ((here - k) % heads) * rows, rows) for k in range(heads)]
    stream_rows = dot_nn(one_hot(jnp.concatenate(groups), block_rows), jnp.concatenate(near, axis=0)).astype(BF)
    up = [(i, i + heads) for i in range(grid.count - heads)]
    down = [(j, i) for i, j in up]
    before = lax.ppermute(stream_rows, BOTH, up)
    behind = lax.ppermute(stream_rows, BOTH, down)
    ext = jnp.concatenate([before, stream_rows, behind], axis=0)

    urgent = jnp.concatenate([w_qkv, small, w_so, w_cqkv, w_co], axis=0)
    urgent_z = along(grid, [(urgent[None], [{}])], "z", True)
    urgent_xy = along(grid, urgent_z, "xy", False)
    moved, stream_rows = beside([m for m, _ in urgent_xy], stream_rows)
    urgent_xy = [(m, p) for m, (_, p) in zip(moved, urgent_xy)]
    held = along(grid, urgent_xy, "c", False)
    wt_qkv, wt_small, wt_so, wt_cqkv, wt_co = place(
        grid, held, [w_qkv.shape[0], 16, n_out, w_cqkv.shape[0], n_out]
    )

    late = jnp.concatenate([w_in, w_out], axis=0)
    late = [late] + grid.others(late, "y")
    late = [late[-k % heads] for k in range(heads)] * 2
    late = lax.dynamic_slice_in_dim(
        jnp.concatenate(late, axis=0), (-here) % heads * late[0].shape[0], heads * late[0].shape[0]
    )
    gathered = lax.all_gather(jnp.concatenate([memory, late], axis=0), "blk", axis=0, tiled=True)
    gathered = gathered.reshape(blocks, -1, D)
    cut = mem_rows * 5 // 8
    smalls = wt_small.reshape(grid.count, 16, D)[:, 0, : 13 * lanes + ffn_bias.shape[0]].astype(F32)
    vec = jnp.transpose(smalls[:, : 13 * lanes].reshape(grid.count, 13, lanes), (1, 0, 2)).reshape(13, D)
    vec = jnp.pad(vec, ((0, 3), (0, 0)))
    hidden_bias = smalls[:, 13 * lanes :].reshape(1, -1)

    place_own = groups[0]
    rank = jnp.sum((place_own[None, :] < place_own[:, None]).astype(jnp.int32), axis=1)
    order = one_hot(rank, rows)
    x = dot_nn(order, tokens).astype(BF)
    cot_hi, cot_lo = hi_lo(cotangent)
    cot = dot_nn(order, cot_hi) + dot_nn(order, cot_lo)
    spot = jnp.sum(jnp.where(rank[None, :] == jnp.arange(rows)[:, None], place_own[None, :], 0), axis=1)
    spot = spot + block_rows
    count = lengths.shape[0]
    tri = jnp.arange(count)[None, :] <= jnp.arange(count)[:, None]
    ends = jnp.sum(jnp.where(tri, lengths[None, :], 0), axis=1)
    starts = ends - lengths
    base = (block - 1) * block_rows
    ext_ends, ext_starts = ends - base, starts - base
    passed = ext_ends[None, :] <= spot[:, None]
    row_begin = jnp.max(jnp.where(passed, ext_ends[None, :], -base), axis=1)
    row_end = jnp.min(jnp.where(passed, jnp.int32(1 << 30), ext_ends[None, :]), axis=1)
    lane = jnp.arange(128)[None, :]
    ranges = jnp.where(lane == 0, row_begin[:, None], row_end[:, None])
    row_ranges = jnp.where(jnp.arange(8)[:, None] == 0, row_begin[None, :], row_end[None, :])
    tq = min(128, rows)
    tk = 256
    lo = jnp.min(row_begin.reshape(-1, tq), axis=1) // tk
    hi = (jnp.max(row_end.reshape(-1, tq), axis=1) + tk - 1) // tk
    lo = jnp.maximum(lo, 0)
    hi = jnp.minimum(hi, 3 * block_rows // tk)

    inside = (ext_starts < 2 * block_rows) & (ext_ends > block_rows)
    number = jnp.arange(count)
    key = jnp.where(inside, mem_index * count + number, blocks * count * 2 + number)
    slot = jnp.sum((key[None, :] < key[:, None]).astype(jnp.int32), axis=1)
    stacked = jnp.stack(groups)
    first = jnp.sum((stacked[None] + block_rows < ext_starts[:, None, None]).astype(jnp.int32), axis=2)
    final = jnp.sum((stacked[None] + block_rows < ext_ends[:, None, None]).astype(jnp.int32), axis=2)
    columns = jnp.concatenate(
        [mem_index[:, None], jnp.stack([first, final], axis=2).reshape(count, -1)], axis=1
    )
    sorted_columns = jnp.sum(
        jnp.where((slot[None, :] == number[:, None])[:, :, None], columns[None], 0), axis=1
    )
    steps = jnp.sum(inside.astype(jnp.int32))
    live = number < steps
    final_mem = jnp.sum(jnp.where(number == steps - 1, sorted_columns[:, 0], 0))
    mem_steps = jnp.where(live, sorted_columns[:, 0], final_mem)
    mem_table = jnp.concatenate([mem_steps, steps[None]])
    memories = jnp.arange(blocks)
    ahead = 0
    for dim, coordinate in (
        ("c", lambda m: m % grid.core),
        ("x", lambda m: m // grid.core % grid.size["x"]),
        ("z", lambda m: m // (grid.core * grid.size["x"])),
    ):
        ahead = ahead * grid.size[dim] + (coordinate(memories) - grid.at[dim]) % grid.size[dim]
    used = jnp.any(inside[:, None] & (mem_index[:, None] == memories[None, :]), axis=0)
    spot_table = jnp.where(used, ahead + 1, -(ahead + 1)).astype(jnp.int32)
    row_table = jnp.where(live[:, None], sorted_columns[:, 1:], 0)
    own_table, other_table = row_table[:, :2].reshape(-1), row_table[:, 2:].reshape(-1)

    bias_q, bias_v = vec[3], vec[4]
    q = ((dot_nt(x, wt_qkv[:D]) + bias_q).astype(BF) * SCALE).astype(BF)
    kv = (dot_nt(ext, wt_qkv[D:]) + jnp.concatenate([jnp.zeros((D,), F32), bias_v])).astype(BF)
    pairs = PAIRS if 3 * block_rows <= 4096 else 1
    att, lse = self_forward(q, kv, ranges, lo, hi, tq, tk, pairs)
    z1, cq = first_rows(x, att, wt_so, wt_cqkv[:D], vec)

    queries = [cq] + grid.others(cq, "y")
    wt_ckv = wt_cqkv[D:]
    bias_kv = jnp.concatenate([jnp.zeros((D,), F32), vec[7]])[None]
    mem_kv = memory_kv(mem_table, gathered, mem_rows, wt_ckv, bias_kv)
    ctq = min(128, rows)
    outs, lses = cross_forward(mem_table, row_table.reshape(-1), mem_kv, queries, ctq)
    own_outs = [outs[0]] + [grid.shift(outs[k], y=-k) for k in range(1, heads)]
    own_lses = [lses[0]] + [grid.shift(lses[k], y=-k) for k in range(1, heads)]
    late = gathered[:, mem_rows:].reshape(grid.count, -1, D)
    late_rows = np.cumsum([0, w_in.shape[0]] + [n_out] * chunks)
    wt_in, *wt_out = (
        late[:, i:j].reshape(-1, D) for i, j in zip(late_rows[:-1], late_rows[1:])
    )
    w2 = jnp.stack(wt_out)
    spots = grid.spots("cxyz")
    send = grid.count - grid.count // grid.core

    def over_cores(packed, sent):
        shape = (grid.core, grid.size["x"] * grid.size["y"], grid.size["z"], -1, D)
        own = packed.reshape(shape)[0]
        if grid.core == 1:
            return [own]
        return [own, grid.shift(sent.reshape(shape[1:]), c=1)]

    y, dz2, dcatt, stat, packed_1, sent_1 = middle_rows(
        spots, z1, cot, own_outs, own_lses, wt_co, wt_in, w2, vec, hidden_bias, max(send, 1)
    )
    upstream = grid.others(dcatt, "y")
    stats = grid.others(stat, "y")
    terms_1 = over_cores(packed_1, sent_1)
    begun = cross_begin(mem_table, own_table, mem_kv, queries[0], dcatt, stat, ctq)
    (begun, own_dcq), (upstream, stats, terms_1) = beside(begun, (upstream, stats, terms_1))
    sum_1 = add(terms_1)
    terms_1 = grid.ahead(sum_1, "xy")
    outputs = cross_backward(
        mem_table,
        spot_table,
        other_table,
        mem_kv,
        gathered,
        wt_ckv,
        begun,
        queries[1:],
        after(upstream, sum_1),
        stats,
        ctq,
        grid.core,
    )
    outputs, terms_1 = beside(outputs, terms_1)
    keep_m, send_m, g_ckv, g_bv, *dcqs = outputs
    own_dcqs = [own_dcq] + [grid.shift(x, y=-k) for k, x in enumerate(dcqs, 1)]
    terms_m = [keep_m] if grid.core == 1 else [keep_m, grid.shift(send_m, c=1)]
    terms_1 = grid.ahead(add(terms_1), "z")
    outputs = last_rows(z1, dz2, att, own_dcqs, wt_cqkv[:D], wt_so, vec)
    outputs, (terms_m, terms_1) = beside(outputs, (terms_m, terms_1))
    dz1, datt, delta, g_so, g_cq, gvec1 = outputs
    delta = jnp.pad(delta.reshape(PAIRS, 2, rows), ((0, 0), (0, 6), (0, 0)))
    terms_m = [t.reshape(grid.size["x"], grid.size["z"], mem_rows, D) for t in terms_m]
    sends_a = [add([t[k, :, :cut] for t in terms_m]) for k in range(1, grid.size["x"])]
    sends_b = [add([t[:, k, cut:] for t in terms_m]) for k in range(1, grid.size["z"])]
    terms_a = [grid.shift(a, x=k) for k, a in enumerate(sends_a, 1)]
    terms_b = [grid.shift(b, z=k) for k, b in enumerate(sends_b, 1)]
    outputs = self_backward(
        q, after(datt, *sends_a, *sends_b), kv, row_ranges, lse, delta, lo, hi, tq, tk, pairs
    )
    outputs, (terms_a, terms_b) = beside(outputs, (terms_a, terms_b))
    sum_a = add([t[0, :, :cut] for t in terms_m] + terms_a)
    sum_b = add([t[:, 0, cut:] for t in terms_m] + terms_b)
    dq, dk, dv = after(list(outputs), sum_a, sum_b)
    terms_a, terms_b = grid.ahead(sum_a, "z"), grid.ahead(sum_b, "x")

    outputs, terms_b = beside(token_grads(dq, dk, dv, wt_qkv), terms_b)
    dxq, back_before, back_here, back_behind = outputs
    from_next = lax.ppermute(back_before, BOTH, down)
    from_prior = lax.ppermute(back_behind, BOTH, up)
    packed_2 = weight_grads(
        spots,
        after(dq, back_here, *terms_b),
        dk,
        dv,
        x,
        (before, stream_rows, behind),
        gvec1,
        g_bv,
        g_so,
        g_cq,
        g_ckv,
        max(send, 1),
    )
    packed_2, (early_a, from_next, from_prior) = beside(packed_2, (terms_a[:2], from_next, from_prior))
    terms_a = early_a + terms_a[2:]
    shared = (
        back_here.astype(F32) + from_next.astype(F32) + from_prior.astype(F32)
    ).astype(BF)

    def dealt(k):
        picks = lax.broadcasted_iota(jnp.int32, (rows, block_rows), 1) == groups[k][:, None]
        return dot_nn(picks.astype(BF), shared)

    grad_in = dz1 + dxq
    grad_hi, grad_lo = hi_lo(grad_in)
    grad_input = dot_tn(order, grad_hi) + dot_tn(order, grad_lo) + dealt(0)
    for k in range(1, heads):
        grad_input = grad_input + grid.shift(dealt(k).astype(BF), y=-k).astype(F32)
    y_hi, y_lo = hi_lo(y)
    layer_out = dot_tn(order, y_hi) + dot_tn(order, y_lo)
    grad_memory = jnp.concatenate([add(terms_a, F32), add(terms_b, F32)], axis=0)

    sum_2 = add(over_cores(*packed_2))
    sum_2 = add(grid.ahead(sum_2, "xy"))
    sum_2 = add(grid.ahead(sum_2, "z"), F32)
    sum_1 = add(terms_1, F32)
    s_in, s_co, *s_out, early = split(
        sum_1, [w_in.shape[0], n_out] + [n_out] * chunks + [sum_1.shape[0] - w_in.shape[0] - n_out * (1 + chunks)]
    )
    s_qkv, s_so, s_cq, final_rows = split(sum_2, [w_qkv.shape[0], n_out, w_cqkv.shape[0], 16])
    me = block * heads + here

    def mine(summed, first, count):
        return lax.dynamic_slice(summed, (first, me * lanes), (count, lanes))

    e, f = mine(early, 0, 6), mine(final_rows, 0, 7)
    width = ffn_bias.shape[0]
    s_bias = lax.dynamic_slice(early, (6 + me * width // D, me * width % D), (1, width))[0]
    return (
        layer_out,
        grad_input,
        grad_memory,
        s_qkv.T,
        s_so.T,
        s_cq.T,
        s_co.T,
        s_in.T,
        jnp.concatenate([s.T for s in s_out], axis=0),
        jnp.stack([f[0], e[3], e[0]]),
        jnp.stack([f[5], f[6], f[2], f[3], f[4], e[5], e[2], f[1], e[4], e[1]]),
        s_bias,
    )


def solution(mesh):
    rows = P(BOTH, None)
    cols = P(None, BOTH)
    return jax.shard_map(
        body,
        mesh=mesh,
        in_specs=(rows, rows, rows, P("blk"), P(), P()) + (cols,) * 8 + (P(BOTH),),
        out_specs=(rows,) * 3 + (cols,) * 8 + (P(BOTH),),
        check_vma=False,
    )
```

```python
import functools
import math

import jax
import jax.numpy as jnp
import numpy as np
from jax import lax
from jax.experimental import pallas as pl
from jax.experimental.pallas import tpu as pltpu
from jax.sharding import PartitionSpec as P

D = 512
HEADS = 8
MEM = 1024
HD = D // HEADS
PAIRS = HEADS // 2
SCALE = 1.0 / math.sqrt(HD)
EPSILON = 1e-05
GELU_SCALE = 0.7978845608028654
FILL = -1e30
FLOOR = -1e20
BOTH = ("blk", "head")
BF = jnp.bfloat16
F32 = jnp.float32
VMEM_BYTES = 60 * 1024 * 1024


def dot_nn(a, b):
    return lax.dot_general(a, b, (((1,), (0,)), ((), ())), preferred_element_type=F32)


def dot_nt(a, b):
    return lax.dot_general(a, b, (((1,), (1,)), ((), ())), preferred_element_type=F32)


def dot_tn(a, b):
    return lax.dot_general(a, b, (((0,), (0,)), ((), ())), preferred_element_type=F32)


def hi_lo(x):
    hi = x.astype(BF)
    return hi, (x - hi.astype(F32)).astype(BF)


class Grid:
    def __init__(self):
        self.blk = lax.axis_size("blk")
        self.head = lax.axis_size("head")
        self.core = 2 if self.blk % 2 == 0 else 1
        rest = self.blk // self.core
        major = 4 if rest % 4 == 0 else rest
        self.size = {"z": major, "x": rest // major, "c": self.core, "y": self.head}
        self.stride = {
            "y": 1,
            "c": self.head,
            "x": self.head * self.core,
            "z": self.head * self.core * (rest // major),
        }
        self.count = self.blk * self.head
        b = lax.axis_index("blk")
        self.at = {
            "y": lax.axis_index("head"),
            "c": b % self.core,
            "x": (b // self.core) % self.size["x"],
            "z": b // (self.core * self.size["x"]),
        }

    def shift(self, array, **steps):
        route = []
        for i in range(self.count):
            to = i
            for dim, step in steps.items():
                size, stride = self.size[dim], self.stride[dim]
                at = (i // stride) % size
                to += ((at + step) % size - at) * stride
            route.append((i, to))
        return lax.ppermute(array, BOTH, route)

    def offsets(self, dims):
        out = [{}]
        for dim in dims:
            out = [dict(o, **{dim: k}) for o in out for k in range(self.size[dim])]
        return out[1:]

    def others(self, array, dims):
        return [self.shift(array, **o) for o in self.offsets(dims)]

    def ahead(self, buffer, dims):
        return [buffer[0]] + [self.shift(buffer[k], **o) for k, o in enumerate(self.offsets(dims), 1)]

    def spots(self, order):
        device = jnp.arange(self.count)
        spot = 0
        for dim in order:
            at = device // self.stride[dim] % self.size[dim]
            spot = spot * self.size[dim] + (at - self.at[dim]) % self.size[dim]
        return spot.astype(jnp.int32)


def add(terms, dtype=BF):
    return sum(t.astype(F32) for t in terms).astype(dtype)


def beside(outputs, arrays):
    return lax.optimization_barrier((outputs, arrays))


def after(values, *first):
    return lax.optimization_barrier((values, *first))[0]


def cost(us):
    return pl.CostEstimate(flops=int(us * 1e3), transcendentals=0, bytes_accessed=0)


def along(grid, held, dims, join):
    out = []
    for array, places in held:
        arrays = [array] + grid.others(array, dims)
        tagged = [[dict(p, **o) for p in places] for o in [{}] + grid.offsets(dims)]
        if join:
            out.append((jnp.concatenate(arrays, axis=0), sum(tagged, [])))
        else:
            out += list(zip(arrays, tagged))
    return out


def place_kernel(z_size, rows, index_ref, *refs):
    arrays, outs = refs[: len(refs) - len(rows)], refs[len(refs) - len(rows) :]
    each = arrays[0].shape[0] // z_size
    i = pl.program_id(0)
    for a, array in enumerate(arrays):

        @pl.when(i // each == a)
        def _(array=array):
            for z in range(z_size):
                source = (i % each) * z_size + (index_ref[0] - z + z_size) % z_size
                start = 0
                for out, n in zip(outs, rows):
                    out[z, 0] = array[source, start : start + n, :]
                    start += n


def place(grid, held, rows):
    arrays = [a for a, _ in held]
    z_size = grid.size["z"]
    other = grid.count // z_size
    slot = []
    for _, places in held:
        for p in places[::z_size]:
            at = 0
            for dim in "xcy":
                at = at * grid.size[dim] + (grid.at[dim] - p.get(dim, 0)) % grid.size[dim]
            slot.append(at)
    index = jnp.stack([grid.at["z"]] + slot).astype(jnp.int32)
    outs = pl.pallas_call(
        functools.partial(place_kernel, z_size, rows),
        grid_spec=pltpu.PrefetchScalarGridSpec(
            num_scalar_prefetch=1,
            grid=(other,),
            in_specs=[pl.BlockSpec(a.shape, lambda i, _: (0, 0, 0)) for a in arrays],
            out_specs=[
                pl.BlockSpec((z_size, 1, n, D), lambda i, index: (0, index[i + 1], 0, 0)) for n in rows
            ],
        ),
        out_shape=[jax.ShapeDtypeStruct((z_size, other, n, D), BF) for n in rows],
        compiler_params=pltpu.CompilerParams(vmem_limit_bytes=VMEM_BYTES),
        cost_estimate=cost(5),
        name="place_weights",
    )(index, *arrays)
    return [out.reshape(grid.count * n, D) for out, n in zip(outs, rows)]


def lane_mask(rows):
    return lax.broadcasted_iota(jnp.int32, (rows, 2 * HD), 1) < HD


def two(low, x):
    zero = jnp.zeros_like(x)
    return jnp.concatenate([jnp.where(low, x, zero), jnp.where(low, zero, x)], axis=0)


def pick(low, x):
    half = x.shape[0] // 2
    return jnp.where(low, x[:half], x[half:])


def with_ones(v):
    return jnp.concatenate([v, jnp.ones_like(v)], axis=1)


def pair_cols(g):
    return slice(g * 2 * HD, (g + 1) * 2 * HD)


def self_forward_kernel(
    pairs, tq, tk, lo_ref, hi_ref, q_ref, k_ref, v_ref, range_ref, att_ref, lse_ref, score_ref, top_ref, acc_ref
):
    width = 2 * HD
    low = lane_mask(tq)
    for i in range(q_ref.shape[0] // tq):
        rows = pl.ds(i * tq, tq)
        begin = jnp.concatenate([range_ref[rows, 0:1]] * 2, axis=0)
        end = jnp.concatenate([range_ref[rows, 1:2]] * 2, axis=0)
        first = lo_ref[i]
        top_ref[...] = jnp.full_like(top_ref, FILL)
        acc_ref[...] = jnp.zeros_like(acc_ref)

        def scores(t, carry, i=i):
            keys = pl.ds(pl.multiple_of(t * tk, tk), tk)
            spot = pl.ds(pl.multiple_of((t - first) * tk, tk), tk)
            place = lax.broadcasted_iota(jnp.int32, (2 * tq, tk), 1) + t * tk
            allowed = (place >= begin) & (place < end)
            for g in range(pairs):
                s = dot_nt(two(low, q_ref[pl.ds(i * tq, tq), pair_cols(g)]), k_ref[keys, pair_cols(g)])
                s = jnp.where(allowed, s, FILL)
                score_ref[g, :, spot] = s
                peak = top_ref[g]
                for c in range(tk // width):
                    peak = jnp.maximum(peak, s[:, c * width : (c + 1) * width])
                top_ref[g] = peak
            return carry

        lax.fori_loop(first, hi_ref[i], scores, 0)
        for g in range(pairs):
            peak = jnp.max(top_ref[g], axis=1, keepdims=True)
            top_ref[g] = jnp.broadcast_to(peak, (2 * tq, width))

        def weigh(t, carry):
            keys = pl.ds(pl.multiple_of(t * tk, tk), tk)
            spot = pl.ds(pl.multiple_of((t - first) * tk, tk), tk)
            for g in range(pairs):
                p = jnp.exp(score_ref[g, :, spot] - top_ref[g, :, 0:1]).astype(BF)
                acc_ref[g] += dot_nn(p, with_ones(v_ref[keys, pair_cols(g)]))
            return carry

        lax.fori_loop(first, hi_ref[i], weigh, 0)
        for g in range(pairs):
            mass = acc_ref[g, :, width:]
            att_ref[rows, pair_cols(g)] = pick(low, acc_ref[g, :, :width] / mass).astype(BF)
            flat = (top_ref[g] + jnp.log(mass)).T
            lse_ref[g, 0:1, rows] = flat[0:1, :tq]
            lse_ref[g, 1:2, rows] = flat[0:1, tq:]


def self_forward(q, kv, ranges, lo, hi, tq, tk, pairs):
    rows, keys = q.shape[0], kv.shape[0]
    width = pairs * 2 * HD
    groups = PAIRS // pairs
    return pl.pallas_call(
        functools.partial(self_forward_kernel, pairs, tq, tk),
        grid_spec=pltpu.PrefetchScalarGridSpec(
            num_scalar_prefetch=2,
            grid=(groups,),
            in_specs=[
                pl.BlockSpec((rows, width), lambda g, *_: (0, g)),
                pl.BlockSpec((keys, width), lambda g, *_: (0, g)),
                pl.BlockSpec((keys, width), lambda g, *_: (0, groups + g)),
                pl.BlockSpec((rows, 128), lambda g, *_: (0, 0)),
            ],
            out_specs=[
                pl.BlockSpec((rows, width), lambda g, *_: (0, g)),
                pl.BlockSpec((pairs, 8, rows), lambda g, *_: (g, 0, 0)),
            ],
            scratch_shapes=[
                pltpu.VMEM((pairs, 2 * tq, keys), F32),
                pltpu.VMEM((pairs, 2 * tq, 2 * HD), F32),
                pltpu.VMEM((pairs, 2 * tq, 4 * HD), F32),
            ],
        ),
        out_shape=[
            jax.ShapeDtypeStruct((rows, D), BF),
            jax.ShapeDtypeStruct((PAIRS, 8, rows), F32),
        ],
        compiler_params=pltpu.CompilerParams(vmem_limit_bytes=VMEM_BYTES),
        cost_estimate=cost(20),
        name="self_forward",
    )(lo, hi, q, kv, kv, ranges)


def self_backward_kernel(
    pairs, tq, tk, lo_ref, hi_ref, q_ref, do_ref, k_ref, v_ref, row_ref, lse_ref, delta_ref, dq_ref, dk_ref, dv_ref,
    acc_q, acc_k, acc_v,
):
    low = lane_mask(tq)
    acc_k[...] = jnp.zeros_like(acc_k)
    acc_v[...] = jnp.zeros_like(acc_v)
    for i in range(q_ref.shape[0] // tq):
        rows = pl.ds(i * tq, tq)
        begin = jnp.concatenate([row_ref[0:1, rows]] * 2, axis=1)
        end = jnp.concatenate([row_ref[1:2, rows]] * 2, axis=1)
        acc_q[...] = jnp.zeros_like(acc_q)

        def step(t, carry, i=i):
            rows = pl.ds(i * tq, tq)
            keys = pl.ds(pl.multiple_of(t * tk, tk), tk)
            place = lax.broadcasted_iota(jnp.int32, (tk, 2 * tq), 0) + t * tk
            allowed = (place >= begin) & (place < end)
            for g in range(pairs):
                cols = pair_cols(g)
                k, v = k_ref[keys, cols], v_ref[keys, cols]
                q2, do2 = two(low, q_ref[rows, cols]), two(low, do_ref[rows, cols])
                lse = jnp.concatenate([lse_ref[g, 0:1, rows], lse_ref[g, 1:2, rows]], axis=1)
                delta = jnp.concatenate([delta_ref[g, 0:1, rows], delta_ref[g, 1:2, rows]], axis=1)
                p = jnp.exp(jnp.where(allowed, dot_nt(k, q2) - lse, FILL))
                ds = (p * (dot_nt(v, do2) - delta)).astype(BF)
                acc_v[keys, cols] += dot_nn(p.astype(BF), do2)
                acc_k[keys, cols] += dot_nn(ds, q2)
                acc_q[g] += dot_tn(ds, k)
            return carry

        lax.fori_loop(lo_ref[i], hi_ref[i], step, 0)
        for g in range(pairs):
            dq_ref[rows, pair_cols(g)] = (pick(low, acc_q[g]) * SCALE).astype(BF)
    dk_ref[...] = acc_k[...].astype(BF)
    dv_ref[...] = acc_v[...].astype(BF)


def self_backward(q, do, kv, row_range, lse, delta, lo, hi, tq, tk, pairs):
    rows, keys = q.shape[0], kv.shape[0]
    width = pairs * 2 * HD
    groups = PAIRS // pairs
    return pl.pallas_call(
        functools.partial(self_backward_kernel, pairs, tq, tk),
        grid_spec=pltpu.PrefetchScalarGridSpec(
            num_scalar_prefetch=2,
            grid=(groups,),
            in_specs=[
                pl.BlockSpec((rows, width), lambda g, *_: (0, g)),
                pl.BlockSpec((rows, width), lambda g, *_: (0, g)),
                pl.BlockSpec((keys, width), lambda g, *_: (0, g)),
                pl.BlockSpec((keys, width), lambda g, *_: (0, groups + g)),
                pl.BlockSpec((8, rows), lambda g, *_: (0, 0)),
                pl.BlockSpec((pairs, 8, rows), lambda g, *_: (g, 0, 0)),
                pl.BlockSpec((pairs, 8, rows), lambda g, *_: (g, 0, 0)),
            ],
            out_specs=[
                pl.BlockSpec((rows, width), lambda g, *_: (0, g)),
                pl.BlockSpec((keys, width), lambda g, *_: (0, g)),
                pl.BlockSpec((keys, width), lambda g, *_: (0, g)),
            ],
            scratch_shapes=[
                pltpu.VMEM((pairs, 2 * tq, 2 * HD), F32),
                pltpu.VMEM((keys, width), F32),
                pltpu.VMEM((keys, width), F32),
            ],
        ),
        out_shape=[
            jax.ShapeDtypeStruct((rows, D), BF),
            jax.ShapeDtypeStruct((keys, D), BF),
            jax.ShapeDtypeStruct((keys, D), BF),
        ],
        compiler_params=pltpu.CompilerParams(vmem_limit_bytes=VMEM_BYTES),
        cost_estimate=cost(40),
        name="self_backward",
    )(lo, hi, q, do, kv, kv, row_range, lse, delta)


def memory_kv_kernel(mem_ref, m_ref, w_ref, b_ref, kv_ref):
    j = pl.program_id(0)

    @pl.when((j == 0) | (mem_ref[j] != mem_ref[jnp.maximum(j - 1, 0)]))
    def _():
        kv_ref[0] = (dot_nt(m_ref[0], w_ref[...]) + b_ref[...]).astype(BF)


def memory_kv(mem, gathered, n, weights, bias):
    blocks = gathered.shape[0]
    by_memory = lambda j, mem: (mem[j], 0, 0)
    return pl.pallas_call(
        memory_kv_kernel,
        grid_spec=pltpu.PrefetchScalarGridSpec(
            num_scalar_prefetch=1,
            grid=(mem.shape[0] - 1,),
            in_specs=[
                pl.BlockSpec((1, n, D), by_memory),
                pl.BlockSpec((2 * D, D), lambda j, *_: (0, 0)),
                pl.BlockSpec((1, 2 * D), lambda j, *_: (0, 0)),
            ],
            out_specs=pl.BlockSpec((1, n, 2 * D), by_memory),
        ),
        out_shape=jax.ShapeDtypeStruct((blocks, n, 2 * D), BF),
        compiler_params=pltpu.CompilerParams(vmem_limit_bytes=VMEM_BYTES),
        cost_estimate=cost(6),
        name="memory_kv",
    )(mem, gathered, weights, bias)


def cross_forward_kernel(parts, tq, mem_ref, table_ref, kv_ref, *refs):
    qs, outs, lses = refs[:parts], refs[parts : 2 * parts], refs[2 * parts : 3 * parts]
    width = 2 * HD
    j = pl.program_id(0)
    low = lane_mask(tq)
    for part in range(parts):
        first_row = table_ref[j * 2 * parts + 2 * part]
        last_row = table_ref[j * 2 * parts + 2 * part + 1]

        def step(t, carry, part=part, first_row=first_row, last_row=last_row):
            offset = pl.multiple_of(t * tq, tq)
            rows = pl.ds(offset, tq)
            at = lax.broadcasted_iota(jnp.int32, (tq, width), 0) + offset
            mine = (at >= first_row) & (at < last_row)
            at_row = lax.broadcasted_iota(jnp.int32, (1, tq), 1) + offset
            mine_row = (at_row >= first_row) & (at_row < last_row)
            for g in range(PAIRS):
                cols = pair_cols(g)
                s = dot_nt(two(low, qs[part][rows, cols]), kv_ref[0, :, cols])
                peak = jnp.max(s, axis=1, keepdims=True)
                p = jnp.exp(s - peak).astype(BF)
                acc = dot_nn(p, with_ones(kv_ref[0, :, pair_cols(PAIRS + g)]))
                mass = acc[:, width:]
                new = pick(low, acc[:, :width] / mass).astype(BF)
                outs[part][rows, cols] = jnp.where(mine, new, outs[part][rows, cols])
                flat = (peak + jnp.log(mass)).T
                for i in range(2):
                    head = slice(2 * g + i, 2 * g + i + 1)
                    lses[part][head, rows] = jnp.where(
                        mine_row, flat[0:1, i * tq : (i + 1) * tq], lses[part][head, rows]
                    )
            return carry

        lax.fori_loop(first_row // tq, (last_row + tq - 1) // tq, step, 0)


def cross_forward(mem, table, kv, queries, tq):
    parts, rows, n = len(queries), queries[0].shape[0], kv.shape[1]
    whole = pl.BlockSpec((rows, D), lambda j, *_: (0, 0))
    flat = pl.BlockSpec((HEADS, rows), lambda j, *_: (0, 0))
    out = pl.pallas_call(
        functools.partial(cross_forward_kernel, parts, tq),
        grid_spec=pltpu.PrefetchScalarGridSpec(
            num_scalar_prefetch=2,
            grid=(mem.shape[0] - 1,),
            in_specs=[pl.BlockSpec((1, n, 2 * D), lambda j, mem, _: (mem[j], 0, 0))] + [whole] * parts,
            out_specs=[whole] * parts + [flat] * parts,
        ),
        out_shape=[jax.ShapeDtypeStruct((rows, D), BF)] * parts
        + [jax.ShapeDtypeStruct((HEADS, rows), F32)] * parts,
        compiler_params=pltpu.CompilerParams(vmem_limit_bytes=VMEM_BYTES),
        cost_estimate=cost(16),
        name="cross_forward",
    )(mem, table, kv, *queries)
    return out[:parts], out[parts:]


def gradient_step(tq, kv_ref, q_ref, do_ref, stat_ref, first_row, last_row, add_k, add_v, add_q):
    low = lane_mask(tq)

    def step(t, carry):
        rows = pl.ds(pl.multiple_of(t * tq, tq), tq)
        at_row = lax.broadcasted_iota(jnp.int32, (1, tq), 1) + t * tq
        mine = (at_row >= first_row) & (at_row < last_row)
        for g in range(PAIRS):
            cols = pair_cols(g)
            k, v = kv_ref[0, :, cols], kv_ref[0, :, pair_cols(PAIRS + g)]
            q2, do2 = two(low, q_ref[rows, cols]), two(low, do_ref[rows, cols])

            def stat(base, g=g):
                return [stat_ref[base + 2 * g + i : base + 2 * g + i + 1, rows] for i in range(2)]

            lse = jnp.concatenate([jnp.where(mine, x, -FILL) for x in stat(0)], axis=1)
            delta = jnp.concatenate(stat(HEADS), axis=1)
            p = jnp.exp(dot_nt(k, q2) - lse)
            ds = (p * (dot_nt(v, do2) - delta)).astype(BF)
            add_v(cols, dot_nn(p.astype(BF), do2))
            add_k(cols, dot_nn(ds, q2))
            add_q(rows, cols, pick(low, dot_tn(ds, k)))
        return carry

    lax.fori_loop(first_row // tq, (last_row + tq - 1) // tq, step, 0)


def cross_begin_kernel(tq, mem_ref, table_ref, kv_ref, q_ref, do_ref, stat_ref, dkv_ref, dq_ref, acc_q):
    j = pl.program_id(0)

    @pl.when(j == 0)
    def _():
        acc_q[...] = jnp.zeros_like(acc_q)

    @pl.when((j == 0) | (mem_ref[j] != mem_ref[jnp.maximum(j - 1, 0)]))
    def _():
        dkv_ref[...] = jnp.zeros_like(dkv_ref)

    def add_k(cols, x):
        dkv_ref[0, :, cols] += x

    def add_v(cols, x):
        dkv_ref[0, :, D + cols.start : D + cols.stop] += x

    def add_q(rows, cols, x):
        acc_q[rows, cols] += x

    gradient_step(
        tq, kv_ref, q_ref, do_ref, stat_ref, table_ref[2 * j], table_ref[2 * j + 1], add_k, add_v, add_q
    )

    @pl.when(j == pl.num_programs(0) - 1)
    def _():
        dq_ref[...] = (acc_q[...] * SCALE).astype(BF)


def cross_begin(mem, table, kv, query, upstream, stat, tq):
    rows, n, blocks = query.shape[0], kv.shape[1], kv.shape[0]
    whole = pl.BlockSpec((rows, D), lambda j, *_: (0, 0))
    by_memory = pl.BlockSpec((1, n, 2 * D), lambda j, mem, *_: (mem[j], 0, 0))
    return pl.pallas_call(
        functools.partial(cross_begin_kernel, tq),
        grid_spec=pltpu.PrefetchScalarGridSpec(
            num_scalar_prefetch=2,
            grid=(mem.shape[0] - 1,),
            in_specs=[by_memory, whole, whole, pl.BlockSpec((2 * HEADS, rows), lambda j, *_: (0, 0))],
            out_specs=[by_memory, whole],
            scratch_shapes=[pltpu.VMEM((rows, D), F32)],
        ),
        out_shape=[jax.ShapeDtypeStruct((blocks, n, 2 * D), F32), jax.ShapeDtypeStruct((rows, D), BF)],
        compiler_params=pltpu.CompilerParams(vmem_limit_bytes=VMEM_BYTES),
        cost_estimate=cost(16),
        name="cross_begin",
    )(mem, table, kv, query, upstream, stat)


def cross_backward_kernel(parts, tq, blocks, mem_ref, spot_ref, table_ref, kv_ref, m_ref, w_ref, begun_ref, *refs):
    qs, dos, stats = refs[:parts], refs[parts : 2 * parts], refs[2 * parts : 3 * parts]
    keep_ref, send_ref, gw_ref, gb_ref = refs[3 * parts : 3 * parts + 4]
    dqs = refs[3 * parts + 4 : 4 * parts + 4]
    acc, acc_q, stage, zero, stage_sem, zero_sem = refs[4 * parts + 4 :]
    j = pl.program_id(0)
    last = mem_ref.shape[0] - 2
    steps = mem_ref[last + 1]
    now = mem_ref[j]
    previous = mem_ref[jnp.maximum(j - 1, 0)]
    following = mem_ref[jnp.minimum(j + 1, last)]
    half = keep_ref.shape[0]

    def to_target(source, spot, sem, wanted, act):
        for target, mine in ((keep_ref, spot < half), (send_ref, spot >= half)):
            copy = pltpu.make_async_copy(source, target.at[spot % half], sem)
            pl.when(wanted & mine)(functools.partial(act, copy))

    start, wait = (lambda copy: copy.start()), (lambda copy: copy.wait())

    def zeros(act):
        for m in range(blocks):
            spot = spot_ref[m]
            to_target(zero, jnp.abs(spot) - 1, zero_sem.at[m], spot < 0, act)

    @pl.when(j == 0)
    def _():
        acc_q[...] = jnp.zeros_like(acc_q)
        gw_ref[...] = jnp.zeros_like(gw_ref)
        gb_ref[...] = jnp.zeros_like(gb_ref)
        zero[...] = jnp.zeros_like(zero)
        zeros(start)

    @pl.when((j == 0) | (now != previous))
    def _():
        acc[...] = begun_ref[0]

    def add_k(cols, x):
        acc[:, cols] += x

    def add_v(cols, x):
        acc[:, D + cols.start : D + cols.stop] += x

    for part in range(parts):

        def add_q(rows, cols, x, part=part):
            acc_q[part, rows, cols] += x

        at = j * 2 * parts + 2 * part
        gradient_step(
            tq, kv_ref, qs[part], dos[part], stats[part], table_ref[at], table_ref[at + 1], add_k, add_v, add_q
        )

    @pl.when((j == steps - 1) | ((j < steps) & (now != following)))
    def _():
        dk, dv = acc[:, :D].astype(BF), acc[:, D:].astype(BF)
        spot = spot_ref[now] - 1
        stage[...] = (dot_nn(dk, w_ref[0:D, :]) + dot_nn(dv, w_ref[D : 2 * D, :])).astype(BF)
        to_target(stage, spot, stage_sem, spot >= 0, start)
        gw_ref[0:D, :] += dot_tn(dk, m_ref[0])
        gw_ref[D : 2 * D, :] += dot_tn(dv, m_ref[0])
        gb_ref[0:1, :] += jnp.sum(dv.astype(F32), axis=0, keepdims=True)
        to_target(stage, spot, stage_sem, spot >= 0, wait)

    @pl.when(j == steps - 1)
    def _():
        for part in range(parts):
            dqs[part][...] = (acc_q[part] * SCALE).astype(BF)
        zeros(wait)


def cross_backward(mem, spot, table, kv, gathered, weights, begun, queries, upstream, stats, tq, cores):
    parts, rows, n = len(queries), queries[0].shape[0], kv.shape[1]
    blocks = kv.shape[0]
    whole = pl.BlockSpec((rows, D), lambda j, *_: (0, 0))
    flat = pl.BlockSpec((2 * HEADS, rows), lambda j, *_: (0, 0))
    by_memory = lambda j, mem, *_: (mem[j], 0, 0)
    anywhere = pl.BlockSpec(memory_space=pl.ANY)
    return pl.pallas_call(
        functools.partial(cross_backward_kernel, parts, tq, blocks),
        grid_spec=pltpu.PrefetchScalarGridSpec(
            num_scalar_prefetch=3,
            grid=(mem.shape[0] - 1,),
            in_specs=[
                pl.BlockSpec((1, n, 2 * D), by_memory),
                pl.BlockSpec((1, n, D), by_memory),
                pl.BlockSpec((2 * D, D), lambda j, *_: (0, 0)),
                pl.BlockSpec((1, n, 2 * D), by_memory),
            ]
            + [whole] * (2 * parts)
            + [flat] * parts,
            out_specs=[
                anywhere,
                anywhere,
                pl.BlockSpec((2 * D, D), lambda j, *_: (0, 0)),
                pl.BlockSpec((8, D), lambda j, *_: (0, 0)),
            ]
            + [whole] * parts,
            scratch_shapes=[
                pltpu.VMEM((n, 2 * D), F32),
                pltpu.VMEM((parts, rows, D), F32),
                pltpu.VMEM((n, D), BF),
                pltpu.VMEM((n, D), BF),
                pltpu.SemaphoreType.DMA,
                pltpu.SemaphoreType.DMA((blocks,)),
            ],
        ),
        out_shape=[jax.ShapeDtypeStruct((blocks // cores, n, D), BF)] * 2
        + [
            jax.ShapeDtypeStruct((2 * D, D), F32),
            jax.ShapeDtypeStruct((8, D), F32),
        ]
        + [jax.ShapeDtypeStruct((rows, D), BF)] * parts,
        compiler_params=pltpu.CompilerParams(vmem_limit_bytes=VMEM_BYTES),
        cost_estimate=cost(20),
        name="cross_backward",
    )(mem, spot, table, kv, gathered, weights, begun, *queries, *upstream, *stats)


def norm(z):
    centre = z - jnp.mean(z, axis=1, keepdims=True)
    inverse = lax.rsqrt(jnp.mean(centre * centre, axis=1, keepdims=True) + EPSILON)
    return centre * inverse, inverse


def norm_back(upstream, normed, inverse, gain):
    scaled = upstream * gain
    return inverse * (
        scaled
        - jnp.mean(scaled, axis=1, keepdims=True)
        - normed * jnp.mean(scaled * normed, axis=1, keepdims=True)
    )


def total(x):
    return jnp.sum(x, axis=0, keepdims=True)


def head_rows():
    lane = lax.broadcasted_iota(jnp.int32, (HEADS, D), 1) // HD
    return (lane == lax.broadcasted_iota(jnp.int32, (HEADS, D), 0)).astype(F32).astype(BF)


def per_head(product):
    hi, lo = hi_lo(product)
    heads = head_rows()
    return dot_nt(heads, hi) + dot_nt(heads, lo)


def spread(rows):
    hi, lo = hi_lo(rows)
    heads = head_rows()
    return dot_tn(hi, heads) + dot_tn(lo, heads)


def deal(packed_ref, spot_ref, start, values):
    count = packed_ref.shape[0]
    for value in values:
        n = value.shape[0] // count
        for i in range(count):
            packed_ref[spot_ref[i], start : start + n, :] = value[i * n : (i + 1) * n]
        start += n
    return start


def to_all(packed_ref, start, rows):
    for i in range(packed_ref.shape[0]):
        packed_ref[i, start : start + rows.shape[0], :] = rows


def first_kernel(x_ref, att_ref, wo_ref, wq_ref, vec_ref, z_ref, cq_ref):
    z = x_ref[...].astype(F32) + dot_nt(att_ref[...], wo_ref[...]) + vec_ref[5:6, :]
    z_ref[...] = z
    n, _ = norm(z)
    low = (n * vec_ref[0:1, :] + vec_ref[10:11, :]).astype(BF)
    cq_ref[...] = ((dot_nt(low, wq_ref[...]) + vec_ref[6:7, :]).astype(BF) * SCALE).astype(BF)


def first_rows(x, att, wo, wq, vec):
    rows = x.shape[0]
    return pl.pallas_call(
        first_kernel,
        out_shape=[jax.ShapeDtypeStruct((rows, D), F32), jax.ShapeDtypeStruct((rows, D), BF)],
        compiler_params=pltpu.CompilerParams(vmem_limit_bytes=VMEM_BYTES),
        cost_estimate=cost(4),
        name="first_rows",
    )(x, att, wo, wq, vec)


def middle_kernel(parts, chunks, spot_ref, *refs):
    z1_ref, cot_ref = refs[:2]
    outs = refs[2 : 2 + parts]
    lses = refs[2 + parts : 2 + 2 * parts]
    wco_ref, w1_ref, w2_ref, vec_ref, fb_ref = refs[2 + 2 * parts : 7 + 2 * parts]
    y_ref, dz2_ref, dcatt_ref, stat_ref, packed_ref, send_ref, hid_ref, slope_ref, gw1_ref = refs[7 + 2 * parts :]
    vec = lambda i: vec_ref[i : i + 1, :]
    peak = lses[0][...]
    for part in range(1, parts):
        peak = jnp.maximum(peak, lses[part][...])
    mass = 0.0
    for part in range(parts):
        mass = mass + jnp.exp(lses[part][...] - peak)
    lse = peak + jnp.log(mass)
    catt32 = 0.0
    for part in range(parts):
        catt32 = catt32 + spread(jnp.exp(lses[part][...] - lse)) * outs[part][...].astype(F32)
    catt = catt32.astype(BF)
    n1, _ = norm(z1_ref[...])
    h1 = n1 * vec(0) + vec(10)
    z2 = h1 + dot_nt(catt, wco_ref[...]) + vec(8)
    n2, r2 = norm(z2)
    h2 = n2 * vec(1) + vec(11)
    h2_low = h2.astype(BF)
    z3 = h2 + vec(9)
    for c in range(chunks):
        cols = slice(c * D, (c + 1) * D)
        u = dot_nt(h2_low, w1_ref[cols, :]) + fb_ref[:, cols]
        square = u * u
        t = jnp.tanh(GELU_SCALE * (u + 0.044715 * u * square))
        hid = (0.5 * u * (1.0 + t)).astype(BF)
        hid_ref[:, cols] = hid
        slope_ref[:, cols] = 0.5 * (1.0 + t) + 0.5 * u * (1.0 - t * t) * (
            GELU_SCALE * (1.0 + 3.0 * 0.044715 * square)
        )
        z3 = z3 + dot_nt(hid, w2_ref[c])
    n3, r3 = norm(z3)
    y_ref[...] = n3 * vec(2) + vec(12)
    cot = cot_ref[...]
    dz3 = norm_back(cot, n3, r3, vec(2))
    df = dz3.astype(BF)
    sums = [total(cot * n3), total(cot), total(df.astype(F32))]
    hidden_sums, g_out = [], []
    e2 = dz3
    for c in range(chunks):
        cols = slice(c * D, (c + 1) * D)
        hid = hid_ref[:, cols]
        g_out.append(dot_tn(df, hid).astype(BF))
        du = (dot_nn(df, w2_ref[c]) * slope_ref[:, cols]).astype(BF)
        gw1_ref[cols, :] = dot_tn(du, h2_low).astype(BF)
        hidden_sums.append(total(du.astype(F32)))
        e2 = e2 + dot_nn(du, w1_ref[cols, :])
    dz2 = norm_back(e2, n2, r2, vec(1))
    dz2_ref[...] = dz2
    dca = dz2.astype(BF)
    sums += [total(e2 * n2), total(e2), total(dca.astype(F32))] + hidden_sums
    sums += [jnp.zeros_like(sums[0])] * (-len(sums) % 16)
    start = deal(packed_ref, spot_ref, 0, [gw1_ref[...], dot_tn(dca, catt).astype(BF)] + g_out)
    to_all(packed_ref, start, jnp.concatenate(sums, axis=0).astype(BF))
    send_ref[...] = packed_ref[packed_ref.shape[0] - send_ref.shape[0] :]
    dcatt = dot_nn(dca, wco_ref[...]).astype(BF)
    dcatt_ref[...] = dcatt
    stat_ref[0:HEADS, :] = lse
    stat_ref[HEADS : 2 * HEADS, :] = per_head(dcatt.astype(F32) * catt32)


def middle_rows(spots, z1, cot, outs, lses, wco, w1, w2, vec, fb, send):
    rows, parts, chunks = z1.shape[0], len(outs), w2.shape[0]
    hidden = chunks * D
    count = spots.shape[0]
    packed = (hidden + (1 + chunks) * D) // count + 6 + chunks + -(6 + chunks) % 16
    operands = [z1, cot, *outs, *lses, wco, w1, w2, vec, fb]
    out_shape = [
        jax.ShapeDtypeStruct((rows, D), F32),
        jax.ShapeDtypeStruct((rows, D), F32),
        jax.ShapeDtypeStruct((rows, D), BF),
        jax.ShapeDtypeStruct((2 * HEADS, rows), F32),
        jax.ShapeDtypeStruct((count, packed, D), BF),
        jax.ShapeDtypeStruct((send, packed, D), BF),
    ]
    whole = pl.BlockSpec(memory_space=pltpu.VMEM)
    return pl.pallas_call(
        functools.partial(middle_kernel, parts, chunks),
        in_specs=[pl.BlockSpec(memory_space=pltpu.SMEM)] + [whole] * len(operands),
        out_specs=[whole] * len(out_shape),
        out_shape=out_shape,
        scratch_shapes=[
            pltpu.VMEM((rows, hidden), BF),
            pltpu.VMEM((rows, hidden), F32),
            pltpu.VMEM((hidden, D), BF),
        ],
        compiler_params=pltpu.CompilerParams(vmem_limit_bytes=VMEM_BYTES),
        cost_estimate=cost(18),
        name="middle_rows",
    )(spots, *operands)


def last_kernel(parts, *refs):
    z1_ref, dz2_ref, att_ref = refs[:3]
    dcqs = refs[3 : 3 + parts]
    wq_ref, wo_ref, vec_ref = refs[3 + parts : 6 + parts]
    dz1_ref, datt_ref, delta_ref, gwo_ref, gwq_ref, gvec_ref = refs[6 + parts :]
    dcq = 0.0
    for part in dcqs:
        dcq = dcq + part[...].astype(F32)
    dcq = dcq.astype(BF)
    n1, r1 = norm(z1_ref[...])
    low = (n1 * vec_ref[0:1, :] + vec_ref[10:11, :]).astype(BF)
    e1 = dz2_ref[...] + dot_nn(dcq, wq_ref[...])
    dz1 = norm_back(e1, n1, r1, vec_ref[0:1, :])
    dz1_ref[...] = dz1
    da = dz1.astype(BF)
    datt = dot_nn(da, wo_ref[...]).astype(BF)
    datt_ref[...] = datt
    delta_ref[...] = per_head(datt.astype(F32) * att_ref[...].astype(F32))
    gwo_ref[...] = dot_tn(da, att_ref[...]).astype(BF)
    gwq_ref[...] = dot_tn(dcq, low).astype(BF)
    gvec_ref[...] = jnp.zeros_like(gvec_ref)
    gvec_ref[0:1, :] = total(e1 * n1)
    gvec_ref[1:2, :] = total(e1)
    gvec_ref[2:3, :] = total(da.astype(F32))
    gvec_ref[3:4, :] = total(dcq.astype(F32))


def last_rows(z1, dz2, att, dcqs, wq, wo, vec):
    rows = z1.shape[0]
    return pl.pallas_call(
        functools.partial(last_kernel, len(dcqs)),
        out_shape=[
            jax.ShapeDtypeStruct((rows, D), F32),
            jax.ShapeDtypeStruct((rows, D), BF),
            jax.ShapeDtypeStruct((HEADS, rows), F32),
            jax.ShapeDtypeStruct((D, D), BF),
            jax.ShapeDtypeStruct((D, D), BF),
            jax.ShapeDtypeStruct((8, D), F32),
        ],
        compiler_params=pltpu.CompilerParams(vmem_limit_bytes=VMEM_BYTES),
        cost_estimate=cost(6),
        name="last_rows",
    )(z1, dz2, att, *dcqs, wq, wo, vec)


def third(steps, part):
    return lambda j: (jnp.clip(j - part * steps, 0, steps - 1), 0)


def token_grads_kernel(dq_ref, dk_ref, dv_ref, w_ref, dx_ref, *backs):
    j = pl.program_id(0)

    @pl.when(j == 0)
    def _():
        dx_ref[...] = dot_nn(dq_ref[...], w_ref[0:D, :])

    back = (dot_nn(dk_ref[...], w_ref[D : 2 * D, :]) + dot_nn(dv_ref[...], w_ref[2 * D : 3 * D, :])).astype(BF)
    for part, back_ref in enumerate(backs):

        @pl.when(j // (pl.num_programs(0) // 3) == part)
        def _(back_ref=back_ref):
            back_ref[...] = back


def token_grads(dq, dk, dv, w):
    rows, keys = dq.shape[0], dk.shape[0]
    tile = 512
    steps = keys // tile // 3
    fixed = lambda shape: pl.BlockSpec(shape, lambda j: (0, 0))
    moving = pl.BlockSpec((tile, D), lambda j: (j, 0))
    return pl.pallas_call(
        token_grads_kernel,
        grid=(3 * steps,),
        in_specs=[fixed((rows, D)), moving, moving, fixed((3 * D, D))],
        out_specs=[fixed((rows, D))] + [pl.BlockSpec((tile, D), third(steps, part)) for part in range(3)],
        out_shape=[jax.ShapeDtypeStruct((rows, D), F32)] + [jax.ShapeDtypeStruct((keys // 3, D), BF)] * 3,
        compiler_params=pltpu.CompilerParams(vmem_limit_bytes=VMEM_BYTES),
        cost_estimate=cost(6),
        name="token_grads",
    )(dq, dk, dv, w)


def weight_grads_kernel(
    spot_ref, dq_ref, dk_ref, dv_ref, x_ref, before_ref, here_ref, behind_ref, a_ref, b_ref, so_ref, cq_ref, ckv_ref,
    packed_ref, send_ref, acc, sum_v,
):
    j = pl.program_id(0)
    part = j // (pl.num_programs(0) // 3)

    @pl.when(j == 0)
    def _():
        acc[...] = jnp.zeros_like(acc)
        acc[0:D, :] = dot_tn(dq_ref[...], x_ref[...])
        sum_v[...] = jnp.zeros_like(sum_v)

    dk, dv = dk_ref[...], dv_ref[...]
    for i, ext_ref in enumerate((before_ref, here_ref, behind_ref)):

        @pl.when(part == i)
        def _(ext_ref=ext_ref):
            acc[D : 2 * D, :] += dot_tn(dk, ext_ref[...])
            acc[2 * D : 3 * D, :] += dot_tn(dv, ext_ref[...])

    sum_v[0:1, :] += total(dv.astype(F32))

    @pl.when(j == pl.num_programs(0) - 1)
    def _():
        sum_q = total(dq_ref[...].astype(F32))
        sums = jnp.concatenate([a_ref[0:4, :], b_ref[0:1, :], sum_q, sum_v[0:1, :], a_ref[0:1, :]], axis=0)
        cross = jnp.concatenate([cq_ref[...], ckv_ref[...].astype(BF)], axis=0)
        start = deal(packed_ref, spot_ref, 0, [acc[...].astype(BF), so_ref[...], cross])
        to_all(packed_ref, start, jnp.concatenate([sums, sums], axis=0).astype(BF))
        send_ref[...] = packed_ref[packed_ref.shape[0] - send_ref.shape[0] :]


def weight_grads(spots, dq, dk, dv, x, exts, a, b, g_so, g_cq, g_ckv, send):
    rows, keys = x.shape[0], dk.shape[0]
    tile = 512
    steps = keys // tile // 3
    count = spots.shape[0]
    packed = 7 * D // count + 16
    fixed = lambda shape: pl.BlockSpec(shape, lambda j: (0,) * len(shape))
    moving = pl.BlockSpec((tile, D), lambda j: (j, 0))
    return pl.pallas_call(
        weight_grads_kernel,
        grid=(3 * steps,),
        in_specs=[pl.BlockSpec(memory_space=pltpu.SMEM), fixed((rows, D)), moving, moving, fixed((rows, D))]
        + [pl.BlockSpec((tile, D), third(steps, part)) for part in range(3)]
        + [fixed((8, D)), fixed((8, D)), fixed((D, D)), fixed((D, D)), fixed((2 * D, D))],
        out_specs=[fixed((count, packed, D)), fixed((send, packed, D))],
        out_shape=[jax.ShapeDtypeStruct((n, packed, D), BF) for n in (count, send)],
        scratch_shapes=[pltpu.VMEM((3 * D, D), F32), pltpu.VMEM((8, D), F32)],
        compiler_params=pltpu.CompilerParams(vmem_limit_bytes=VMEM_BYTES),
        cost_estimate=cost(9),
        name="weight_grads",
    )(spots, dq, dk, dv, x, *exts, a, b, g_so, g_cq, g_ckv)


def split(summed, rows):
    pieces, start = [], 0
    for n in rows:
        pieces.append(summed[start : start + n])
        start += n
    return pieces


def one_hot(targets, count):
    return (lax.broadcasted_iota(jnp.int32, (count, targets.shape[0]), 0) == targets[None, :]).astype(BF)


def body(
    tokens,
    memory,
    cotangent,
    deal_order,
    lengths,
    mem_index,
    self_qkv,
    self_out,
    cross_qkv,
    cross_out,
    ffn_in,
    ffn_out,
    norm_gains,
    biases,
    ffn_bias,
):
    grid = Grid()
    heads, blocks = grid.head, grid.blk
    rows = tokens.shape[0]
    block_rows = rows * heads
    mem_rows = memory.shape[0]
    assert mem_rows * heads == MEM
    block = lax.axis_index("blk")
    here = lax.axis_index("head")
    chunks = ffn_out.shape[0] // D

    w_qkv, w_so, w_cqkv, w_co, w_in = (
        w.T for w in (self_qkv, self_out, cross_qkv, cross_out, ffn_in)
    )
    w_out = jnp.transpose(ffn_out.reshape(chunks, D, -1), (0, 2, 1)).reshape(-1, D)
    n_out = w_so.shape[0]
    lanes = norm_gains.shape[1]
    small = jnp.concatenate([norm_gains.reshape(-1), biases.reshape(-1), ffn_bias])
    small = jnp.pad(small[None], ((0, 15), (0, D - small.shape[0])))

    near = [tokens] + grid.others(tokens, "y")
    in_group = deal_order - block * block_rows
    groups = [lax.dynamic_slice_in_dim(in_group, ((here - k) % heads) * rows, rows) for k in range(heads)]
    stream_rows = dot_nn(one_hot(jnp.concatenate(groups), block_rows), jnp.concatenate(near, axis=0)).astype(BF)
    up = [(i, i + heads) for i in range(grid.count - heads)]
    down = [(j, i) for i, j in up]
    before = lax.ppermute(stream_rows, BOTH, up)
    behind = lax.ppermute(stream_rows, BOTH, down)
    ext = jnp.concatenate([before, stream_rows, behind], axis=0)

    urgent = jnp.concatenate([w_qkv, small, w_so, w_cqkv, w_co], axis=0)
    urgent_z = along(grid, [(urgent[None], [{}])], "z", True)
    urgent_xy = along(grid, urgent_z, "xy", False)
    moved, stream_rows = beside([m for m, _ in urgent_xy], stream_rows)
    urgent_xy = [(m, p) for m, (_, p) in zip(moved, urgent_xy)]
    held = along(grid, urgent_xy, "c", False)
    wt_qkv, wt_small, wt_so, wt_cqkv, wt_co = place(
        grid, held, [w_qkv.shape[0], 16, n_out, w_cqkv.shape[0], n_out]
    )

    late = jnp.concatenate([w_in, w_out], axis=0)
    late = [late] + grid.others(late, "y")
    late = [late[-k % heads] for k in range(heads)] * 2
    late = lax.dynamic_slice_in_dim(
        jnp.concatenate(late, axis=0), (-here) % heads * late[0].shape[0], heads * late[0].shape[0]
    )
    gathered = lax.all_gather(jnp.concatenate([memory, late], axis=0), "blk", axis=0, tiled=True)
    gathered = gathered.reshape(blocks, -1, D)
    cut = mem_rows * 5 // 8
    smalls = wt_small.reshape(grid.count, 16, D)[:, 0, : 13 * lanes + ffn_bias.shape[0]].astype(F32)
    vec = jnp.transpose(smalls[:, : 13 * lanes].reshape(grid.count, 13, lanes), (1, 0, 2)).reshape(13, D)
    vec = jnp.pad(vec, ((0, 3), (0, 0)))
    hidden_bias = smalls[:, 13 * lanes :].reshape(1, -1)

    place_own = groups[0]
    rank = jnp.sum((place_own[None, :] < place_own[:, None]).astype(jnp.int32), axis=1)
    order = one_hot(rank, rows)
    x = dot_nn(order, tokens).astype(BF)
    cot_hi, cot_lo = hi_lo(cotangent)
    cot = dot_nn(order, cot_hi) + dot_nn(order, cot_lo)
    spot = jnp.sum(jnp.where(rank[None, :] == jnp.arange(rows)[:, None], place_own[None, :], 0), axis=1)
    spot = spot + block_rows
    count = lengths.shape[0]
    tri = jnp.arange(count)[None, :] <= jnp.arange(count)[:, None]
    ends = jnp.sum(jnp.where(tri, lengths[None, :], 0), axis=1)
    starts = ends - lengths
    base = (block - 1) * block_rows
    ext_ends, ext_starts = ends - base, starts - base
    passed = ext_ends[None, :] <= spot[:, None]
    row_begin = jnp.max(jnp.where(passed, ext_ends[None, :], -base), axis=1)
    row_end = jnp.min(jnp.where(passed, jnp.int32(1 << 30), ext_ends[None, :]), axis=1)
    lane = jnp.arange(128)[None, :]
    ranges = jnp.where(lane == 0, row_begin[:, None], row_end[:, None])
    row_ranges = jnp.where(jnp.arange(8)[:, None] == 0, row_begin[None, :], row_end[None, :])
    tq = min(128, rows)
    tk = 256
    lo = jnp.min(row_begin.reshape(-1, tq), axis=1) // tk
    hi = (jnp.max(row_end.reshape(-1, tq), axis=1) + tk - 1) // tk
    lo = jnp.maximum(lo, 0)
    hi = jnp.minimum(hi, 3 * block_rows // tk)

    inside = (ext_starts < 2 * block_rows) & (ext_ends > block_rows)
    number = jnp.arange(count)
    key = jnp.where(inside, mem_index * count + number, blocks * count * 2 + number)
    slot = jnp.sum((key[None, :] < key[:, None]).astype(jnp.int32), axis=1)
    stacked = jnp.stack(groups)
    first = jnp.sum((stacked[None] + block_rows < ext_starts[:, None, None]).astype(jnp.int32), axis=2)
    final = jnp.sum((stacked[None] + block_rows < ext_ends[:, None, None]).astype(jnp.int32), axis=2)
    columns = jnp.concatenate(
        [mem_index[:, None], jnp.stack([first, final], axis=2).reshape(count, -1)], axis=1
    )
    sorted_columns = jnp.sum(
        jnp.where((slot[None, :] == number[:, None])[:, :, None], columns[None], 0), axis=1
    )
    steps = jnp.sum(inside.astype(jnp.int32))
    live = number < steps
    final_mem = jnp.sum(jnp.where(number == steps - 1, sorted_columns[:, 0], 0))
    mem_steps = jnp.where(live, sorted_columns[:, 0], final_mem)
    mem_table = jnp.concatenate([mem_steps, steps[None]])
    memories = jnp.arange(blocks)
    ahead = 0
    for dim, coordinate in (
        ("c", lambda m: m % grid.core),
        ("x", lambda m: m // grid.core % grid.size["x"]),
        ("z", lambda m: m // (grid.core * grid.size["x"])),
    ):
        ahead = ahead * grid.size[dim] + (coordinate(memories) - grid.at[dim]) % grid.size[dim]
    used = jnp.any(inside[:, None] & (mem_index[:, None] == memories[None, :]), axis=0)
    spot_table = jnp.where(used, ahead + 1, -(ahead + 1)).astype(jnp.int32)
    row_table = jnp.where(live[:, None], sorted_columns[:, 1:], 0)
    own_table, other_table = row_table[:, :2].reshape(-1), row_table[:, 2:].reshape(-1)

    bias_q, bias_v = vec[3], vec[4]
    q = ((dot_nt(x, wt_qkv[:D]) + bias_q).astype(BF) * SCALE).astype(BF)
    kv = (dot_nt(ext, wt_qkv[D:]) + jnp.concatenate([jnp.zeros((D,), F32), bias_v])).astype(BF)
    pairs = PAIRS if 3 * block_rows <= 4096 else 1
    att, lse = self_forward(q, kv, ranges, lo, hi, tq, tk, pairs)
    z1, cq = first_rows(x, att, wt_so, wt_cqkv[:D], vec)

    queries = [cq] + grid.others(cq, "y")
    wt_ckv = wt_cqkv[D:]
    bias_kv = jnp.concatenate([jnp.zeros((D,), F32), vec[7]])[None]
    mem_kv = memory_kv(mem_table, gathered, mem_rows, wt_ckv, bias_kv)
    ctq = min(128, rows)
    outs, lses = cross_forward(mem_table, row_table.reshape(-1), mem_kv, queries, ctq)
    own_outs = [outs[0]] + [grid.shift(outs[k], y=-k) for k in range(1, heads)]
    own_lses = [lses[0]] + [grid.shift(lses[k], y=-k) for k in range(1, heads)]
    late = gathered[:, mem_rows:].reshape(grid.count, -1, D)
    late_rows = np.cumsum([0, w_in.shape[0]] + [n_out] * chunks)
    wt_in, *wt_out = (
        late[:, i:j].reshape(-1, D) for i, j in zip(late_rows[:-1], late_rows[1:])
    )
    w2 = jnp.stack(wt_out)
    spots = grid.spots("cxyz")
    send = grid.count - grid.count // grid.core

    def over_cores(packed, sent):
        shape = (grid.core, grid.size["x"] * grid.size["y"], grid.size["z"], -1, D)
        own = packed.reshape(shape)[0]
        if grid.core == 1:
            return [own]
        return [own, grid.shift(sent.reshape(shape[1:]), c=1)]

    y, dz2, dcatt, stat, packed_1, sent_1 = middle_rows(
        spots, z1, cot, own_outs, own_lses, wt_co, wt_in, w2, vec, hidden_bias, max(send, 1)
    )
    upstream = grid.others(dcatt, "y")
    stats = grid.others(stat, "y")
    terms_1 = over_cores(packed_1, sent_1)
    begun = cross_begin(mem_table, own_table, mem_kv, queries[0], dcatt, stat, ctq)
    (begun, own_dcq), (upstream, stats, terms_1) = beside(begun, (upstream, stats, terms_1))
    sum_1 = add(terms_1)
    terms_1 = grid.ahead(sum_1, "xy")
    outputs = cross_backward(
        mem_table,
        spot_table,
        other_table,
        mem_kv,
        gathered,
        wt_ckv,
        begun,
        queries[1:],
        after(upstream, sum_1),
        stats,
        ctq,
        grid.core,
    )
    outputs, terms_1 = beside(outputs, terms_1)
    keep_m, send_m, g_ckv, g_bv, *dcqs = outputs
    own_dcqs = [own_dcq] + [grid.shift(x, y=-k) for k, x in enumerate(dcqs, 1)]
    terms_m = [keep_m] if grid.core == 1 else [keep_m, grid.shift(send_m, c=1)]
    terms_1 = grid.ahead(add(terms_1), "z")
    outputs = last_rows(z1, dz2, att, own_dcqs, wt_cqkv[:D], wt_so, vec)
    outputs, (terms_m, terms_1) = beside(outputs, (terms_m, terms_1))
    dz1, datt, delta, g_so, g_cq, gvec1 = outputs
    delta = jnp.pad(delta.reshape(PAIRS, 2, rows), ((0, 0), (0, 6), (0, 0)))
    terms_m = [t.reshape(grid.size["x"], grid.size["z"], mem_rows, D) for t in terms_m]
    sends_a = [add([t[k, :, :cut] for t in terms_m]) for k in range(1, grid.size["x"])]
    sends_b = [add([t[:, k, cut:] for t in terms_m]) for k in range(1, grid.size["z"])]
    terms_a = [grid.shift(a, x=k) for k, a in enumerate(sends_a, 1)]
    terms_b = [grid.shift(b, z=k) for k, b in enumerate(sends_b, 1)]
    outputs = self_backward(
        q, after(datt, *sends_a, *sends_b), kv, row_ranges, lse, delta, lo, hi, tq, tk, pairs
    )
    outputs, (terms_a, terms_b) = beside(outputs, (terms_a, terms_b))
    sum_a = add([t[0, :, :cut] for t in terms_m] + terms_a)
    sum_b = add([t[:, 0, cut:] for t in terms_m] + terms_b)
    dq, dk, dv = after(list(outputs), sum_a, sum_b)
    terms_a, terms_b = grid.ahead(sum_a, "z"), grid.ahead(sum_b, "x")

    outputs, terms_b = beside(token_grads(dq, dk, dv, wt_qkv), terms_b)
    dxq, back_before, back_here, back_behind = outputs
    from_next = lax.ppermute(back_before, BOTH, down)
    from_prior = lax.ppermute(back_behind, BOTH, up)
    packed_2 = weight_grads(
        spots,
        after(dq, back_here, *terms_b),
        dk,
        dv,
        x,
        (before, stream_rows, behind),
        gvec1,
        g_bv,
        g_so,
        g_cq,
        g_ckv,
        max(send, 1),
    )
    packed_2, (from_next, from_prior) = beside(packed_2, (from_next, from_prior))
    shared = (
        back_here.astype(F32) + from_next.astype(F32) + from_prior.astype(F32)
    ).astype(BF)

    def dealt(k):
        picks = lax.broadcasted_iota(jnp.int32, (rows, block_rows), 1) == groups[k][:, None]
        return dot_nn(picks.astype(BF), shared)

    grad_in = dz1 + dxq
    grad_hi, grad_lo = hi_lo(grad_in)
    grad_input = dot_tn(order, grad_hi) + dot_tn(order, grad_lo) + dealt(0)
    for k in range(1, heads):
        grad_input = grad_input + grid.shift(dealt(k).astype(BF), y=-k).astype(F32)
    y_hi, y_lo = hi_lo(y)
    layer_out = dot_tn(order, y_hi) + dot_tn(order, y_lo)
    grad_memory = jnp.concatenate([add(terms_a, F32), add(terms_b, F32)], axis=0)

    sum_2 = add(over_cores(*packed_2))
    sum_2 = add(grid.ahead(sum_2, "xy"))
    sum_2 = add(grid.ahead(sum_2, "z"), F32)
    sum_1 = add(terms_1, F32)
    s_in, s_co, *s_out, early = split(
        sum_1, [w_in.shape[0], n_out] + [n_out] * chunks + [sum_1.shape[0] - w_in.shape[0] - n_out * (1 + chunks)]
    )
    s_qkv, s_so, s_cq, final_rows = split(sum_2, [w_qkv.shape[0], n_out, w_cqkv.shape[0], 16])
    me = block * heads + here

    def mine(summed, first, count):
        return lax.dynamic_slice(summed, (first, me * lanes), (count, lanes))

    e, f = mine(early, 0, 6), mine(final_rows, 0, 7)
    width = ffn_bias.shape[0]
    s_bias = lax.dynamic_slice(early, (6 + me * width // D, me * width % D), (1, width))[0]
    return (
        layer_out,
        grad_input,
        grad_memory,
        s_qkv.T,
        s_so.T,
        s_cq.T,
        s_co.T,
        s_in.T,
        jnp.concatenate([s.T for s in s_out], axis=0),
        jnp.stack([f[0], e[3], e[0]]),
        jnp.stack([f[5], f[6], f[2], f[3], f[4], e[5], e[2], f[1], e[4], e[1]]),
        s_bias,
    )


def solution(mesh):
    rows = P(BOTH, None)
    cols = P(None, BOTH)
    return jax.shard_map(
        body,
        mesh=mesh,
        in_specs=(rows, rows, rows, P("blk"), P(), P()) + (cols,) * 8 + (P(BOTH),),
        out_specs=(rows,) * 3 + (cols,) * 8 + (P(BOTH),),
        check_vma=False,
    )
```
